32 devices in a mesh: dp: 8 (over y, x, core), tensor: 4 (over z).
Axes of the slice: x: 2, y: 2, z: 4, core: 2. Of those that a mesh axis runs over, the one named last changes fastest.
Arguments:
- hidden: bfloat16 [16384, 768], P('dp'), may hold values from -6 to 6
- teacher: float32 [16384, 768], P('dp'), may hold values from -6 to 6
- valid: int32 [8, 2048], P('dp'), may hold values from 0 to 1, as said below
- w_qkv: bfloat16 [3, 768, 768], P(None, None, 'tensor'), may hold values from -0.21875 to 0.21875
- b_qv: float32 [2, 768], P(None, 'tensor'), may hold values from -1 to 1
- w_attn_out: bfloat16 [768, 768], P('tensor'), may hold values from -1.25 to 1.25
- b_attn_out: float32 [768], replicated, may hold values from -1.5 to 1.5
- gain_one: float32 [768], replicated, may hold values from 0.5 to 1.5
- bias_one: float32 [768], replicated, may hold values from -1.5 to 1.5
- w_up: bfloat16 [768, 3072], P(None, 'tensor'), may hold values from -0.21875 to 0.21875
- b_up: float32 [3072], P('tensor'), may hold values from -2.5 to 2.5
- w_down: bfloat16 [3072, 768], P('tensor'), may hold values from -0.109375 to 0.109375
- b_down: float32 [768], replicated, may hold values from -1.5 to 1.5
- gain_two: float32 [768], replicated, may hold values from 0.5 to 1.5
- bias_two: float32 [768], replicated, may hold values from -1.5 to 1.5
- pairwise_gate_odds_table: float32 [12, 512, 512], P('tensor'), may hold values from -5 to 5
- gate_random_perturbation: float32 [12, 512, 512], P('tensor'), may hold values from -2 to 2
Outputs:
- out_states: float32 [16384, 768], P('dp')
- loss: float32 [], replicated
- grad_hidden: float32 [16384, 768], P('dp')
- grad_w_qkv: float32 [3, 768, 768], P(None, None, 'tensor')
- grad_b_qv: float32 [2, 768], P(None, 'tensor')
- grad_w_attn_out: float32 [768, 768], P('tensor')
- grad_b_attn_out: float32 [768], replicated
- grad_gain_one: float32 [768], replicated
- derivative_first_offset: float32 [768], replicated
- grad_w_up: float32 [768, 3072], P(None, 'tensor')
- grad_b_up: float32 [3072], P('tensor')
- grad_w_down: float32 [3072, 768], P('tensor')
- grad_b_down: float32 [768], replicated
- grad_gain_two: float32 [768], replicated
- grad_bias_two: float32 [768], replicated
- grad_mask_logits: float32 [12, 512, 512], P('tensor')
The draws below stay inside these ranges and needn't reach their ends.
Inputs may be any that keep to these rules, and one draw needn't show every extreme that they name: The first token of every sequence is valid.
All inputs are finite; a program needn't handle non-finite values.
Results may differ from the reference program's by a relative error of at most 0.019.
Values may be sent and summed in bfloat16 or wider, within the bound.
No kernel may reach another device: no remote copies, remote signals or barrier semaphores. Data moves between devices by JAX's collectives and lax.ppermute only.
A program may use at most 256 MiB of HBM per device.

```python
import math
import jax
import jax.numpy as jnp
from jax import lax

D = 768
HEADS = 12
HEAD_DIM = 64
FF = 3072
MASK_LEN = 512
BLOCK = 256
SEQ_LEN = 2048
SEQS = 8
TOKENS = 16384
N_TENSOR = 4


def draw_valid(key, part):
    sequence_ids = jnp.arange(SEQS, dtype=jnp.int32)[:, None]
    threshold = 250 + 500 * sequence_ids // max(SEQS - 1, 1)
    samples = jax.random.randint(key, (SEQS, SEQ_LEN), 0, 1000)
    flags = (samples < threshold).astype(jnp.int32)
    return flags.at[:, 0].set(1)


def steps_of(key, dims, split, smallest, high):
    loudness, own = 1.0, jax.random.fold_in(key, 6)
    for dim, shards_of in split:
        steps = jnp.exp(jax.random.uniform(jax.random.fold_in(own, dim), (shards_of,), jnp.float32, smallest / len(split), high / len(split)))
        loudness = loudness * jnp.repeat(steps, dims[dim] // shards_of).reshape([-1 if axis == dim else 1 for axis in range(len(dims))])
    return loudness


def gaussian(key, extent, spread, most, pieces=(), held_as=jnp.bfloat16):
    drawn = jax.random.normal(key, extent, jnp.float32) * spread
    if len(pieces) > 0:
        drawn = steps_of(key, extent, pieces, -0.22, 0.18) * drawn
    return jnp.clip(drawn, min=-most, max=most).astype(held_as)


def setup_inputs(seed: int = 0) -> dict:
    keys = jax.random.split(jax.random.key(seed), 18)
    return {
        "hidden": gaussian(keys[0], (TOKENS, D), 1.0, 6.0, ((0, 8),)),
        "teacher": gaussian(keys[1], (TOKENS, D), 1.0, 6.0, ((0, 8),), jnp.float32),
        "valid": draw_valid(jax.random.fold_in(keys[17], 71), 0),
        "w_qkv": gaussian(keys[3], (3, D, D), D ** -0.5, 0.21875, ((2, 4),)),
        "b_qv": gaussian(keys[4], (2, D), 0.2, 1.0, ((1, 4),), jnp.float32),
        "w_attn_out": gaussian(keys[5], (D, D), (D // 32) ** -0.5, 1.25, ((0, 4),)),
        "b_attn_out": gaussian(keys[6], (D,), 0.3, 1.5, (), jnp.float32),
        "gain_one": jnp.clip(1.0 + 0.1 * jax.random.normal(keys[7], (D,), jnp.float32), 0.5, 1.5),
        "bias_one": gaussian(keys[8], (D,), 0.3, 1.5, (), jnp.float32),
        "w_up": gaussian(keys[9], (D, FF), D ** -0.5, 0.21875, ((1, 4),)),
        "b_up": gaussian(keys[10], (FF,), 0.5, 2.5, ((0, 4),), jnp.float32),
        "w_down": gaussian(keys[11], (FF, D), FF ** -0.5, 0.109375, ((0, 4),)),
        "b_down": gaussian(keys[12], (D,), 0.3, 1.5, (), jnp.float32),
        "gain_two": jnp.clip(1.0 + 0.1 * jax.random.normal(keys[13], (D,), jnp.float32), 0.5, 1.5),
        "bias_two": gaussian(keys[14], (D,), 0.3, 1.5, (), jnp.float32),
        "pairwise_gate_odds_table": gaussian(keys[15], (HEADS, MASK_LEN, MASK_LEN), 1.0, 5.0, ((0, 4),), jnp.float32),
        "gate_random_perturbation": jnp.clip(jax.random.uniform(keys[16], (HEADS, MASK_LEN, MASK_LEN), jnp.float32, -2.0, 2.0) * steps_of(keys[16], (HEADS, MASK_LEN, MASK_LEN), ((0, 4),), -0.4, 0.0), -2.0, 2.0),
    }


@jax.custom_vjp
def low(v):
    return lax.optimization_barrier(v.astype(jnp.bfloat16)).astype(jnp.float32)

@jax.custom_vjp
def low_back(v):
    return v

def low_keep(v):
    return (low(v), None)

def low_pass(kept, grad):
    return (grad,)

def back_keep(v):
    return (v, None)

def back_low(kept, grad):
    return (low(grad),)
low.defvjp(low_keep, low_pass)
low_back.defvjp(back_keep, back_low)
epsilon = 1e-06
gumbel_softening_factor = 0.5
highest_prec = lax.Precision.HIGHEST

def normed(resid, gain, shift):
    average = lax.optimization_barrier(jnp.mean(resid, axis=-1, keepdims=True))
    centred = resid - average
    variance = lax.optimization_barrier(jnp.mean(centred * centred, axis=-1, keepdims=True))
    return centred * lax.rsqrt(variance + epsilon) * gain + shift

def apply_attention_over_series(queries, key_vectors, value_vectors, gate_natural_log):
    length = queries.shape[0]
    repeats = length // MASK_LEN
    score_scale = 1.0 / math.sqrt(HEAD_DIM)
    scores = jnp.einsum('qhd,khd->hqk', queries, key_vectors, precision=highest_prec) * score_scale
    scores = low_back(scores + jnp.tile(gate_natural_log, (1, repeats, repeats)))
    row_block = lax.broadcasted_iota(jnp.int32, (length, length), 0) // BLOCK
    col_block = lax.broadcasted_iota(jnp.int32, (length, length), 1) // BLOCK
    scores = jnp.where((col_block <= row_block)[None], scores, -1e+30)
    soft_weights = low(jax.nn.softmax(scores, axis=-1))
    return jnp.einsum('hqk,khd->qhd', soft_weights, value_vectors, precision=highest_prec)

def forward(hidden, w_qkv, b_qv, w_attn_out, b_attn_out, gain_one, bias_one, w_up, b_up, w_down, b_down, gain_two, bias_two, pairwise_gate_odds_table, gate_random_perturbation):
    tokens_all = hidden.shape[0]
    groups = N_TENSOR
    projected = jnp.einsum('td,kde->kte', hidden, w_qkv, precision=highest_prec)
    queries = low_back(low(projected[0] + b_qv[0]))
    key_vectors = low_back(low(projected[1]))
    value_vectors = low_back(low(projected[2] + b_qv[1]))
    gate_natural_log = jax.nn.log_sigmoid((pairwise_gate_odds_table + gate_random_perturbation) / gumbel_softening_factor)

    def shaped(array):
        return array.reshape(tokens_all // SEQ_LEN, SEQ_LEN, HEADS, HEAD_DIM)
    attend_saved = jax.checkpoint(apply_attention_over_series)

    def one_sequence(triple):
        return attend_saved(triple[0], triple[1], triple[2], gate_natural_log)
    context = lax.map(one_sequence, (shaped(queries), shaped(key_vectors), shaped(value_vectors)))
    context = low_back(low(context.reshape(tokens_all, D)))
    attn_parts = jnp.einsum('tgc,gce->gte', context.reshape(tokens_all, groups, D // groups), w_attn_out.reshape(groups, D // groups, D), precision=highest_prec)
    attention = low_back(lax.optimization_barrier(jnp.sum(low(attn_parts), axis=0)) + b_attn_out)
    first = normed(hidden + attention, gain_one, bias_one)
    before = low_back(jnp.dot(low(first), w_up, precision=highest_prec) + b_up)
    activated = low(jax.nn.gelu(before, approximate=False))
    ffn_parts = jnp.einsum('tgc,gce->gte', activated.reshape(tokens_all, groups, FF // groups), w_down.reshape(groups, FF // groups, D), precision=highest_prec)
    feedforward = low_back(lax.optimization_barrier(jnp.sum(low(ffn_parts), axis=0)) + b_down)
    return normed(first + feedforward, gain_two, bias_two)

def reference(hidden, teacher, valid, w_qkv, b_qv, w_attn_out, b_attn_out, gain_one, bias_one, w_up, b_up, w_down, b_down, gain_two, bias_two, pairwise_gate_odds_table, gate_random_perturbation):
    params = (hidden.astype(jnp.float32), w_qkv.astype(jnp.float32), b_qv, w_attn_out.astype(jnp.float32), b_attn_out, gain_one, bias_one, w_up.astype(jnp.float32), b_up, w_down.astype(jnp.float32), b_down, gain_two, bias_two, pairwise_gate_odds_table)
    valid_rows = valid.reshape(-1).astype(jnp.float32)[:, None]
    valid_total = jnp.sum(valid_rows)

    def with_error(*inputs):
        out_states = forward(*inputs, gate_random_perturbation)
        residue = out_states - teacher
        return (out_states, jnp.sum(valid_rows * residue * residue))
    (out_states, error), pullback = jax.vjp(with_error, *params)
    grads = pullback((jnp.zeros_like(out_states), SEQ_LEN / valid_total))
    loss_value = error / (valid_total * D)
    return (out_states, loss_value, grads[0], grads[1], grads[2], grads[3], grads[4], grads[5], grads[6], grads[7], grads[8], grads[9], grads[10], grads[11], grads[12], grads[13])
```

```python
import functools
import math

import jax
import jax.numpy as jnp
from jax import lax
from jax.experimental import pallas as pl
from jax.experimental.pallas import tpu as pltpu
from jax.sharding import PartitionSpec as P

BLOCK = 256
LOG2E = math.log2(math.e)
SOFTENING = 0.5
EPS = 1e-6
F32 = jnp.float32
BF16 = jnp.bfloat16


def dot(a, b):
    return jnp.dot(a, b, preferred_element_type=F32)


def dot_nt(a, b):
    return lax.dot_general(a, b, (((1,), (1,)), ((), ())), preferred_element_type=F32)


def dot_tn(a, b):
    return lax.dot_general(a, b, (((0,), (0,)), ((), ())), preferred_element_type=F32)


def dot_tt(a, b):
    return lax.dot_general(a, b, (((0,), (1,)), ((), ())), preferred_element_type=F32)


def attn_fwd_kernel(hid, w, b, bt, table, noise, ctx, ctxt, q3, k3, v3, qt, kt, lse, lmt, vt):
    heads, period = table.shape[0], table.shape[1]
    tokens = hid.shape[0]
    hd = q3.shape[2]
    width = heads * hd
    coef = LOG2E / math.sqrt(hd)
    parts = period // BLOCK
    for h in range(heads):
        x = (table[h] + noise[h]) * (1.0 / SOFTENING)
        ls = jnp.minimum(x, 0.0) - jnp.log1p(jnp.exp(-jnp.abs(x)))
        lmt[h] = jnp.transpose(ls * LOG2E)

    step = 2 * BLOCK

    def project(i, _):
        rows = pl.ds(pl.multiple_of(i * step, step), step)
        x = hid[rows, :]
        for n, (nat, tr) in enumerate(((q3, qt), (k3, kt), (v3, vt))):
            y = dot(x, w[n])
            yt = dot_tt(w[n], x)
            if n != 1:
                y = y + b[n // 2 : n // 2 + 1, :]
                yt = yt + bt[:, n // 2 : n // 2 + 1]
            y = y.astype(BF16)
            for h in range(heads):
                nat[h, rows, :] = y[:, h * hd : (h + 1) * hd]
            tr[:, rows] = yt.astype(BF16)
        return 0

    lax.fori_loop(0, tokens // step, project, 0)
    lse[...] = jnp.zeros(lse.shape, F32)

    def per_q(qb, _):
        qcol = pl.ds(pl.multiple_of(qb * BLOCK, BLOCK), BLOCK)
        mcol = pl.ds(pl.multiple_of(lax.rem(qb, parts) * BLOCK, BLOCK), BLOCK)

        def per_k(kb, carry):
            krow = pl.ds(pl.multiple_of(kb * BLOCK, BLOCK), BLOCK)
            mrow = pl.ds(pl.multiple_of(lax.rem(kb, parts) * BLOCK, BLOCK), BLOCK)
            out = []
            ss = [dot(k3[h, krow, :], qt[h * hd : (h + 1) * hd, qcol]) for h in range(heads)]
            for h in range(heads):
                m, l, acc = carry[h]
                s = ss[h] * coef + lmt[h, mrow, mcol]
                mn = jnp.maximum(m, jnp.max(s, axis=0, keepdims=True))
                al = jnp.exp2(m - mn)
                p = jnp.exp2(s - mn)
                l = l * al + jnp.sum(p, axis=0, keepdims=True)
                acc = acc * al + dot(vt[h * hd : (h + 1) * hd, krow], p.astype(BF16))
                out.append((mn, l, acc))
            return tuple(out)

        init = tuple(
            (
                jnp.full((1, BLOCK), -1e30, F32),
                jnp.zeros((1, BLOCK), F32),
                jnp.zeros((hd, BLOCK), F32),
            )
            for _ in range(heads)
        )
        res = lax.fori_loop(0, qb + 1, per_k, init)
        cols = []
        for h in range(heads):
            m, l, acc = res[h]
            c = acc / l
            ctxt[h * hd : (h + 1) * hd, qcol] = c
            lse[h : h + 1, qcol] = m + jnp.log2(l)
            cols.append(c)
        pad = -width % 128
        if pad:
            cols.append(jnp.zeros((pad, BLOCK), F32))
        full = jnp.transpose(jnp.concatenate(cols, axis=0))
        ctx[qcol, :] = full[:, :width].astype(BF16)
        return 0

    lax.fori_loop(0, tokens // BLOCK, per_q, 0)


def attn_fwd(hidden, w_qkv, b_qv, table, noise):
    tokens = hidden.shape[0]
    heads, period = table.shape[0], table.shape[1]
    width = w_qkv.shape[2]
    hd = width // heads
    sd = jax.ShapeDtypeStruct
    nat = sd((heads, tokens, hd), BF16)
    tr = sd((width, tokens), BF16)
    return pl.pallas_call(
        attn_fwd_kernel,
        out_shape=(
            sd((tokens, width), BF16),
            sd((width, tokens), F32),
            nat, nat, nat, tr, tr,
            sd((8, tokens), F32),
            sd(table.shape, F32),
        ),
        scratch_shapes=[pltpu.VMEM((width, tokens), BF16)],
        compiler_params=pltpu.CompilerParams(vmem_limit_bytes=56 << 20),
        name="attn_fwd",
    )(hidden, w_qkv, b_qv, b_qv.T, table, noise)


def attn_bwd_kernel(gctx, ctxt, q3, k3, v3, qt, kt, lse, lmt, gqkv, glm, gk, gv, g3, glmt):
    heads, tokens, hd = q3.shape
    period = lmt.shape[1]
    width = heads * hd
    coef = LOG2E / math.sqrt(hd)
    scale = 1.0 / math.sqrt(hd)
    parts = period // BLOCK
    pad = -width % 128
    gk[...] = jnp.zeros(gk.shape, F32)
    gv[...] = jnp.zeros(gv.shape, F32)
    glmt[...] = jnp.zeros(glmt.shape, F32)

    def per_q(i, _):
        qb = tokens // BLOCK - 1 - i
        qcol = pl.ds(pl.multiple_of(qb * BLOCK, BLOCK), BLOCK)
        mcol = pl.ds(pl.multiple_of(lax.rem(qb, parts) * BLOCK, BLOCK), BLOCK)
        g = gctx[qcol, :].astype(F32)
        gpad = jnp.concatenate([g, jnp.zeros((BLOCK, pad), F32)], axis=1) if pad else g
        gt = jnp.transpose(gpad)
        delta, gtb = [], []
        for h in range(heads):
            gth = gt[h * hd : (h + 1) * hd, :]
            delta.append(jnp.sum(gth * ctxt[h * hd : (h + 1) * hd, qcol], axis=0, keepdims=True))
            gtb.append(gth.astype(BF16))
            g3[h] = gctx[qcol, h * hd : (h + 1) * hd]

        def per_k(kb, carry):
            krow = pl.ds(pl.multiple_of(kb * BLOCK, BLOCK), BLOCK)
            mrow = pl.ds(pl.multiple_of(lax.rem(kb, parts) * BLOCK, BLOCK), BLOCK)
            out = []
            for h in range(heads):
                hs = slice(h * hd, (h + 1) * hd)
                s = dot(k3[h, krow, :], qt[hs, qcol]) * coef + lmt[h, mrow, mcol]
                p = jnp.exp2(s - lse[h : h + 1, qcol])
                dp = dot(v3[h, krow, :], gtb[h])
                ds = p * (dp - delta[h])
                dsb = ds.astype(BF16)
                glmt[h, mrow, mcol] += ds
                gv[h, krow, :] += dot(p.astype(BF16), g3[h])
                gk[h, krow, :] += dot(dsb, q3[h, qcol, :])
                out.append(carry[h] + dot(kt[hs, krow], dsb))
            return tuple(out)

        init = tuple(jnp.zeros((hd, BLOCK), F32) for _ in range(heads))
        res = lax.fori_loop(0, qb + 1, per_k, init)
        rows = [r * scale for r in res]
        if pad:
            rows.append(jnp.zeros((pad, BLOCK), F32))
        gq = jnp.transpose(jnp.concatenate(rows, axis=0))[:, :width]
        gkb = jnp.concatenate([gk[h, qcol, :] for h in range(heads)], axis=1) * scale
        gvb = jnp.concatenate([gv[h, qcol, :] for h in range(heads)], axis=1)
        gqkv[0, qcol, :] = gq.astype(BF16)
        gqkv[1, qcol, :] = gkb.astype(BF16)
        gqkv[2, qcol, :] = gvb.astype(BF16)
        return 0

    lax.fori_loop(0, tokens // BLOCK, per_q, 0)
    for h in range(heads):
        glm[h] = jnp.transpose(glmt[h])


def attn_bwd(gctx, ctxt, q3, k3, v3, qt, kt, lse, lmt):
    heads, tokens, hd = q3.shape
    width = heads * hd
    sd = jax.ShapeDtypeStruct
    return pl.pallas_call(
        attn_bwd_kernel,
        out_shape=(sd((3, tokens, width), BF16), sd(lmt.shape, F32)),
        scratch_shapes=[
            pltpu.VMEM((heads, tokens, hd), F32),
            pltpu.VMEM((heads, tokens, hd), F32),
            pltpu.VMEM((heads, BLOCK, hd), BF16),
            pltpu.VMEM(lmt.shape, F32),
        ],
        compiler_params=pltpu.CompilerParams(vmem_limit_bytes=56 << 20),
        name="attn_bwd",
    )(gctx, ctxt, q3, k3, v3, qt, kt, lse, lmt)


def shift(x, axis, size, amount):
    return lax.ppermute(x, axis, [(j, (j + amount) % size) for j in range(size)])


def swap(x, axis, size, bit):
    return lax.ppermute(x, axis, [(j, j ^ bit) for j in range(size)])


def small_sum(x, axis, size):
    bit = 1
    while bit < size:
        x = x + swap(x, axis, size, bit)
        bit *= 2
    return x


def rows_of(x, start, count):
    return lax.dynamic_slice_in_dim(x, start, count, axis=0)


def norm_parts(resid):
    centred = resid - jnp.mean(resid, axis=-1, keepdims=True)
    rstd = lax.rsqrt(jnp.mean(centred * centred, axis=-1, keepdims=True) + EPS)
    return centred * rstd, rstd


def norm_back(grad, xhat, rstd, gain):
    gy = grad * gain
    return rstd * (
        gy
        - jnp.mean(gy, axis=-1, keepdims=True)
        - xhat * jnp.mean(gy * xhat, axis=-1, keepdims=True)
    )


def bit_orders(size):
    bits = []
    bit = 2
    while bit < size:
        bits.append(bit)
        bit *= 2
    return bits, bits[::-1]


def gather_dp(x, size, dp_bits, index):
    for bit in dp_bits:
        other = swap(x, "dp", size, bit)
        x = (x, other)
        x = jnp.stack(x)
    return x


def body(
    hidden, teacher, valid, w_qkv, b_qv, w_attn_out, b_attn_out, gain_one, bias_one,
    w_up, b_up, w_down, b_down, gain_two, bias_two, table, noise, *, n_d, n_t,
):
    tokens, width = hidden.shape
    units = w_up.shape[1]
    local = w_qkv.shape[2]
    chunk = tokens // n_t
    ti = lax.axis_index("tensor")
    di = lax.axis_index("dp")
    slab = units // n_d
    low_bits, high_bits = bit_orders(n_d)
    valid_f = valid[0].astype(F32)
    total_valid = small_sum(jnp.sum(valid_f).reshape(1, 1), "dp", n_d)[0, 0]

    def own_slabs(w):
        return [rows_of(w, (di ^ r) * slab, slab) for r in range(n_d)]

    def gather_weight(w, bits):
        mine = rows_of(w, di * slab, slab)
        blocks = [own_slabs(w)]
        for s in range(1, n_t):
            held = {0: shift(mine, "tensor", n_t, s)}
            for bit in bits + [1]:
                keys = sorted(held)
                sent = jnp.concatenate([held[r] for r in keys], axis=0)
                got = swap(sent, "dp", n_d, bit)
                for n, r in enumerate(keys):
                    held[r | bit] = got[n * slab : (n + 1) * slab]
            blocks.append([held[r] for r in range(n_d)])
        return jnp.stack([jnp.concatenate([b[r] for b in blocks for r in range(half, n_d, 2)]) for half in (0, 1)])

    up_t = gather_weight(w_up.T, low_bits)
    down = gather_weight(w_down, high_bits)
    out_w = [w_attn_out] + [shift(w_attn_out, "tensor", n_t, s) for s in range(1, n_t)]
    order = jnp.stack([di ^ r for r in range(n_d)])
    b_all = [b_up] + [shift(b_up, "tensor", n_t, s) for s in range(1, n_t)]
    b_all = jnp.stack(b_all).reshape(n_t, n_d, slab)[:, order]
    b_half = [b_all[:, half::2].reshape(-1) for half in (0, 1)]

    ctx, ctxt, q3, k3, v3, qt, kt, lse, lmt = attn_fwd(hidden, w_qkv, b_qv, table, noise)

    ctx_parts = [rows_of(ctx, ti * chunk, chunk)] + [
        shift(rows_of(ctx, lax.rem(ti + s, n_t) * chunk, chunk), "tensor", n_t, s)
        for s in range(1, n_t)
    ]
    ctx_rel = jnp.concatenate(ctx_parts, axis=1)
    wo_rel = jnp.concatenate(out_w, axis=0)
    hid_own = rows_of(hidden, ti * chunk, chunk).astype(F32)
    teach_own = rows_of(teacher, ti * chunk, chunk)
    valid_own = lax.dynamic_slice_in_dim(valid_f, ti * chunk, chunk)[:, None]

    attention = dot(ctx_rel, wo_rel) + b_attn_out
    xhat1, rstd1 = norm_parts(hid_own + attention)
    first = xhat1 * gain_one + bias_one
    first_low = first.astype(BF16)
    acts, slopes = [], []
    for half in (0, 1):
        before = dot_nt(first_low, up_t[half]) + b_half[half]
        phi = 0.5 * (1.0 + lax.erf(before * math.sqrt(0.5)))
        dens = jnp.exp(-0.5 * before * before) * (1.0 / math.sqrt(2.0 * math.pi))
        a, d = lax.optimization_barrier(
            ((before * phi).astype(BF16), (phi + before * dens).astype(BF16))
        )
        acts.append(a)
        slopes.append(d)
    feed = dot(acts[0], down[0]) + dot(acts[1], down[1]) + b_down
    xhat2, rstd2 = norm_parts(first + feed)
    out_own = xhat2 * gain_two + bias_two
    residue = out_own - teach_own
    error = jnp.sum(valid_own * residue * residue)
    grad_out = (2.0 * tokens / total_valid) * valid_own * residue
    g_gain_two = jnp.sum(grad_out * xhat2, axis=0)
    g_bias_two = jnp.sum(grad_out, axis=0)
    grad_second = norm_back(grad_out, xhat2, rstd2, gain_two)
    grad_ffn = grad_second.astype(BF16)
    g_b_down = jnp.sum(grad_ffn.astype(F32), axis=0)
    out_low = out_own.astype(BF16)
    out_parts = [out_low] + [shift(out_low, "tensor", n_t, s) for s in range(1, n_t)]

    gb = [(dot_nt(grad_ffn, down[half]) * slopes[half].astype(F32)).astype(BF16) for half in (0, 1)]
    g_b_up = [jnp.sum(g.astype(F32), axis=0) for g in gb]
    grad_first = grad_second + dot(gb[0], up_t[0]) + dot(gb[1], up_t[1])
    g_gain_one = jnp.sum(grad_first * xhat1, axis=0)
    g_bias_one = jnp.sum(grad_first, axis=0)
    grad_resid = norm_back(grad_first, xhat1, rstd1, gain_one)
    grad_attn = grad_resid.astype(BF16)
    g_b_ao = jnp.sum(grad_attn.astype(F32), axis=0)
    gctx_rel = dot_nt(grad_attn, wo_rel).astype(BF16)
    gctx = jnp.zeros((tokens, local), BF16)
    gctx = lax.dynamic_update_slice(gctx, gctx_rel[:, :local], (ti * chunk, 0))
    for s in range(1, n_t):
        got = shift(gctx_rel[:, s * local : (s + 1) * local], "tensor", n_t, -s)
        gctx = lax.dynamic_update_slice(gctx, got, (lax.rem(ti + s, n_t) * chunk, 0))

    def reduce_weight(lhs, rhs, bits):
        sent = dot_tn(lhs[1], rhs).astype(BF16)
        got = swap(sent, "dp", n_d, 1)
        g = (dot_tn(lhs[0], rhs) + got.astype(F32)).astype(BF16)
        g = g.reshape((n_t,) + (2,) * len(low_bits) + (slab, width))
        axes = list(low_bits)[::-1]
        for bit in bits:
            ax = 1 + axes.index(bit)
            axes.remove(bit)
            keep = lax.index_in_dim(g, 0, ax, keepdims=False)
            send = lax.index_in_dim(g, 1, ax, keepdims=False)
            got = swap(send, "dp", n_d, bit)
            g = (keep.astype(F32) + got.astype(F32)).astype(BF16)
        total = g[0].astype(F32)
        for s in range(1, n_t):
            total = total + shift(g[s], "tensor", n_t, -s).astype(F32)
        return gather_absolute(total.astype(BF16), bits)

    def gather_absolute(x, bits):
        held = {0: x}
        for bit in bits + [1]:
            keys = sorted(held)
            got = swap(jnp.concatenate([held[r] for r in keys], axis=0), "dp", n_d, bit)
            n = x.shape[0]
            for m, r in enumerate(keys):
                held[r | bit] = got[m * n : (m + 1) * n]
        stack = jnp.stack([held[r] for r in range(n_d)])
        return jnp.concatenate([lax.dynamic_index_in_dim(stack, di ^ a, 0, keepdims=False) for a in range(n_d)], axis=0).astype(F32)

    g_down = reduce_weight(acts, grad_ffn, high_bits)
    g_up = reduce_weight(gb, first_low, low_bits).T

    g_ao_rel = dot_tn(ctx_rel, grad_attn).astype(BF16).reshape(n_t, local, width)

    def halve(x, bits):
        for bit in bits:
            half = x.shape[0] // 2
            up = (di // bit) % 2
            send = rows_of(x, (1 - up) * half, half)
            keep = rows_of(x, up * half, half)
            x = (keep.astype(F32) + swap(send, "dp", n_d, bit).astype(F32)).astype(BF16)
        return x

    def unhalve(x, bits):
        for bit in bits[::-1]:
            up = (di // bit) % 2
            other = swap(x, "dp", n_d, bit)
            pair = jnp.stack([x, other])
            x = jnp.concatenate([lax.dynamic_index_in_dim(pair, up, 0, keepdims=False), lax.dynamic_index_in_dim(pair, 1 - up, 0, keepdims=False)], axis=0)
        return x

    bits = [1] + low_bits
    g_ao = g_ao_rel.reshape(n_t, n_d, local // n_d, width).transpose(1, 0, 2, 3).reshape(n_d, -1, width)
    g_ao = halve(g_ao, bits)[0].reshape(n_t, local // n_d, width)
    total = g_ao[0].astype(F32)
    for s in range(1, n_t):
        total = total + shift(g_ao[s], "tensor", n_t, -s).astype(F32)
    g_ao = unhalve(total.astype(BF16)[None], bits).reshape(local, width).astype(F32)

    gbu = jnp.stack(g_b_up).reshape(2, n_t, n_d // 2, slab).transpose(1, 2, 0, 3).reshape(n_t, n_d, slab)
    gbu = gbu[:, order].reshape(n_t, units)
    gbu = gbu[jnp.stack([lax.rem(ti - z + n_t, n_t) for z in range(n_t)])]
    pack = jnp.concatenate(
        [
            jnp.stack([g_b_ao, g_gain_one, g_bias_one, g_b_down, g_gain_two, g_bias_two]).reshape(-1),
            gbu.reshape(-1),
            jnp.full((width,), error),
        ]
    ).reshape(-1, 128)
    pack = small_sum(small_sum(pack, "dp", n_d), "tensor", n_t).reshape(-1)
    vecs = [pack[n * width : (n + 1) * width] for n in range(6)]
    gbu = lax.dynamic_slice_in_dim(pack, 6 * width + ti * units, units)
    loss = pack[6 * width + n_t * units] / (total_valid * width)

    gqkv, glm = attn_bwd(gctx, ctxt, q3, k3, v3, qt, kt, lse, lmt)
    back = jnp.einsum("kte,kde->td", gqkv, w_qkv, preferred_element_type=F32).astype(BF16)
    mine = grad_resid + rows_of(back, ti * chunk, chunk).astype(F32)
    for s in range(1, n_t):
        mine = mine + shift(rows_of(back, lax.rem(ti + s, n_t) * chunk, chunk), "tensor", n_t, s).astype(F32)
    gh_low = mine.astype(BF16)
    gh_parts = [gh_low] + [shift(gh_low, "tensor", n_t, s) for s in range(1, n_t)]

    def whole(own, parts):
        out = jnp.zeros((tokens, width), F32)
        out = lax.dynamic_update_slice(out, own, (ti * chunk, 0))
        for s in range(1, n_t):
            out = lax.dynamic_update_slice(out, parts[s].astype(F32), (lax.rem(ti - s + n_t, n_t) * chunk, 0))
        return out

    grad_hidden = whole(mine, gh_parts)
    out_states = whole(out_own, out_parts)

    g_qkv_w = jnp.einsum("td,kte->kde", hidden, gqkv, preferred_element_type=F32).astype(BF16)
    slope = jax.nn.sigmoid((table + noise) * (-1.0 / SOFTENING)) * (1.0 / SOFTENING)
    g_mask = (glm * slope).astype(BF16)
    g_qkv_w = unhalve(halve(g_qkv_w.reshape(-1, local), [1] + low_bits), [1] + low_bits)
    g_mask = unhalve(halve(g_mask.reshape(-1, table.shape[2]), [1] + high_bits), [1] + high_bits)
    g_b_qv = small_sum(jnp.sum(gqkv[0::2].astype(F32), axis=1), "dp", n_d)
    return (
        out_states, loss, grad_hidden,
        g_qkv_w.reshape(w_qkv.shape).astype(F32), g_b_qv, g_ao, vecs[0], vecs[1], vecs[2],
        g_up, gbu, g_down, vecs[3], vecs[4], vecs[5],
        g_mask.reshape(table.shape).astype(F32),
    )


def solution(mesh):
    row, col = P("tensor", None), P(None, "tensor")
    heads = P("tensor", None, None)
    dp = P("dp", None)
    qkv = P(None, None, "tensor")
    sizes = dict(mesh.shape)
    return jax.shard_map(
        functools.partial(body, n_d=sizes["dp"], n_t=sizes["tensor"]),
        mesh=mesh,
        in_specs=(dp, dp, dp, qkv, col, row, P(), P(), P(), col, P("tensor"), row, P(), P(), P(), heads, heads),
        out_specs=(dp, P(), dp, qkv, col, row, P(), P(), P(), col, P("tensor"), row, P(), P(), P(), heads),
        check_vma=False,
    )
```

```python
import functools
import math

import jax
import jax.numpy as jnp
from jax import lax
from jax.experimental import pallas as pl
from jax.experimental.pallas import tpu as pltpu
from jax.sharding import PartitionSpec as P

BLOCK = 256
LOG2E = math.log2(math.e)
SOFTENING = 0.5
EPS = 1e-6
F32 = jnp.float32
BF16 = jnp.bfloat16


def dot(a, b):
    return jnp.dot(a, b, preferred_element_type=F32)


def dot_nt(a, b):
    return lax.dot_general(a, b, (((1,), (1,)), ((), ())), preferred_element_type=F32)


def dot_tn(a, b):
    return lax.dot_general(a, b, (((0,), (0,)), ((), ())), preferred_element_type=F32)


def dot_tt(a, b):
    return lax.dot_general(a, b, (((0,), (1,)), ((), ())), preferred_element_type=F32)


def prep_kernel(hid, w, b, bt, table, noise, q3, k3, v3, qt, kt, vt, lmt):
    heads = table.shape[0]
    tokens = hid.shape[0]
    hd = q3.shape[2]
    for h in range(heads):
        x = (table[h] + noise[h]) * (1.0 / SOFTENING)
        ls = jnp.minimum(x, 0.0) - jnp.log1p(jnp.exp(-jnp.abs(x)))
        lmt[h] = jnp.transpose(ls * LOG2E)

    step = 2 * BLOCK

    def project(i, _):
        rows = pl.ds(pl.multiple_of(i * step, step), step)
        x = hid[rows, :]
        for n, (nat, tr) in enumerate(((q3, qt), (k3, kt), (v3, vt))):
            y = dot(x, w[n])
            yt = dot_tt(w[n], x)
            if n != 1:
                y = y + b[n // 2 : n // 2 + 1, :]
                yt = yt + bt[:, n // 2 : n // 2 + 1]
            y = y.astype(BF16)
            for h in range(heads):
                nat[h, rows, :] = y[:, h * hd : (h + 1) * hd]
            tr[:, rows] = yt.astype(BF16)
        return 0

    lax.fori_loop(0, tokens // step, project, 0)


def attn_prep(hidden, w_qkv, b_qv, table, noise):
    tokens = hidden.shape[0]
    heads = table.shape[0]
    width = w_qkv.shape[2]
    sd = jax.ShapeDtypeStruct
    nat = sd((heads, tokens, width // heads), BF16)
    tr = sd((width, tokens), BF16)
    return pl.pallas_call(
        prep_kernel,
        out_shape=(nat, nat, nat, tr, tr, tr, sd(table.shape, F32)),
        compiler_params=pltpu.CompilerParams(vmem_limit_bytes=56 << 20),
        name="attn_prep",
    )(hidden, w_qkv, b_qv, b_qv.T, table, noise)


def attn_fwd_kernel(lo, n_prev, qt, k3, vt, lmt, *refs):
    ctx, ctxt, lse = refs[n_prev:]
    heads, tokens, hd = k3.shape
    period = lmt.shape[1]
    width = heads * hd
    coef = LOG2E / math.sqrt(hd)
    parts = period // BLOCK
    lse[...] = jnp.zeros(lse.shape, F32)
    first = (pl.program_id(0) + lo) * parts

    def per_q(j, _):
        qb = first + j
        qcol = pl.ds(pl.multiple_of(qb * BLOCK, BLOCK), BLOCK)
        ocol = pl.ds(pl.multiple_of(j * BLOCK, BLOCK), BLOCK)
        mcol = ocol

        def per_k(kb, carry):
            krow = pl.ds(pl.multiple_of(kb * BLOCK, BLOCK), BLOCK)
            mrow = pl.ds(pl.multiple_of(lax.rem(kb, parts) * BLOCK, BLOCK), BLOCK)
            out = []
            ss = [dot(k3[h, krow, :], qt[h * hd : (h + 1) * hd, qcol]) for h in range(heads)]
            for h in range(heads):
                m, l, acc = carry[h]
                s = ss[h] * coef + lmt[h, mrow, mcol]
                mn = jnp.maximum(m, jnp.max(s, axis=0, keepdims=True))
                al = jnp.exp2(m - mn)
                p = jnp.exp2(s - mn)
                l = l * al + jnp.sum(p, axis=0, keepdims=True)
                acc = acc * al + dot(vt[h * hd : (h + 1) * hd, krow], p.astype(BF16))
                out.append((mn, l, acc))
            return tuple(out)

        init = tuple(
            (
                jnp.full((1, BLOCK), -1e30, F32),
                jnp.zeros((1, BLOCK), F32),
                jnp.zeros((hd, BLOCK), F32),
            )
            for _ in range(heads)
        )
        res = lax.fori_loop(0, qb + 1, per_k, init)
        cols = []
        for h in range(heads):
            m, l, acc = res[h]
            c = acc / l
            ctxt[h * hd : (h + 1) * hd, ocol] = c
            lse[h : h + 1, ocol] = m + jnp.log2(l)
            cols.append(c)
        pad = -width % 128
        if pad:
            cols.append(jnp.zeros((pad, BLOCK), F32))
        full = jnp.transpose(jnp.concatenate(cols, axis=0))
        ctx[ocol, :] = full[:, :width].astype(BF16)
        return 0

    lax.fori_loop(0, parts, per_q, 0)


def attn_fwd(qt, k3, vt, lmt, lo, hi, prev=()):
    heads, tokens, hd = k3.shape
    width = heads * hd
    period = lmt.shape[1]
    sd = jax.ShapeDtypeStruct
    whole = lambda x: pl.BlockSpec(x.shape, lambda i, n=len(x.shape): (0,) * n)
    return pl.pallas_call(
        functools.partial(attn_fwd_kernel, lo, len(prev)),
        grid=(hi - lo,),
        in_specs=[whole(x) for x in (qt, k3, vt, lmt)] + [pl.BlockSpec(memory_space=pl.ANY)] * len(prev),
        out_specs=(
            pl.BlockSpec((period, width), lambda i: (i + lo, 0)),
            pl.BlockSpec((width, period), lambda i: (0, i + lo)),
            pl.BlockSpec((8, period), lambda i: (0, i + lo)),
        ),
        out_shape=(sd((tokens, width), BF16), sd((width, tokens), F32), sd((8, tokens), F32)),
        input_output_aliases={4 + n: n for n in range(len(prev))},
        compiler_params=pltpu.CompilerParams(vmem_limit_bytes=56 << 20),
        name="attn_fwd",
    )(qt, k3, vt, lmt, *prev)


def attn_bwd_kernel(gctx, ctxt, q3, k3, v3, qt, kt, lse, lmt, gqkv, glm, gk, gv, g3, glmt):
    heads, tokens, hd = q3.shape
    period = lmt.shape[1]
    width = heads * hd
    coef = LOG2E / math.sqrt(hd)
    scale = 1.0 / math.sqrt(hd)
    parts = period // BLOCK
    pad = -width % 128
    gk[...] = jnp.zeros(gk.shape, F32)
    gv[...] = jnp.zeros(gv.shape, F32)
    glmt[...] = jnp.zeros(glmt.shape, F32)

    def per_q(i, _):
        qb = tokens // BLOCK - 1 - i
        qcol = pl.ds(pl.multiple_of(qb * BLOCK, BLOCK), BLOCK)
        mcol = pl.ds(pl.multiple_of(lax.rem(qb, parts) * BLOCK, BLOCK), BLOCK)
        g = gctx[qcol, :].astype(F32)
        gpad = jnp.concatenate([g, jnp.zeros((BLOCK, pad), F32)], axis=1) if pad else g
        gt = jnp.transpose(gpad)
        delta, gtb = [], []
        for h in range(heads):
            gth = gt[h * hd : (h + 1) * hd, :]
            delta.append(jnp.sum(gth * ctxt[h * hd : (h + 1) * hd, qcol], axis=0, keepdims=True))
            gtb.append(gth.astype(BF16))
            g3[h] = gctx[qcol, h * hd : (h + 1) * hd]

        def per_k(kb, carry):
            krow = pl.ds(pl.multiple_of(kb * BLOCK, BLOCK), BLOCK)
            mrow = pl.ds(pl.multiple_of(lax.rem(kb, parts) * BLOCK, BLOCK), BLOCK)
            out = []
            for h in range(heads):
                hs = slice(h * hd, (h + 1) * hd)
                s = dot(k3[h, krow, :], qt[hs, qcol]) * coef + lmt[h, mrow, mcol]
                p = jnp.exp2(s - lse[h : h + 1, qcol])
                dp = dot(v3[h, krow, :], gtb[h])
                ds = p * (dp - delta[h])
                dsb = ds.astype(BF16)
                glmt[h, mrow, mcol] += ds
                gv[h, krow, :] += dot(p.astype(BF16), g3[h])
                gk[h, krow, :] += dot(dsb, q3[h, qcol, :])
                out.append(carry[h] + dot(kt[hs, krow], dsb))
            return tuple(out)

        init = tuple(jnp.zeros((hd, BLOCK), F32) for _ in range(heads))
        res = lax.fori_loop(0, qb + 1, per_k, init)
        rows = [r * scale for r in res]
        if pad:
            rows.append(jnp.zeros((pad, BLOCK), F32))
        gq = jnp.transpose(jnp.concatenate(rows, axis=0))[:, :width]
        gkb = jnp.concatenate([gk[h, qcol, :] for h in range(heads)], axis=1) * scale
        gvb = jnp.concatenate([gv[h, qcol, :] for h in range(heads)], axis=1)
        gqkv[0, qcol, :] = gq.astype(BF16)
        gqkv[1, qcol, :] = gkb.astype(BF16)
        gqkv[2, qcol, :] = gvb.astype(BF16)
        return 0

    lax.fori_loop(0, tokens // BLOCK, per_q, 0)
    for h in range(heads):
        glm[h] = jnp.transpose(glmt[h])


def attn_bwd(gctx, ctxt, q3, k3, v3, qt, kt, lse, lmt):
    heads, tokens, hd = q3.shape
    width = heads * hd
    sd = jax.ShapeDtypeStruct
    return pl.pallas_call(
        attn_bwd_kernel,
        out_shape=(sd((3, tokens, width), BF16), sd(lmt.shape, F32)),
        scratch_shapes=[
            pltpu.VMEM((heads, tokens, hd), F32),
            pltpu.VMEM((heads, tokens, hd), F32),
            pltpu.VMEM((heads, BLOCK, hd), BF16),
            pltpu.VMEM(lmt.shape, F32),
        ],
        compiler_params=pltpu.CompilerParams(vmem_limit_bytes=56 << 20),
        name="attn_bwd",
    )(gctx, ctxt, q3, k3, v3, qt, kt, lse, lmt)


def norm_parts(resid):
    centred = resid - jnp.mean(resid, axis=-1, keepdims=True)
    rstd = lax.rsqrt(jnp.mean(centred * centred, axis=-1, keepdims=True) + EPS)
    return centred * rstd, rstd


def norm_back(grad, xhat, rstd, gain):
    gy = grad * gain
    return rstd * (
        gy
        - jnp.mean(gy, axis=-1, keepdims=True)
        - xhat * jnp.mean(gy * xhat, axis=-1, keepdims=True)
    )


def ffn_kernel(
    n_t, slab, core, coef, *refs
):
    ctx = refs[:n_t]
    (wao, hid, teach, valid, vec, bup, up_o, up_m, up_t, dn_o, dn_m, dn_t,
     out, out_low, act, gb, first_low, grad_ffn, grad_attn, grad_resid, gctx, vecs, gbup,
     up_s, dn_s, slope, xhat_s, sems) = refs[n_t:]
    units, width = up_s.shape
    half = units // 2
    spots = half // (n_t * slab)
    c = core[0]
    copies = []
    for n, (o, m, t, dst) in enumerate(((up_o, up_m, up_t, up_s), (dn_o, dn_m, dn_t, dn_s))):
        for side, f in enumerate((m, t)):
            base = (c if side == 0 else 1 - c) * (spots * slab)
            for p in range(spots):
                to = side * half + p * n_t * slab
                copies.append((n, o.at[pl.ds(pl.multiple_of(base + p * slab, slab), slab)], dst.at[pl.ds(to, slab)]))
                rest = (n_t - 1) * slab
                copies.append((n, f.at[pl.ds(p * rest, rest)], dst.at[pl.ds(to + slab, rest)]))
    copies = [pltpu.make_async_copy(a, b, sems.at[i]) for i, (n, a, b) in enumerate(copies)]
    for cp in copies:
        cp.start()
    b_ao, g1, b1, b_dn, g2, b2 = (vec[n : n + 1, :] for n in range(6))
    attention = sum(dot(ctx[s][...], wao[s]) for s in range(n_t)) + b_ao
    xhat1, rstd1 = norm_parts(hid[...].astype(F32) + attention)
    first = xhat1 * g1 + b1
    first_low[...] = first.astype(BF16)
    xhat_s[...] = xhat1
    for cp in copies:
        cp.wait()
    blocks, _, size = bup.shape

    def forward(i, feed):
        rows = pl.ds(pl.multiple_of(i * size, size), size)
        before = dot_nt(first_low[...], up_s[rows, :]) + bup[i]
        phi = 0.5 * (1.0 + lax.erf(before * math.sqrt(0.5)))
        dens = jnp.exp(-0.5 * before * before) * (1.0 / math.sqrt(2.0 * math.pi))
        low = (before * phi).astype(BF16)
        act[:, rows] = low
        slope[:, rows] = (phi + before * dens).astype(BF16)
        return feed + dot(low, dn_s[rows, :])

    feed = lax.fori_loop(0, blocks, forward, jnp.zeros(out.shape, F32))
    xhat2, rstd2 = norm_parts(first + feed + b_dn)
    own = xhat2 * g2 + b2
    out[...] = own
    out_low[...] = own.astype(BF16)
    residue = own - teach[...]
    weighed = valid[...] * residue
    grad_out = coef[0] * weighed
    total = lambda x: jnp.sum(x, axis=0, keepdims=True)
    vecs[...] = jnp.zeros(vecs.shape, F32)
    vecs[4:5, :] = total(grad_out * xhat2)
    vecs[5:6, :] = total(grad_out)
    vecs[6:7, :] = total(weighed * residue)
    grad_second = norm_back(grad_out, xhat2, rstd2, g2)
    grad_resid[...] = grad_second
    low = grad_second.astype(BF16)
    grad_ffn[...] = low
    vecs[3:4, :] = total(low.astype(F32))

    def backward(i, acc):
        rows = pl.ds(pl.multiple_of(i * size, size), size)
        g = dot_nt(grad_ffn[...], dn_s[rows, :]) * slope[:, rows].astype(F32)
        low = g.astype(BF16)
        gb[:, rows] = low
        gbup[i] = total(low.astype(F32))
        return acc + dot(low, up_s[rows, :])

    grad_first = lax.fori_loop(0, blocks, backward, jnp.zeros(out.shape, F32)) + grad_resid[...]
    xhat1 = xhat_s[...]
    vecs[1:2, :] = total(grad_first * xhat1)
    vecs[2:3, :] = total(grad_first)
    back = norm_back(grad_first, xhat1, rstd1, g1)
    grad_resid[...] = back
    low = back.astype(BF16)
    grad_attn[...] = low
    vecs[0:1, :] = total(low.astype(F32))
    local = ctx[0].shape[1]
    for s in range(n_t):
        gctx[s] = dot_nt(low, wao[s]).astype(BF16)


def ffn(core, coef, ctx, wao, hid, teach, valid, vec, bup, ups, downs, slab):
    n_t = len(ctx)
    chunk, width = hid.shape
    local = ctx[0].shape[1]
    blocks, _, size = bup.shape
    units = blocks * size
    spots = units // (2 * n_t * slab)
    sd = jax.ShapeDtypeStruct
    vm = pl.BlockSpec(memory_space=pltpu.VMEM)
    sm = pl.BlockSpec(memory_space=pltpu.SMEM)
    hbm = pl.BlockSpec(memory_space=pl.ANY)
    return pl.pallas_call(
        functools.partial(ffn_kernel, n_t, slab),
        in_specs=[sm, sm] + [vm] * (n_t + 6) + [hbm] * 6,
        out_shape=(
            sd((chunk, width), F32),
            sd((chunk, width), BF16),
            sd((chunk, units), BF16),
            sd((chunk, units), BF16),
            sd((chunk, width), BF16),
            sd((chunk, width), BF16),
            sd((chunk, width), BF16),
            sd((chunk, width), F32),
            sd((n_t, chunk, local), BF16),
            sd((8, width), F32),
            sd((blocks, 1, size), F32),
        ),
        scratch_shapes=[
            pltpu.VMEM((units, width), BF16),
            pltpu.VMEM((units, width), BF16),
            pltpu.VMEM((chunk, units), BF16),
            pltpu.VMEM((chunk, width), F32),
            pltpu.SemaphoreType.DMA((8 * spots,)),
        ],
        compiler_params=pltpu.CompilerParams(vmem_limit_bytes=56 << 20),
        name="ffn",
    )(core, coef, *ctx, wao, hid, teach, valid, vec, bup, *ups, *downs)


def shift(x, size, amount):
    return lax.ppermute(x, "tensor", [(j, (j + amount) % size) for j in range(size)])


def swap(x, axis, size, bit):
    return lax.ppermute(x, axis, [(j, j ^ bit) for j in range(size)])


def rows_of(x, start, count):
    return lax.dynamic_slice_in_dim(x, start, count, axis=0)


def body(
    hidden, teacher, valid, w_qkv, b_qv, w_attn_out, b_attn_out, gain_one, bias_one,
    w_up, b_up, w_down, b_down, gain_two, bias_two, table, noise, *, n_d, n_t,
):
    tokens, width = hidden.shape
    units = w_up.shape[1]
    local = w_qkv.shape[2]
    chunk = tokens // n_t
    ti = lax.axis_index("tensor")
    di = lax.axis_index("dp")
    group = min(n_d, 8)
    low_bits = [b for b in (2, 4) if b < group]
    high_bits = low_bits[::-1]
    extra = [b for b in (8, 16, 32, 64, 128, 256, 512) if b < n_d]
    spots = group // 2
    slab = units // group
    piece = local // spots
    core = di % 2
    spot = (di // 2) % spots

    def bit_of(bit):
        return (di // bit) % 2

    def dp_swap(x, bit):
        return swap(x, "dp", n_d, bit)

    def everyone(x):
        bit = 1
        while bit < n_d:
            x = x + dp_swap(x, bit)
            bit *= 2
        return x

    def spread(x, bits):
        done = []
        for bit in bits:
            other = dp_swap(x, bit)
            up = bit_of(bit) == 1
            pos = sum(1 for b in done if b > bit)
            x = jnp.stack([jnp.where(up, other, x), jnp.where(up, x, other)], axis=pos)
            done.append(bit)
        return x.reshape((-1,) + x.shape[len(done) :])

    def narrow(x, bits):
        left = sorted(bits, reverse=True)
        for bit in bits:
            ax = left.index(bit)
            left.remove(bit)
            up = bit_of(bit)
            send = lax.dynamic_index_in_dim(x, 1 - up, ax, keepdims=False)
            keep = lax.dynamic_index_in_dim(x, up, ax, keepdims=False)
            x = (keep.astype(F32) + dp_swap(send, bit).astype(F32)).astype(BF16)
        return x

    def finish(x):
        for bit in extra:
            x = (x.astype(F32) + dp_swap(x, bit).astype(F32)).astype(BF16)
        return x

    valid_f = valid[0].astype(F32)
    total_valid = everyone(jnp.sum(valid_f).reshape(1, 1))[0, 0]

    up_own = w_up.T
    b_hi = b_up.astype(BF16)
    b_lo = (b_up - b_hi.astype(F32)).astype(BF16)
    start = core * (spots * slab) + spot * slab
    sent = jnp.concatenate(
        [
            rows_of(up_own, start, slab),
            rows_of(w_attn_out, spot * piece, piece),
            rows_of(w_down, start, slab),
            b_hi[None],
            b_lo[None],
            jnp.zeros((14, width), BF16),
        ]
    )
    came = [shift(sent, n_t, s) for s in range(1, n_t)]

    q3, k3, v3, qt, kt, vt, lmt = attn_prep(hidden, w_qkv, b_qv, table, noise)
    n_sup = tokens // lmt.shape[1]
    part = attn_fwd(qt, k3, vt, lmt, 0, n_sup - 1)
    part, came = lax.optimization_barrier((part, came))

    cut = slab + piece
    wide_a = jnp.stack([x[:cut] for x in came])
    wide_b = jnp.stack([x[cut : cut + slab] for x in came])
    wide_a = spread(wide_a, low_bits)
    wide_b = spread(wide_b, high_bits)
    up_m = wide_a[:, :, :slab].reshape(-1, width)
    down_m = wide_b.reshape(-1, width)
    wao = wide_a[:, :, slab:].transpose(1, 0, 2, 3).reshape(n_t - 1, local, width)
    wao = jnp.concatenate([w_attn_out[None], wao])
    up_t = dp_swap(up_m, 1)
    down_t = dp_swap(down_m, 1)
    b_all = jnp.stack(
        [b_up]
        + [x[cut + slab].astype(F32) + x[cut + slab + 1].astype(F32) for x in came]
    ).reshape(n_t, 2, spots, slab)
    b_mine = lax.dynamic_index_in_dim(b_all, core, 1, keepdims=False)
    b_theirs = lax.dynamic_index_in_dim(b_all, 1 - core, 1, keepdims=False)
    bup = jnp.stack([b_mine, b_theirs]).transpose(0, 2, 1, 3).reshape(2 * spots, 1, n_t * slab)

    ctx, ctxt, lse = attn_fwd(qt, k3, vt, lmt, n_sup - 1, n_sup, part)

    ctx_parts = [rows_of(ctx, ti * chunk, chunk)] + [
        shift(rows_of(ctx, lax.rem(ti + s, n_t) * chunk, chunk), n_t, s) for s in range(1, n_t)
    ]
    vec = jnp.stack([b_attn_out, gain_one, bias_one, b_down, gain_two, bias_two, b_down, b_down])
    coef = (2.0 * tokens / total_valid).reshape(1)
    (out_own, out_low, act, gb, first_low, grad_ffn, grad_attn, grad_resid, gctx_rel, vecs, gbup) = ffn(
        core.reshape(1),
        coef,
        ctx_parts,
        wao,
        rows_of(hidden, ti * chunk, chunk),
        rows_of(teacher, ti * chunk, chunk),
        lax.dynamic_slice_in_dim(valid_f, ti * chunk, chunk)[:, None],
        vec,
        bup,
        (up_own, up_m, up_t),
        (w_down, down_m, down_t),
        slab,
    )
    out_all = lax.all_gather(out_low, "tensor", axis=0, tiled=True)

    gctx = jnp.zeros((tokens, local), BF16)
    gctx = lax.dynamic_update_slice(gctx, gctx_rel[0], (ti * chunk, 0))
    for s in range(1, n_t):
        got = shift(gctx_rel[s], n_t, -s)
        gctx = lax.dynamic_update_slice(gctx, got, (lax.rem(ti + s, n_t) * chunk, 0))

    half = n_t * units // 2
    lead = (2,) * len(low_bits)
    send_up = dot_tn(gb[:, half:], first_low).astype(BF16).reshape(spots, n_t, slab, width)
    g_ao = jnp.stack([dot_tn(c, grad_attn) for c in ctx_parts]).astype(BF16)
    g_ao = g_ao.reshape(n_t, spots, piece, width).transpose(1, 0, 2, 3)
    send_a = jnp.concatenate([send_up, g_ao], axis=2)
    send_b = dot_tn(act[:, half:], grad_ffn).astype(BF16)
    got_a = dp_swap(send_a, 1)
    got_b = dp_swap(send_b, 1)
    keep_up = dot_tn(gb[:, :half], first_low).reshape(spots, n_t, slab, width)
    keep_a = jnp.concatenate([keep_up.astype(BF16), g_ao], axis=2)
    g_a = (keep_a.astype(F32) + got_a.astype(F32)).astype(BF16)
    g_b = (dot_tn(act[:, :half], grad_ffn) + got_b.astype(F32)).astype(BF16)
    gctx, g_a, g_b = lax.optimization_barrier((gctx, g_a, g_b))
    g_a = finish(narrow(g_a.reshape(lead + (n_t, cut, width)), low_bits))
    g_b = finish(narrow(g_b.reshape(lead + (n_t, slab, width)), high_bits))

    gqkv, glm = attn_bwd(gctx, ctxt, q3, k3, v3, qt, kt, lse, lmt)
    back = jnp.einsum("kte,kde->td", gqkv, w_qkv, preferred_element_type=F32)
    mine = (jnp.arange(n_t) == ti)[:, None, None]
    back = back.reshape(n_t, chunk, width) + jnp.where(mine, grad_resid[None], 0.0)
    grad_hidden = lax.psum(back.reshape(tokens, width).astype(BF16), "tensor").astype(F32)
    out_states = out_all.astype(F32)

    g_qkv_w = jnp.einsum("td,kte->kde", hidden, gqkv, preferred_element_type=F32).astype(BF16)
    slope = jax.nn.sigmoid((table + noise) * (-1.0 / SOFTENING)) * (1.0 / SOFTENING)
    g_mask = (glm * slope).astype(BF16)
    g_qkv_w = finish(narrow(g_qkv_w.reshape(lead + (2, -1, local)), [1] + low_bits))
    g_mask = finish(narrow(g_mask.reshape(lead + (2, -1, table.shape[2])), [1] + high_bits))
    g_qkv_w = spread(g_qkv_w, low_bits + [1])
    g_mask = spread(g_mask, high_bits + [1])

    total = jnp.concatenate([g_a, g_b], axis=1)
    summed = total[0].astype(F32)
    for s in range(1, n_t):
        summed = summed + shift(total[s], n_t, -s).astype(F32)
    summed = summed.astype(BF16)
    all_a = spread(summed[:cut], low_bits)
    all_b = spread(summed[cut:], high_bits)
    g_ao = all_a[:, slab:].reshape(local, width).astype(F32)
    pair = jnp.stack([all_a[:, :slab].reshape(-1, width), all_b.reshape(-1, width)])
    other = dp_swap(pair, 1)
    up = core == 1
    pair = jnp.concatenate([jnp.where(up, other, pair), jnp.where(up, pair, other)], axis=1)
    g_up = pair[0].T.astype(F32)
    g_down = pair[1].astype(F32)

    gbu = gbup.reshape(2, spots, n_t, slab)
    gbu = jnp.where(up, gbu[::-1], gbu).transpose(2, 0, 1, 3).reshape(n_t, units)
    gbu = gbu[jnp.stack([lax.rem(ti - z + n_t, n_t) for z in range(n_t)])]
    g_b_qv = jnp.sum(gqkv[0::2].astype(F32), axis=1)
    g_b_qv = jnp.where(mine, g_b_qv[None], 0.0)
    pack = jnp.concatenate([vecs[:7].reshape(-1), gbu.reshape(-1), g_b_qv.reshape(-1)]).reshape(-1, 128)
    pack = everyone(pack)
    bit = 1
    while bit < n_t:
        pack = pack + swap(pack, "tensor", n_t, bit)
        bit *= 2
    pack = pack.reshape(-1)
    rows = [pack[n * width : (n + 1) * width] for n in range(7)]
    gbu = lax.dynamic_slice_in_dim(pack, 7 * width + ti * units, units)
    g_b_qv = lax.dynamic_slice_in_dim(pack, 7 * width + n_t * units + ti * 2 * local, 2 * local)
    loss = jnp.sum(rows[6]) / (total_valid * width)
    return (
        out_states, loss, grad_hidden,
        g_qkv_w.reshape(w_qkv.shape).astype(F32), g_b_qv.reshape(2, local), g_ao, rows[0], rows[1], rows[2],
        g_up, gbu, g_down, rows[3], rows[4], rows[5],
        g_mask.reshape(table.shape).astype(F32),
    )


def solution(mesh):
    row, col = P("tensor", None), P(None, "tensor")
    heads = P("tensor", None, None)
    dp = P("dp", None)
    qkv = P(None, None, "tensor")
    sizes = dict(mesh.shape)
    return jax.shard_map(
        functools.partial(body, n_d=sizes["dp"], n_t=sizes["tensor"]),
        mesh=mesh,
        in_specs=(dp, dp, dp, qkv, col, row, P(), P(), P(), col, P("tensor"), row, P(), P(), P(), heads, heads),
        out_specs=(dp, P(), dp, qkv, col, row, P(), P(), P(), col, P("tensor"), row, P(), P(), P(), heads),
        check_vma=False,
    )
```

```python
import functools
import math

import jax
import jax.numpy as jnp
from jax import lax
from jax.experimental import pallas as pl
from jax.experimental.pallas import tpu as pltpu
from jax.sharding import PartitionSpec as P

BLOCK = 256
LOG2E = math.log2(math.e)
SOFTENING = 0.5
EPS = 1e-6
F32 = jnp.float32
BF16 = jnp.bfloat16


def dot(a, b):
    return jnp.dot(a, b, preferred_element_type=F32)


def dot_nt(a, b):
    return lax.dot_general(a, b, (((1,), (1,)), ((), ())), preferred_element_type=F32)


def dot_tn(a, b):
    return lax.dot_general(a, b, (((0,), (0,)), ((), ())), preferred_element_type=F32)


def dot_tt(a, b):
    return lax.dot_general(a, b, (((0,), (1,)), ((), ())), preferred_element_type=F32)


def cost(micros, moved):
    return pl.CostEstimate(flops=int(micros * 1e9), transcendentals=0, bytes_accessed=moved)


def prep_kernel(hid, w, b, bt, table, noise, q3, k3, v3, qt, kt, vt, lmt):
    heads = table.shape[0]
    tokens = hid.shape[0]
    hd = q3.shape[2]
    for h in range(heads):
        x = (table[h] + noise[h]) * (1.0 / SOFTENING)
        ls = jnp.minimum(x, 0.0) - jnp.log1p(jnp.exp(-jnp.abs(x)))
        lmt[h] = jnp.transpose(ls * LOG2E)

    step = 2 * BLOCK

    def project(i, _):
        rows = pl.ds(pl.multiple_of(i * step, step), step)
        x = hid[rows, :]
        for n, (nat, tr) in enumerate(((q3, qt), (k3, kt), (v3, vt))):
            y = dot(x, w[n])
            yt = dot_tt(w[n], x)
            if n != 1:
                y = y + b[n // 2 : n // 2 + 1, :]
                yt = yt + bt[:, n // 2 : n // 2 + 1]
            y = y.astype(BF16)
            for h in range(heads):
                nat[h, rows, :] = y[:, h * hd : (h + 1) * hd]
            tr[:, rows] = yt.astype(BF16)
        return 0

    lax.fori_loop(0, tokens // step, project, 0)


def attn_prep(hidden, w_qkv, b_qv, table, noise):
    tokens = hidden.shape[0]
    heads = table.shape[0]
    width = w_qkv.shape[2]
    sd = jax.ShapeDtypeStruct
    nat = sd((heads, tokens, width // heads), BF16)
    tr = sd((width, tokens), BF16)
    return pl.pallas_call(
        prep_kernel,
        out_shape=(nat, nat, nat, tr, tr, tr, sd(table.shape, F32)),
        compiler_params=pltpu.CompilerParams(vmem_limit_bytes=56 << 20),
        cost_estimate=cost(15, 20 << 20),
        name="attn_prep",
    )(hidden, w_qkv, b_qv, b_qv.T, table, noise)


def attn_fwd_kernel(lo, n_prev, qt, k3, vt, lmt, *refs):
    ctx, ctxt, lse = refs[n_prev:]
    heads, tokens, hd = k3.shape
    period = lmt.shape[1]
    width = heads * hd
    coef = LOG2E / math.sqrt(hd)
    parts = period // BLOCK
    lse[...] = jnp.zeros(lse.shape, F32)
    first = (pl.program_id(0) + lo) * parts

    def per_q(j, _):
        qb = first + j
        qcol = pl.ds(pl.multiple_of(qb * BLOCK, BLOCK), BLOCK)
        ocol = pl.ds(pl.multiple_of(j * BLOCK, BLOCK), BLOCK)
        mcol = ocol

        def per_k(kb, carry):
            krow = pl.ds(pl.multiple_of(kb * BLOCK, BLOCK), BLOCK)
            mrow = pl.ds(pl.multiple_of(lax.rem(kb, parts) * BLOCK, BLOCK), BLOCK)
            out = []
            ss = [dot(k3[h, krow, :], qt[h * hd : (h + 1) * hd, qcol]) for h in range(heads)]
            for h in range(heads):
                m, l, acc = carry[h]
                s = ss[h] * coef + lmt[h, mrow, mcol]
                mn = jnp.maximum(m, jnp.max(s, axis=0, keepdims=True))
                al = jnp.exp2(m - mn)
                p = jnp.exp2(s - mn)
                l = l * al + jnp.sum(p, axis=0, keepdims=True)
                acc = acc * al + dot(vt[h * hd : (h + 1) * hd, krow], p.astype(BF16))
                out.append((mn, l, acc))
            return tuple(out)

        init = tuple(
            (
                jnp.full((1, BLOCK), -1e30, F32),
                jnp.zeros((1, BLOCK), F32),
                jnp.zeros((hd, BLOCK), F32),
            )
            for _ in range(heads)
        )
        res = lax.fori_loop(0, qb + 1, per_k, init)
        cols = []
        for h in range(heads):
            m, l, acc = res[h]
            c = acc / l
            ctxt[h * hd : (h + 1) * hd, ocol] = c
            lse[h : h + 1, ocol] = m + jnp.log2(l)
            cols.append(c)
        pad = -width % 128
        if pad:
            cols.append(jnp.zeros((pad, BLOCK), F32))
        full = jnp.transpose(jnp.concatenate(cols, axis=0))
        ctx[ocol, :] = full[:, :width].astype(BF16)
        return 0

    lax.fori_loop(0, parts, per_q, 0)


def attn_fwd(qt, k3, vt, lmt, lo, hi, prev=()):
    heads, tokens, hd = k3.shape
    width = heads * hd
    period = lmt.shape[1]
    sd = jax.ShapeDtypeStruct
    whole = lambda x: pl.BlockSpec(x.shape, lambda i, n=len(x.shape): (0,) * n)
    return pl.pallas_call(
        functools.partial(attn_fwd_kernel, lo, len(prev)),
        grid=(hi - lo,),
        in_specs=[whole(x) for x in (qt, k3, vt, lmt)] + [pl.BlockSpec(memory_space=pl.ANY)] * len(prev),
        out_specs=(
            pl.BlockSpec((period, width), lambda i: (i + lo, 0)),
            pl.BlockSpec((width, period), lambda i: (0, i + lo)),
            pl.BlockSpec((8, period), lambda i: (0, i + lo)),
        ),
        out_shape=(sd((tokens, width), BF16), sd((width, tokens), F32), sd((8, tokens), F32)),
        input_output_aliases={4 + n: n for n in range(len(prev))},
        compiler_params=pltpu.CompilerParams(vmem_limit_bytes=56 << 20),
        cost_estimate=cost(1.5 * (hi * hi - lo * lo) / 2, 8 << 20),
        name="attn_fwd",
    )(qt, k3, vt, lmt, *prev)


def attn_bwd_kernel(n_t, place, *refs):
    pieces = refs[:n_t]
    (ctxt, q3, k3, v3, qt, kt, lse, lmt, gqkv, glm, gk, gv, g3, glmt, gctx, sems) = refs[n_t:]
    heads, tokens, hd = q3.shape
    chunk = tokens // n_t
    copies = []
    for s in range(n_t):
        at = lax.rem(place[0] + s, n_t) * chunk
        to = gctx.at[pl.ds(pl.multiple_of(at, chunk), chunk), :]
        copies.append(pltpu.make_async_copy(pieces[s], to, sems.at[s]))
    for cp in copies:
        cp.start()
    period = lmt.shape[1]
    width = heads * hd
    coef = LOG2E / math.sqrt(hd)
    scale = 1.0 / math.sqrt(hd)
    parts = period // BLOCK
    pad = -width % 128
    gk[...] = jnp.zeros(gk.shape, F32)
    gv[...] = jnp.zeros(gv.shape, F32)
    glmt[...] = jnp.zeros(glmt.shape, F32)
    for cp in copies:
        cp.wait()

    def per_q(i, _):
        qb = tokens // BLOCK - 1 - i
        qcol = pl.ds(pl.multiple_of(qb * BLOCK, BLOCK), BLOCK)
        mcol = pl.ds(pl.multiple_of(lax.rem(qb, parts) * BLOCK, BLOCK), BLOCK)
        g = gctx[qcol, :].astype(F32)
        gpad = jnp.concatenate([g, jnp.zeros((BLOCK, pad), F32)], axis=1) if pad else g
        gt = jnp.transpose(gpad)
        delta, gtb = [], []
        for h in range(heads):
            gth = gt[h * hd : (h + 1) * hd, :]
            delta.append(jnp.sum(gth * ctxt[h * hd : (h + 1) * hd, qcol], axis=0, keepdims=True))
            gtb.append(gth.astype(BF16))
            g3[h] = gctx[qcol, h * hd : (h + 1) * hd]

        def per_k(kb, carry):
            krow = pl.ds(pl.multiple_of(kb * BLOCK, BLOCK), BLOCK)
            mrow = pl.ds(pl.multiple_of(lax.rem(kb, parts) * BLOCK, BLOCK), BLOCK)
            out = []
            for h in range(heads):
                hs = slice(h * hd, (h + 1) * hd)
                s = dot(k3[h, krow, :], qt[hs, qcol]) * coef + lmt[h, mrow, mcol]
                p = jnp.exp2(s - lse[h : h + 1, qcol])
                dp = dot(v3[h, krow, :], gtb[h])
                ds = p * (dp - delta[h])
                dsb = ds.astype(BF16)
                glmt[h, mrow, mcol] += ds
                gv[h, krow, :] += dot(p.astype(BF16), g3[h])
                gk[h, krow, :] += dot(dsb, q3[h, qcol, :])
                out.append(carry[h] + dot(kt[hs, krow], dsb))
            return tuple(out)

        init = tuple(jnp.zeros((hd, BLOCK), F32) for _ in range(heads))
        res = lax.fori_loop(0, qb + 1, per_k, init)
        rows = [r * scale for r in res]
        if pad:
            rows.append(jnp.zeros((pad, BLOCK), F32))
        gq = jnp.transpose(jnp.concatenate(rows, axis=0))[:, :width]
        gkb = jnp.concatenate([gk[h, qcol, :] for h in range(heads)], axis=1) * scale
        gvb = jnp.concatenate([gv[h, qcol, :] for h in range(heads)], axis=1)
        gqkv[0, qcol, :] = gq.astype(BF16)
        gqkv[1, qcol, :] = gkb.astype(BF16)
        gqkv[2, qcol, :] = gvb.astype(BF16)
        return 0

    lax.fori_loop(0, tokens // BLOCK, per_q, 0)
    for h in range(heads):
        glm[h] = jnp.transpose(glmt[h])


def attn_bwd(place, parts, ctxt, q3, k3, v3, qt, kt, lse, lmt):
    heads, tokens, hd = q3.shape
    width = heads * hd
    n_t = len(parts)
    sd = jax.ShapeDtypeStruct
    vm = pl.BlockSpec(memory_space=pltpu.VMEM)
    return pl.pallas_call(
        functools.partial(attn_bwd_kernel, n_t),
        in_specs=[pl.BlockSpec(memory_space=pltpu.SMEM)] + [pl.BlockSpec(memory_space=pl.ANY)] * n_t + [vm] * 8,
        out_shape=(sd((3, tokens, width), BF16), sd(lmt.shape, F32)),
        scratch_shapes=[
            pltpu.VMEM((heads, tokens, hd), F32),
            pltpu.VMEM((heads, tokens, hd), F32),
            pltpu.VMEM((heads, BLOCK, hd), BF16),
            pltpu.VMEM(lmt.shape, F32),
            pltpu.VMEM((tokens, width), BF16),
            pltpu.SemaphoreType.DMA((n_t,)),
        ],
        compiler_params=pltpu.CompilerParams(vmem_limit_bytes=56 << 20),
        cost_estimate=cost(40, 20 << 20),
        name="attn_bwd",
    )(place, *parts, ctxt, q3, k3, v3, qt, kt, lse, lmt)


def norm_parts(resid):
    centred = resid - jnp.mean(resid, axis=-1, keepdims=True)
    rstd = lax.rsqrt(jnp.mean(centred * centred, axis=-1, keepdims=True) + EPS)
    return centred * rstd, rstd


def norm_back(grad, xhat, rstd, gain):
    gy = grad * gain
    return rstd * (
        gy
        - jnp.mean(gy, axis=-1, keepdims=True)
        - xhat * jnp.mean(gy * xhat, axis=-1, keepdims=True)
    )


def ffn_kernel(
    n_t, slab, core, *refs
):
    ctx = refs[:n_t]
    (wao, hid, teach, valid, vec, bup, up_o, up_m, up_t, dn_o, dn_m, dn_t,
     out, out_low, act, gb, first_low, grad_ffn, grad_attn, grad_resid, gctx, vecs, gbup,
     up_s, dn_s, slope, xhat_s, sems) = refs[n_t:]
    units, width = up_s.shape
    half = units // 2
    spots = half // (n_t * slab)
    c = core[0]
    copies = []
    for n, (o, m, t, dst) in enumerate(((up_o, up_m, up_t, up_s), (dn_o, dn_m, dn_t, dn_s))):
        for side, f in enumerate((m, t)):
            base = (c if side == 0 else 1 - c) * (spots * slab)
            for p in range(spots):
                to = side * half + p * n_t * slab
                copies.append((n, o.at[pl.ds(pl.multiple_of(base + p * slab, slab), slab)], dst.at[pl.ds(to, slab)]))
                rest = (n_t - 1) * slab
                copies.append((n, f.at[pl.ds(p * rest, rest)], dst.at[pl.ds(to + slab, rest)]))
    copies = [pltpu.make_async_copy(a, b, sems.at[i]) for i, (n, a, b) in enumerate(copies)]
    for cp in copies:
        cp.start()
    b_ao, g1, b1, b_dn, g2, b2 = (vec[n : n + 1, :] for n in range(6))
    attention = sum(dot(ctx[s][...], wao[s]) for s in range(n_t)) + b_ao
    xhat1, rstd1 = norm_parts(hid[...].astype(F32) + attention)
    first = xhat1 * g1 + b1
    first_low[...] = first.astype(BF16)
    xhat_s[...] = xhat1
    for cp in copies:
        cp.wait()
    blocks, _, size = bup.shape

    def forward(i, feed):
        rows = pl.ds(pl.multiple_of(i * size, size), size)
        before = dot_nt(first_low[...], up_s[rows, :]) + bup[i]
        phi = 0.5 * (1.0 + lax.erf(before * math.sqrt(0.5)))
        dens = jnp.exp(-0.5 * before * before) * (1.0 / math.sqrt(2.0 * math.pi))
        low = (before * phi).astype(BF16)
        act[:, rows] = low
        slope[:, rows] = (phi + before * dens).astype(BF16)
        return feed + dot(low, dn_s[rows, :])

    feed = lax.fori_loop(0, blocks, forward, jnp.zeros(out.shape, F32))
    xhat2, rstd2 = norm_parts(first + feed + b_dn)
    own = xhat2 * g2 + b2
    out[...] = own
    out_low[...] = own.astype(BF16)
    residue = own - teach[...]
    weighed = valid[...] * residue
    grad_out = weighed
    total = lambda x: jnp.sum(x, axis=0, keepdims=True)
    vecs[4:5, :] = total(grad_out * xhat2)
    vecs[5:6, :] = total(grad_out)
    vecs[6:7, :] = total(weighed * residue)
    vecs[7:8, :] = jnp.broadcast_to(jnp.sum(valid[...], axis=0, keepdims=True), (1, width))
    grad_second = norm_back(grad_out, xhat2, rstd2, g2)
    grad_resid[...] = grad_second
    low = grad_second.astype(BF16)
    grad_ffn[...] = low
    vecs[3:4, :] = total(low.astype(F32))

    def backward(i, acc):
        rows = pl.ds(pl.multiple_of(i * size, size), size)
        g = dot_nt(grad_ffn[...], dn_s[rows, :]) * slope[:, rows].astype(F32)
        low = g.astype(BF16)
        gb[:, rows] = low
        gbup[i] = total(low.astype(F32))
        return acc + dot(low, up_s[rows, :])

    grad_first = lax.fori_loop(0, blocks, backward, jnp.zeros(out.shape, F32)) + grad_resid[...]
    xhat1 = xhat_s[...]
    vecs[1:2, :] = total(grad_first * xhat1)
    vecs[2:3, :] = total(grad_first)
    back = norm_back(grad_first, xhat1, rstd1, g1)
    grad_resid[...] = back
    low = back.astype(BF16)
    grad_attn[...] = low
    vecs[0:1, :] = total(low.astype(F32))
    local = ctx[0].shape[1]
    for s in range(n_t):
        gctx[s] = dot_nt(low, wao[s]).astype(BF16)


def ffn(core, ctx, wao, hid, teach, valid, vec, bup, ups, downs, slab):
    n_t = len(ctx)
    chunk, width = hid.shape
    local = ctx[0].shape[1]
    blocks, _, size = bup.shape
    units = blocks * size
    spots = units // (2 * n_t * slab)
    sd = jax.ShapeDtypeStruct
    vm = pl.BlockSpec(memory_space=pltpu.VMEM)
    sm = pl.BlockSpec(memory_space=pltpu.SMEM)
    hbm = pl.BlockSpec(memory_space=pl.ANY)
    return pl.pallas_call(
        functools.partial(ffn_kernel, n_t, slab),
        in_specs=[sm] + [vm] * (n_t + 6) + [hbm] * 6,
        out_shape=(
            sd((chunk, width), F32),
            sd((chunk, width), BF16),
            sd((chunk, units), BF16),
            sd((chunk, units), BF16),
            sd((chunk, width), BF16),
            sd((chunk, width), BF16),
            sd((chunk, width), BF16),
            sd((chunk, width), F32),
            sd((n_t, chunk, local), BF16),
            sd((8, width), F32),
            sd((blocks, 1, size), F32),
        ),
        scratch_shapes=[
            pltpu.VMEM((units, width), BF16),
            pltpu.VMEM((units, width), BF16),
            pltpu.VMEM((chunk, units), BF16),
            pltpu.VMEM((chunk, width), F32),
            pltpu.SemaphoreType.DMA((8 * spots,)),
        ],
        compiler_params=pltpu.CompilerParams(vmem_limit_bytes=56 << 20),
        cost_estimate=cost(34, 25 << 20),
        name="ffn",
    )(core, *ctx, wao, hid, teach, valid, vec, bup, *ups, *downs)


def shift(x, size, amount):
    return lax.ppermute(x, "tensor", [(j, (j + amount) % size) for j in range(size)])


def swap(x, axis, size, bit):
    return lax.ppermute(x, axis, [(j, j ^ bit) for j in range(size)])


def rows_of(x, start, count):
    return lax.dynamic_slice_in_dim(x, start, count, axis=0)


def body(
    hidden, teacher, valid, w_qkv, b_qv, w_attn_out, b_attn_out, gain_one, bias_one,
    w_up, b_up, w_down, b_down, gain_two, bias_two, table, noise, *, n_d, n_t,
):
    tokens, width = hidden.shape
    units = w_up.shape[1]
    local = w_qkv.shape[2]
    chunk = tokens // n_t
    ti = lax.axis_index("tensor")
    di = lax.axis_index("dp")
    group = min(n_d, 8)
    low_bits = [b for b in (2, 4) if b < group]
    high_bits = low_bits[::-1]
    extra = [b for b in (8, 16, 32, 64, 128, 256, 512) if b < n_d]
    spots = group // 2
    slab = units // group
    piece = local // spots
    core = di % 2
    spot = (di // 2) % spots

    def bit_of(bit):
        return (di // bit) % 2

    def dp_swap(x, bit):
        return swap(x, "dp", n_d, bit)

    def everyone(x):
        bit = 1
        while bit < n_d:
            x = x + dp_swap(x, bit)
            bit *= 2
        return x

    def spread(x, bits, other=None):
        done = []
        for bit in bits:
            if done or other is None:
                other = dp_swap(x, bit)
            up = bit_of(bit) == 1
            pos = sum(1 for b in done if b > bit)
            x = jnp.stack([jnp.where(up, other, x), jnp.where(up, x, other)], axis=pos)
            done.append(bit)
        return x.reshape((-1,) + x.shape[len(done) :])

    def narrow_start(x, bits):
        ax = sorted(bits, reverse=True).index(bits[0])
        up = bit_of(bits[0])
        send = lax.dynamic_index_in_dim(x, 1 - up, ax, keepdims=False)
        keep = lax.dynamic_index_in_dim(x, up, ax, keepdims=False)
        return keep, dp_swap(send, bits[0])

    def narrow(x, bits):
        left = sorted(bits, reverse=True)
        for bit in bits:
            ax = left.index(bit)
            left.remove(bit)
            up = bit_of(bit)
            send = lax.dynamic_index_in_dim(x, 1 - up, ax, keepdims=False)
            keep = lax.dynamic_index_in_dim(x, up, ax, keepdims=False)
            x = (keep.astype(F32) + dp_swap(send, bit).astype(F32)).astype(BF16)
        return x

    def quad_parts(x):
        return [lax.dynamic_index_in_dim(x, spot ^ r, 0, keepdims=False) for r in range(spots)]

    def quad_sum(x):
        pieces = quad_parts(x)
        total = pieces[0].astype(F32)
        for r in range(1, spots):
            total = total + dp_swap(pieces[r], 2 * r).astype(F32)
        return total.astype(BF16)

    def quad_gather(x):
        held = [x] + [dp_swap(x, 2 * r) for r in range(1, spots)]
        step = 1
        while step < spots:
            flip = bit_of(2 * step) == 1
            held = [jnp.where(flip, held[r ^ step], held[r]) for r in range(spots)]
            step *= 2
        return held

    def finish(x):
        for bit in extra:
            x = (x.astype(F32) + dp_swap(x, bit).astype(F32)).astype(BF16)
        return x

    valid_f = valid[0].astype(F32)

    up_own = w_up.T
    b_hi = b_up.astype(BF16)
    b_lo = (b_up - b_hi.astype(F32)).astype(BF16)
    start = core * (spots * slab) + spot * slab
    sent = jnp.concatenate(
        [
            rows_of(up_own, start, slab),
            rows_of(w_attn_out, spot * piece, piece),
            rows_of(w_down, start, slab),
            b_hi[None],
            b_lo[None],
            jnp.zeros((14, width), BF16),
        ]
    )
    came = [shift(sent, n_t, s) for s in range(1, n_t)]

    q3, k3, v3, qt, kt, vt, lmt = attn_prep(hidden, w_qkv, b_qv, table, noise)
    n_sup = tokens // lmt.shape[1]
    cuts = [max(n_sup - 2, 1), max(n_sup - 1, 2)]
    part = attn_fwd(qt, k3, vt, lmt, 0, cuts[0])
    part, came = lax.optimization_barrier((part, came))

    cut = slab + piece
    wide_a = jnp.stack([x[:cut] for x in came])
    wide_b = jnp.stack([x[cut : cut + slab] for x in came])
    first_a = dp_swap(wide_a, low_bits[0])
    first_b = dp_swap(wide_b, high_bits[0])
    part = attn_fwd(qt, k3, vt, lmt, cuts[0], cuts[1], part)
    part, first_a, first_b = lax.optimization_barrier((part, first_a, first_b))
    ctx, ctxt, lse = attn_fwd(qt, k3, vt, lmt, cuts[1], n_sup, part)
    wide_a = spread(wide_a, low_bits, first_a)
    wide_b = spread(wide_b, high_bits, first_b)
    ctx_parts = [rows_of(ctx, ti * chunk, chunk)] + [
        shift(rows_of(ctx, lax.rem(ti + s, n_t) * chunk, chunk), n_t, s) for s in range(1, n_t)
    ]
    *ctx_parts, wide_a, wide_b = lax.optimization_barrier((*ctx_parts, wide_a, wide_b))
    up_m = wide_a[:, :, :slab].reshape(-1, width)
    down_m = wide_b.reshape(-1, width)
    wao = wide_a[:, :, slab:].transpose(1, 0, 2, 3).reshape(n_t - 1, local, width)
    wao = jnp.concatenate([w_attn_out[None], wao])
    up_t = dp_swap(up_m, 1)
    down_t = dp_swap(down_m, 1)
    b_all = jnp.stack(
        [b_up]
        + [x[cut + slab].astype(F32) + x[cut + slab + 1].astype(F32) for x in came]
    ).reshape(n_t, 2, spots, slab)
    b_mine = lax.dynamic_index_in_dim(b_all, core, 1, keepdims=False)
    b_theirs = lax.dynamic_index_in_dim(b_all, 1 - core, 1, keepdims=False)
    bup = jnp.stack([b_mine, b_theirs]).transpose(0, 2, 1, 3).reshape(2 * spots, 1, n_t * slab)

    vec = jnp.stack([b_attn_out, gain_one, bias_one, b_down, gain_two, bias_two, b_down, b_down])
    (out_own, out_low, act, gb, first_low, grad_ffn, grad_attn, grad_resid, gctx_rel, vecs, gbup) = ffn(
        core.reshape(1),
        ctx_parts,
        wao,
        rows_of(hidden, ti * chunk, chunk),
        rows_of(teacher, ti * chunk, chunk),
        lax.dynamic_slice_in_dim(valid_f, ti * chunk, chunk)[:, None],
        vec,
        bup,
        (up_own, up_m, up_t),
        (w_down, down_m, down_t),
        slab,
    )
    out_all = lax.all_gather(out_low, "tensor", axis=0, tiled=True)

    parts = [gctx_rel[0]] + [shift(gctx_rel[s], n_t, -s) for s in range(1, n_t)]
    parts[1], gb, act, first_low, grad_ffn, grad_attn = lax.optimization_barrier(
        (parts[1], gb, act, first_low, grad_ffn, grad_attn)
    )

    up = core == 1
    gbu = gbup.reshape(2, spots, n_t, slab)
    gbu = jnp.where(up, gbu[::-1], gbu).transpose(2, 0, 1, 3).reshape(n_t, units)
    gbu = gbu[jnp.stack([lax.rem(ti - z + n_t, n_t) for z in range(n_t)])]
    pack = jnp.concatenate([vecs.reshape(-1), gbu.reshape(-1)]).reshape(-1, 128)
    pack = everyone(pack)
    bit = 1
    while bit < n_t:
        pack = pack + swap(pack, "tensor", n_t, bit)
        bit *= 2

    half = n_t * units // 2
    lead = (2,) * len(low_bits)
    send_up = dot_tn(gb[:, half:], first_low).astype(BF16).reshape(spots, n_t, slab, width)
    g_ao = jnp.stack([dot_tn(c, grad_attn) for c in ctx_parts]).astype(BF16)
    g_ao = g_ao.reshape(n_t, spots, piece, width).transpose(1, 0, 2, 3)
    send_a = jnp.concatenate([send_up, g_ao], axis=2)
    send_b = dot_tn(act[:, half:], grad_ffn).astype(BF16)
    got_a = dp_swap(send_a, 1)
    got_b = dp_swap(send_b, 1)
    parts[3], gb, act = lax.optimization_barrier((parts[3], gb, act))
    keep_up = dot_tn(gb[:, :half], first_low).reshape(spots, n_t, slab, width)
    keep_a = jnp.concatenate([keep_up.astype(BF16), g_ao], axis=2)
    g_a = (keep_a.astype(F32) + got_a.astype(F32)).astype(BF16)
    g_b = (dot_tn(act[:, :half], grad_ffn) + got_b.astype(F32)).astype(BF16)
    parts[2], g_a, g_b, pack = lax.optimization_barrier((parts[2], g_a, g_b, pack))
    a_keep, a_came = narrow_start(g_a.reshape(lead + (n_t, cut, width)), low_bits)
    b_keep, b_came = narrow_start(g_b.reshape(lead + (n_t, slab, width)), high_bits)

    gqkv, glm = attn_bwd(ti.reshape(1), parts, ctxt, q3, k3, v3, qt, kt, lse, lmt)
    back = jnp.einsum("kte,kde->td", gqkv, w_qkv, preferred_element_type=F32)
    mine = (jnp.arange(n_t) == ti)[:, None, None]
    back = back.reshape(n_t, chunk, width) + jnp.where(mine, grad_resid[None], 0.0)
    back = back.reshape(tokens, width).astype(BF16)
    grad_hidden = lax.psum(back, "tensor")
    gqkv, glm, a_keep, a_came, b_keep, b_came, _ = lax.optimization_barrier(
        (gqkv, glm, a_keep, a_came, b_keep, b_came, back)
    )
    g_a = finish(narrow((a_keep.astype(F32) + a_came.astype(F32)).astype(BF16), low_bits[1:]))
    g_b = finish(narrow((b_keep.astype(F32) + b_came.astype(F32)).astype(BF16), high_bits[1:]))

    g_qkv_w = [dot_tn(hidden, gqkv[n]).astype(BF16) for n in range(3)]
    slope = jax.nn.sigmoid((table + noise) * (-1.0 / SOFTENING)) * (1.0 / SOFTENING)
    g_mask = (glm * slope).astype(BF16).reshape(2, -1, table.shape[2])
    tail = jnp.concatenate([g_mask[0], g_mask[1]] + g_qkv_w, axis=1)
    tail = tail.reshape(2, spots, -1, tail.shape[1])
    send = lax.dynamic_index_in_dim(tail, 1 - core, 0, keepdims=False)
    keep = lax.dynamic_index_in_dim(tail, core, 0, keepdims=False)
    tail = (keep.astype(F32) + dp_swap(send, 1).astype(F32)).astype(BF16)
    tail = jnp.concatenate(quad_gather(finish(quad_sum(tail))))
    other = dp_swap(tail, 1)
    tail = jnp.concatenate([jnp.where(up, other, tail), jnp.where(up, tail, other)])
    cols = table.shape[2]
    g_mask = jnp.stack([tail[:, :cols], tail[:, cols : 2 * cols]])
    g_qkv_w = jnp.stack([tail[:, 2 * cols + n * local : 2 * cols + (n + 1) * local] for n in range(3)])
    g_b_qv = everyone(jnp.sum(gqkv[0::2].astype(F32), axis=1))

    g_a, g_b, out_all = lax.optimization_barrier((g_a, g_b, out_all))
    out_states = out_all.astype(F32)
    total = jnp.concatenate([g_a, g_b], axis=1)
    summed = total[0].astype(F32)
    for s in range(1, n_t):
        summed = summed + shift(total[s], n_t, -s).astype(F32)
    summed = summed.astype(BF16)
    held = quad_gather(summed)
    g_ao = jnp.concatenate([x[slab:cut] for x in held])
    pair = jnp.stack([jnp.concatenate([x[:slab] for x in held]), jnp.concatenate([x[cut:] for x in held])])
    other = dp_swap(pair, 1)
    pair = jnp.concatenate([jnp.where(up, other, pair), jnp.where(up, pair, other)], axis=1)
    g_up = pair[0].T
    g_down = pair[1]

    pack = pack.reshape(-1)
    rows = [pack[n * width : (n + 1) * width] for n in range(8)]
    gbu = lax.dynamic_slice_in_dim(pack, 8 * width + ti * units, units)
    total_valid = rows[7][0]
    loss = jnp.sum(rows[6]) / (total_valid * width)
    coef = 2.0 * tokens / total_valid
    grads = [
        grad_hidden, g_qkv_w.reshape(w_qkv.shape), g_b_qv.reshape(2, local), g_ao, rows[0], rows[1], rows[2],
        g_up, gbu, g_down, rows[3], rows[4], rows[5], g_mask.reshape(table.shape),
    ]
    return (out_states, loss, *[g.astype(F32) * coef for g in grads])


def solution(mesh):
    row, col = P("tensor", None), P(None, "tensor")
    heads = P("tensor", None, None)
    dp = P("dp", None)
    qkv = P(None, None, "tensor")
    sizes = dict(mesh.shape)
    return jax.shard_map(
        functools.partial(body, n_d=sizes["dp"], n_t=sizes["tensor"]),
        mesh=mesh,
        in_specs=(dp, dp, dp, qkv, col, row, P(), P(), P(), col, P("tensor"), row, P(), P(), P(), heads, heads),
        out_specs=(dp, P(), dp, qkv, col, row, P(), P(), P(), col, P("tensor"), row, P(), P(), P(), heads),
        check_vma=False,
    )
```

```python
import functools
import math

import jax
import jax.numpy as jnp
from jax import lax
from jax.experimental import pallas as pl
from jax.experimental.pallas import tpu as pltpu
from jax.sharding import PartitionSpec as P

BLOCK = 256
LOG2E = math.log2(math.e)
SOFTENING = 0.5
EPS = 1e-6
F32 = jnp.float32
BF16 = jnp.bfloat16


def dot(a, b):
    return jnp.dot(a, b, preferred_element_type=F32)


def dot_nt(a, b):
    return lax.dot_general(a, b, (((1,), (1,)), ((), ())), preferred_element_type=F32)


def dot_tn(a, b):
    return lax.dot_general(a, b, (((0,), (0,)), ((), ())), preferred_element_type=F32)


def dot_tt(a, b):
    return lax.dot_general(a, b, (((0,), (1,)), ((), ())), preferred_element_type=F32)


def cost(micros, moved):
    return pl.CostEstimate(flops=int(micros * 1e9), transcendentals=0, bytes_accessed=moved)


def prep_kernel(hid, w, b, bt, table, noise, q3, k3, v3, qt, kt, vt, lmt):
    heads = table.shape[0]
    tokens = hid.shape[0]
    hd = q3.shape[2]
    for h in range(heads):
        x = (table[h] + noise[h]) * (1.0 / SOFTENING)
        ls = jnp.minimum(x, 0.0) - jnp.log1p(jnp.exp(-jnp.abs(x)))
        lmt[h] = jnp.transpose(ls * LOG2E)

    step = 2 * BLOCK

    def project(i, _):
        rows = pl.ds(pl.multiple_of(i * step, step), step)
        x = hid[rows, :]
        for n, (nat, tr) in enumerate(((q3, qt), (k3, kt), (v3, vt))):
            y = dot(x, w[n])
            yt = dot_tt(w[n], x)
            if n != 1:
                y = y + b[n // 2 : n // 2 + 1, :]
                yt = yt + bt[:, n // 2 : n // 2 + 1]
            y = y.astype(BF16)
            for h in range(heads):
                nat[h, rows, :] = y[:, h * hd : (h + 1) * hd]
            tr[:, rows] = yt.astype(BF16)
        return 0

    lax.fori_loop(0, tokens // step, project, 0)


def attn_prep(hidden, w_qkv, b_qv, table, noise):
    tokens = hidden.shape[0]
    heads = table.shape[0]
    width = w_qkv.shape[2]
    sd = jax.ShapeDtypeStruct
    nat = sd((heads, tokens, width // heads), BF16)
    tr = sd((width, tokens), BF16)
    return pl.pallas_call(
        prep_kernel,
        out_shape=(nat, nat, nat, tr, tr, tr, sd(table.shape, F32)),
        compiler_params=pltpu.CompilerParams(vmem_limit_bytes=56 << 20),
        cost_estimate=cost(15, 20 << 20),
        name="attn_prep",
    )(hidden, w_qkv, b_qv, b_qv.T, table, noise)


def attn_fwd_kernel(lo, n_prev, qt, k3, vt, lmt, *refs):
    ctx, ctxt, lse = refs[n_prev:]
    heads, tokens, hd = k3.shape
    period = lmt.shape[1]
    width = heads * hd
    coef = LOG2E / math.sqrt(hd)
    parts = period // BLOCK
    lse[...] = jnp.zeros(lse.shape, F32)
    first = (pl.program_id(0) + lo) * parts

    def per_q(j, _):
        qb = first + j
        qcol = pl.ds(pl.multiple_of(qb * BLOCK, BLOCK), BLOCK)
        ocol = pl.ds(pl.multiple_of(j * BLOCK, BLOCK), BLOCK)
        mcol = ocol

        def per_k(kb, carry):
            krow = pl.ds(pl.multiple_of(kb * BLOCK, BLOCK), BLOCK)
            mrow = pl.ds(pl.multiple_of(lax.rem(kb, parts) * BLOCK, BLOCK), BLOCK)
            out = []
            ss = [dot(k3[h, krow, :], qt[h * hd : (h + 1) * hd, qcol]) for h in range(heads)]
            for h in range(heads):
                m, l, acc = carry[h]
                s = ss[h] * coef + lmt[h, mrow, mcol]
                mn = jnp.maximum(m, jnp.max(s, axis=0, keepdims=True))
                al = jnp.exp2(m - mn)
                p = jnp.exp2(s - mn)
                l = l * al + jnp.sum(p, axis=0, keepdims=True)
                acc = acc * al + dot(vt[h * hd : (h + 1) * hd, krow], p.astype(BF16))
                out.append((mn, l, acc))
            return tuple(out)

        init = tuple(
            (
                jnp.full((1, BLOCK), -1e30, F32),
                jnp.zeros((1, BLOCK), F32),
                jnp.zeros((hd, BLOCK), F32),
            )
            for _ in range(heads)
        )
        res = lax.fori_loop(0, qb + 1, per_k, init)
        cols = []
        for h in range(heads):
            m, l, acc = res[h]
            c = acc / l
            ctxt[h * hd : (h + 1) * hd, ocol] = c
            lse[h : h + 1, ocol] = m + jnp.log2(l)
            cols.append(c)
        pad = -width % 128
        if pad:
            cols.append(jnp.zeros((pad, BLOCK), F32))
        full = jnp.transpose(jnp.concatenate(cols, axis=0))
        ctx[ocol, :] = full[:, :width].astype(BF16)
        return 0

    lax.fori_loop(0, parts, per_q, 0)


def attn_fwd(qt, k3, vt, lmt, lo, hi, prev=()):
    heads, tokens, hd = k3.shape
    width = heads * hd
    period = lmt.shape[1]
    sd = jax.ShapeDtypeStruct
    whole = lambda x: pl.BlockSpec(x.shape, lambda i, n=len(x.shape): (0,) * n)
    return pl.pallas_call(
        functools.partial(attn_fwd_kernel, lo, len(prev)),
        grid=(hi - lo,),
        in_specs=[whole(x) for x in (qt, k3, vt, lmt)] + [pl.BlockSpec(memory_space=pl.ANY)] * len(prev),
        out_specs=(
            pl.BlockSpec((period, width), lambda i: (i + lo, 0)),
            pl.BlockSpec((width, period), lambda i: (0, i + lo)),
            pl.BlockSpec((8, period), lambda i: (0, i + lo)),
        ),
        out_shape=(sd((tokens, width), BF16), sd((width, tokens), F32), sd((8, tokens), F32)),
        input_output_aliases={4 + n: n for n in range(len(prev))},
        compiler_params=pltpu.CompilerParams(vmem_limit_bytes=56 << 20),
        cost_estimate=cost(1.5 * (hi * hi - lo * lo) / 2, 8 << 20),
        name="attn_fwd",
    )(qt, k3, vt, lmt, *prev)


def attn_bwd_kernel(n_t, place, *refs):
    pieces = refs[:n_t]
    (ctxt, q3, k3, v3, qt, kt, lse, lmt, gqkv, glm, gk, gv, g3, glmt, gctx, sems) = refs[n_t:]
    heads, tokens, hd = q3.shape
    chunk = tokens // n_t
    copies = []
    for s in range(n_t):
        at = lax.rem(place[0] + s, n_t) * chunk
        to = gctx.at[pl.ds(pl.multiple_of(at, chunk), chunk), :]
        copies.append(pltpu.make_async_copy(pieces[s], to, sems.at[s]))
    for cp in copies:
        cp.start()
    period = lmt.shape[1]
    width = heads * hd
    coef = LOG2E / math.sqrt(hd)
    scale = 1.0 / math.sqrt(hd)
    parts = period // BLOCK
    pad = -width % 128
    gk[...] = jnp.zeros(gk.shape, F32)
    gv[...] = jnp.zeros(gv.shape, F32)
    glmt[...] = jnp.zeros(glmt.shape, F32)
    for cp in copies:
        cp.wait()

    def per_q(i, _):
        qb = tokens // BLOCK - 1 - i
        qcol = pl.ds(pl.multiple_of(qb * BLOCK, BLOCK), BLOCK)
        mcol = pl.ds(pl.multiple_of(lax.rem(qb, parts) * BLOCK, BLOCK), BLOCK)
        g = gctx[qcol, :].astype(F32)
        gpad = jnp.concatenate([g, jnp.zeros((BLOCK, pad), F32)], axis=1) if pad else g
        gt = jnp.transpose(gpad)
        delta, gtb = [], []
        for h in range(heads):
            gth = gt[h * hd : (h + 1) * hd, :]
            delta.append(jnp.sum(gth * ctxt[h * hd : (h + 1) * hd, qcol], axis=0, keepdims=True))
            gtb.append(gth.astype(BF16))
            g3[h] = gctx[qcol, h * hd : (h + 1) * hd]

        def per_k(kb, carry):
            krow = pl.ds(pl.multiple_of(kb * BLOCK, BLOCK), BLOCK)
            mrow = pl.ds(pl.multiple_of(lax.rem(kb, parts) * BLOCK, BLOCK), BLOCK)
            out = []
            for h in range(heads):
                hs = slice(h * hd, (h + 1) * hd)
                s = dot(k3[h, krow, :], qt[hs, qcol]) * coef + lmt[h, mrow, mcol]
                p = jnp.exp2(s - lse[h : h + 1, qcol])
                dp = dot(v3[h, krow, :], gtb[h])
                ds = p * (dp - delta[h])
                dsb = ds.astype(BF16)
                glmt[h, mrow, mcol] += ds
                gv[h, krow, :] += dot(p.astype(BF16), g3[h])
                gk[h, krow, :] += dot(dsb, q3[h, qcol, :])
                out.append(carry[h] + dot(kt[hs, krow], dsb))
            return tuple(out)

        init = tuple(jnp.zeros((hd, BLOCK), F32) for _ in range(heads))
        res = lax.fori_loop(0, qb + 1, per_k, init)
        rows = [r * scale for r in res]
        if pad:
            rows.append(jnp.zeros((pad, BLOCK), F32))
        gq = jnp.transpose(jnp.concatenate(rows, axis=0))[:, :width]
        gkb = jnp.concatenate([gk[h, qcol, :] for h in range(heads)], axis=1) * scale
        gvb = jnp.concatenate([gv[h, qcol, :] for h in range(heads)], axis=1)
        rows = [gq, gkb, gvb]
        if gqkv.shape[1] > 3 * width:
            rows.append(jnp.zeros((BLOCK, gqkv.shape[1] - 3 * width), F32))
        gqkv[qcol, :] = jnp.concatenate(rows, axis=1).astype(BF16)
        return 0

    lax.fori_loop(0, tokens // BLOCK, per_q, 0)
    for h in range(heads):
        glm[h] = jnp.transpose(glmt[h])


def attn_bwd(place, parts, ctxt, q3, k3, v3, qt, kt, lse, lmt):
    heads, tokens, hd = q3.shape
    width = heads * hd
    n_t = len(parts)
    sd = jax.ShapeDtypeStruct
    vm = pl.BlockSpec(memory_space=pltpu.VMEM)
    return pl.pallas_call(
        functools.partial(attn_bwd_kernel, n_t),
        in_specs=[pl.BlockSpec(memory_space=pltpu.SMEM)] + [pl.BlockSpec(memory_space=pl.ANY)] * n_t + [vm] * 8,
        out_shape=(sd((tokens, -(-3 * width // 128) * 128), BF16), sd(lmt.shape, F32)),
        scratch_shapes=[
            pltpu.VMEM((heads, tokens, hd), F32),
            pltpu.VMEM((heads, tokens, hd), F32),
            pltpu.VMEM((heads, BLOCK, hd), BF16),
            pltpu.VMEM(lmt.shape, F32),
            pltpu.VMEM((tokens, width), BF16),
            pltpu.SemaphoreType.DMA((n_t,)),
        ],
        compiler_params=pltpu.CompilerParams(vmem_limit_bytes=56 << 20),
        cost_estimate=cost(400, 20 << 20),
        name="attn_bwd",
    )(place, *parts, ctxt, q3, k3, v3, qt, kt, lse, lmt)


def wgrad_kernel(slab, gb, first, act, grad_ffn, grad_attn, *refs):
    ctx, (to, ao) = refs[:-2], refs[-2:]
    i = pl.program_id(0)
    n_t = len(ctx)
    piece = to.shape[2] - 2 * slab

    @pl.when(i == 0)
    def _():
        for z in range(n_t):
            ao[z] = dot_tn(ctx[z][...], grad_attn[...]).astype(BF16)

    up = dot_tn(gb[...], first[...]).astype(BF16)
    down = dot_tn(act[...], grad_ffn[...]).astype(BF16)
    rows = pl.ds(pl.multiple_of(i * piece, piece), piece)
    for z in range(n_t):
        to[0, z, :slab, :] = up[z * slab : (z + 1) * slab]
        to[0, z, slab : slab + piece, :] = ao[z, rows, :]
        to[0, z, slab + piece :, :] = down[z * slab : (z + 1) * slab]


def wgrad(slab, spots, gb, first, act, grad_ffn, grad_attn, ctx):
    chunk, width = first.shape
    n_t = len(ctx)
    local = ctx[0].shape[1]
    wide = n_t * slab
    tall = 2 * slab + local // spots
    vm = pl.BlockSpec(memory_space=pltpu.VMEM)
    cols = pl.BlockSpec((chunk, wide), lambda i: (0, i))
    return pl.pallas_call(
        functools.partial(wgrad_kernel, slab),
        grid=(spots,),
        in_specs=[cols, vm, cols, vm, vm] + [vm] * n_t,
        out_specs=pl.BlockSpec((1, n_t, tall, width), lambda i: (i, 0, 0, 0)),
        out_shape=jax.ShapeDtypeStruct((spots, n_t, tall, width), BF16),
        scratch_shapes=[pltpu.VMEM((n_t, local, width), BF16)],
        compiler_params=pltpu.CompilerParams(vmem_limit_bytes=40 << 20),
        cost_estimate=cost(60, 10 << 20),
        name="wgrad",
    )(gb, first, act, grad_ffn, grad_attn, *ctx)


def tail_kernel(hid, gqkv, glm, table, noise, tail, acc):
    heads, period, _ = glm.shape
    tokens, width = hid.shape
    wide = acc.shape[1]
    tall, lanes = tail.shape
    at = 2 * period + wide
    extra = lanes - at
    step = 2 * BLOCK
    for n in range(heads * period // BLOCK):
        h, at = n * BLOCK // period, n * BLOCK % period
        x = (table[h, at : at + BLOCK, :] + noise[h, at : at + BLOCK, :]) * (1.0 / SOFTENING)
        e = jnp.exp(-jnp.abs(x))
        slope = jnp.where(x > 0, e, 1.0) / (1.0 + e) * (1.0 / SOFTENING)
        g = (glm[h, at : at + BLOCK, :] * slope).astype(BF16)
        row, col = n * BLOCK % tall, n * BLOCK // tall * period
        tail[row : row + BLOCK, col : col + period] = g
    acc[...] = jnp.zeros(acc.shape, F32)

    def add(i, total):
        rows = pl.ds(pl.multiple_of(i * step, step), step)
        y = gqkv[rows, :wide]
        acc[...] += dot_tn(hid[rows, :], y)
        return total + jnp.sum(y.astype(F32), axis=0, keepdims=True)

    total = lax.fori_loop(0, tokens // step, add, jnp.zeros((1, wide), F32))
    rows = [total[:, n * extra : (n + 1) * extra] for n in range(wide // extra)]
    rows.append(jnp.zeros((tall - len(rows), extra), F32))
    tail[:, 2 * period :] = jnp.concatenate([acc[...], jnp.concatenate(rows, axis=0)], axis=1).astype(BF16)


def tail_of(hidden, gqkv, glm, table, noise, wide):
    heads, period, _ = glm.shape
    width = hidden.shape[1]
    lanes = 2 * period + wide
    sd = jax.ShapeDtypeStruct
    return pl.pallas_call(
        tail_kernel,
        out_shape=sd((heads * period // 2, -(-lanes // 128) * 128), BF16),
        scratch_shapes=[pltpu.VMEM((width, wide), F32)],
        compiler_params=pltpu.CompilerParams(vmem_limit_bytes=56 << 20),
        cost_estimate=cost(400, 20 << 20),
        name="tail",
    )(hidden, gqkv, glm, table, noise)


def back_kernel(place, w, resid, *refs):
    pieces, out = refs[:-1], refs[-1]
    n_t, wide, _ = w.shape
    total = resid[...]
    for s in range(n_t):
        total = total + dot(pieces[s][:, :wide], w[lax.rem(place[0] + n_t - s, n_t)])
    out[...] = total.astype(BF16)


def back_of(place, w, resid, pieces):
    vm = pl.BlockSpec(memory_space=pltpu.VMEM)
    return pl.pallas_call(
        back_kernel,
        in_specs=[pl.BlockSpec(memory_space=pltpu.SMEM)] + [vm] * (2 + len(pieces)),
        out_shape=jax.ShapeDtypeStruct(resid.shape, BF16),
        compiler_params=pltpu.CompilerParams(vmem_limit_bytes=40 << 20),
        cost_estimate=cost(5, 10 << 20),
        name="back",
    )(place, w, resid, *pieces)


def norm_parts(resid):
    centred = resid - jnp.mean(resid, axis=-1, keepdims=True)
    rstd = lax.rsqrt(jnp.mean(centred * centred, axis=-1, keepdims=True) + EPS)
    return centred * rstd, rstd


def norm_back(grad, xhat, rstd, gain):
    gy = grad * gain
    return rstd * (
        gy
        - jnp.mean(gy, axis=-1, keepdims=True)
        - xhat * jnp.mean(gy * xhat, axis=-1, keepdims=True)
    )


def ffn_kernel(
    n_t, slab, core, *refs
):
    ctx = refs[:n_t]
    (wao, hid, teach, valid, vec, bup, up_o, up_m, up_t, dn_o, dn_m, dn_t,
     out, out_low, act_k, act_s, gb_k, gb_s, first_low, grad_ffn, grad_attn, grad_resid, vecs, gbup) = (
        refs[n_t : n_t + 24]
    )
    gctx = refs[n_t + 24 : 2 * n_t + 24]
    up_s, dn_s, slope, xhat_s, sems = refs[2 * n_t + 24 :]
    units, width = up_s.shape
    half = units // 2
    spots = half // (n_t * slab)
    c = core[0]
    copies = []
    for n, (o, m, t, dst) in enumerate(((up_o, up_m, up_t, up_s), (dn_o, dn_m, dn_t, dn_s))):
        for side, f in enumerate((m, t)):
            base = (c if side == 0 else 1 - c) * (spots * slab)
            for p in range(spots):
                to = side * half + p * n_t * slab
                copies.append((n, o.at[pl.ds(pl.multiple_of(base + p * slab, slab), slab)], dst.at[pl.ds(to, slab)]))
                rest = (n_t - 1) * slab
                copies.append((n, f.at[pl.ds(p * rest, rest)], dst.at[pl.ds(to + slab, rest)]))
    copies = [pltpu.make_async_copy(a, b, sems.at[i]) for i, (n, a, b) in enumerate(copies)]
    for cp in copies:
        cp.start()
    b_ao, g1, b1, b_dn, g2, b2 = (vec[n : n + 1, :] for n in range(6))
    attention = sum(dot(ctx[s][...], wao[s]) for s in range(n_t)) + b_ao
    xhat1, rstd1 = norm_parts(hid[...].astype(F32) + attention)
    first = xhat1 * g1 + b1
    first_low[...] = first.astype(BF16)
    xhat_s[...] = xhat1
    for cp in copies:
        cp.wait()
    blocks, _, size = bup.shape

    def halves(i, kept, sent, value):
        @pl.when(i < spots)
        def _():
            kept[:, pl.ds(pl.multiple_of(i * size, size), size)] = value

        @pl.when(i >= spots)
        def _():
            sent[:, pl.ds(pl.multiple_of((i - spots) * size, size), size)] = value

    def forward(i, feed):
        rows = pl.ds(pl.multiple_of(i * size, size), size)
        before = dot_nt(first_low[...], up_s[rows, :]) + bup[i]
        phi = 0.5 * (1.0 + lax.erf(before * math.sqrt(0.5)))
        dens = jnp.exp(-0.5 * before * before) * (1.0 / math.sqrt(2.0 * math.pi))
        low = (before * phi).astype(BF16)
        halves(i, act_k, act_s, low)
        slope[:, rows] = (phi + before * dens).astype(BF16)
        return feed + dot(low, dn_s[rows, :])

    feed = lax.fori_loop(0, blocks, forward, jnp.zeros(out.shape, F32))
    xhat2, rstd2 = norm_parts(first + feed + b_dn)
    own = xhat2 * g2 + b2
    out[...] = own
    out_low[...] = own.astype(BF16)
    residue = own - teach[...]
    weighed = valid[...] * residue
    grad_out = weighed
    total = lambda x: jnp.sum(x, axis=0, keepdims=True)
    vecs[4:5, :] = total(grad_out * xhat2)
    vecs[5:6, :] = total(grad_out)
    vecs[6:7, :] = total(weighed * residue)
    vecs[7:8, :] = jnp.broadcast_to(jnp.sum(valid[...], axis=0, keepdims=True), (1, width))
    grad_second = norm_back(grad_out, xhat2, rstd2, g2)
    grad_resid[...] = grad_second
    low = grad_second.astype(BF16)
    grad_ffn[...] = low
    vecs[3:4, :] = total(low.astype(F32))

    def backward(i, acc):
        rows = pl.ds(pl.multiple_of(i * size, size), size)
        g = dot_nt(grad_ffn[...], dn_s[rows, :]) * slope[:, rows].astype(F32)
        low = g.astype(BF16)
        halves(i, gb_k, gb_s, low)
        gbup[i] = total(low.astype(F32))
        return acc + dot(low, up_s[rows, :])

    grad_first = lax.fori_loop(0, blocks, backward, jnp.zeros(out.shape, F32)) + grad_resid[...]
    xhat1 = xhat_s[...]
    vecs[1:2, :] = total(grad_first * xhat1)
    vecs[2:3, :] = total(grad_first)
    back = norm_back(grad_first, xhat1, rstd1, g1)
    grad_resid[...] = back
    low = back.astype(BF16)
    grad_attn[...] = low
    vecs[0:1, :] = total(low.astype(F32))
    local = ctx[0].shape[1]
    for s in range(n_t):
        gctx[s][...] = dot_nt(low, wao[s]).astype(BF16)


def ffn(core, ctx, wao, hid, teach, valid, vec, bup, ups, downs, slab):
    n_t = len(ctx)
    chunk, width = hid.shape
    local = ctx[0].shape[1]
    blocks, _, size = bup.shape
    units = blocks * size
    spots = units // (2 * n_t * slab)
    sd = jax.ShapeDtypeStruct
    vm = pl.BlockSpec(memory_space=pltpu.VMEM)
    sm = pl.BlockSpec(memory_space=pltpu.SMEM)
    hbm = pl.BlockSpec(memory_space=pl.ANY)
    return pl.pallas_call(
        functools.partial(ffn_kernel, n_t, slab),
        in_specs=[sm] + [vm] * (n_t + 6) + [hbm] * 6,
        out_shape=(
            sd((chunk, width), F32),
            sd((chunk, width), BF16),
            *[sd((chunk, units // 2), BF16)] * 4,
            sd((chunk, width), BF16),
            sd((chunk, width), BF16),
            sd((chunk, width), BF16),
            sd((chunk, width), F32),
            sd((8, width), F32),
            sd((blocks, 1, size), F32),
            *[sd((chunk, local), BF16)] * n_t,
        ),
        scratch_shapes=[
            pltpu.VMEM((units, width), BF16),
            pltpu.VMEM((units, width), BF16),
            pltpu.VMEM((chunk, units), BF16),
            pltpu.VMEM((chunk, width), F32),
            pltpu.SemaphoreType.DMA((8 * spots,)),
        ],
        compiler_params=pltpu.CompilerParams(vmem_limit_bytes=56 << 20),
        cost_estimate=cost(34, 25 << 20),
        name="ffn",
    )(core, *ctx, wao, hid, teach, valid, vec, bup, *ups, *downs)


def shift(x, size, amount):
    return lax.ppermute(x, "tensor", [(j, (j + amount) % size) for j in range(size)])


def swap(x, axis, size, bit):
    return lax.ppermute(x, axis, [(j, j ^ bit) for j in range(size)])


def rows_of(x, start, count):
    return lax.dynamic_slice_in_dim(x, start, count, axis=0)


def body(
    hidden, teacher, valid, w_qkv, b_qv, w_attn_out, b_attn_out, gain_one, bias_one,
    w_up, b_up, w_down, b_down, gain_two, bias_two, table, noise, *, n_d, n_t,
):
    tokens, width = hidden.shape
    units = w_up.shape[1]
    local = w_qkv.shape[2]
    chunk = tokens // n_t
    ti = lax.axis_index("tensor")
    di = lax.axis_index("dp")
    group = min(n_d, 8)
    low_bits = [b for b in (2, 4) if b < group]
    high_bits = low_bits[::-1]
    extra = [b for b in (8, 16, 32, 64, 128, 256, 512) if b < n_d]
    spots = group // 2
    slab = units // group
    piece = local // spots
    core = di % 2
    spot = (di // 2) % spots

    def bit_of(bit):
        return (di // bit) % 2

    def dp_swap(x, bit):
        return swap(x, "dp", n_d, bit)

    def everyone(x):
        bit = 1
        while bit < n_d:
            x = x + dp_swap(x, bit)
            bit *= 2
        return x

    def spread(x, bits, other=None):
        done = []
        for bit in bits:
            if done or other is None:
                other = dp_swap(x, bit)
            up = bit_of(bit) == 1
            pos = sum(1 for b in done if b > bit)
            x = jnp.stack([jnp.where(up, other, x), jnp.where(up, x, other)], axis=pos)
            done.append(bit)
        return x.reshape((-1,) + x.shape[len(done) :])

    def narrow_start(x, bits):
        ax = sorted(bits, reverse=True).index(bits[0])
        up = bit_of(bits[0])
        send = lax.dynamic_index_in_dim(x, 1 - up, ax, keepdims=False)
        keep = lax.dynamic_index_in_dim(x, up, ax, keepdims=False)
        return keep, dp_swap(send, bits[0])

    def narrow_pair(x, y, bits):
        ax = sorted(bits, reverse=True).index(bits[0])
        up = bit_of(bits[0])
        part = lambda v, i: lax.dynamic_index_in_dim(v, i, ax, keepdims=False).astype(F32)
        send = (part(x, 1 - up) + part(y, 1 - up)).astype(BF16)
        keep = (part(x, up) + part(y, up)).astype(BF16)
        return keep, send, bits[0]

    def narrow(x, bits):
        left = sorted(bits, reverse=True)
        for bit in bits:
            ax = left.index(bit)
            left.remove(bit)
            up = bit_of(bit)
            send = lax.dynamic_index_in_dim(x, 1 - up, ax, keepdims=False)
            keep = lax.dynamic_index_in_dim(x, up, ax, keepdims=False)
            x = (keep.astype(F32) + dp_swap(send, bit).astype(F32)).astype(BF16)
        return x

    def quad_parts(x):
        return [lax.dynamic_index_in_dim(x, spot ^ r, 0, keepdims=False) for r in range(spots)]

    def quad_sum(x):
        pieces = quad_parts(x)
        total = pieces[0].astype(F32)
        for r in range(1, spots):
            total = total + dp_swap(pieces[r], 2 * r).astype(F32)
        return total.astype(BF16)

    def quad_gather(x):
        held = [x] + [dp_swap(x, 2 * r) for r in range(1, spots)]
        step = 1
        while step < spots:
            flip = bit_of(2 * step) == 1
            held = [jnp.where(flip, held[r ^ step], held[r]) for r in range(spots)]
            step *= 2
        return held

    def finish(x):
        for bit in extra:
            x = (x.astype(F32) + dp_swap(x, bit).astype(F32)).astype(BF16)
        return x

    valid_f = valid[0].astype(F32)

    up_own = w_up.T
    b_hi = b_up.astype(BF16)
    b_lo = (b_up - b_hi.astype(F32)).astype(BF16)
    start = core * (spots * slab) + spot * slab
    sent = jnp.concatenate(
        [
            rows_of(up_own, start, slab),
            rows_of(w_attn_out, spot * piece, piece),
            rows_of(w_down, start, slab),
            b_hi[None],
            b_lo[None],
            jnp.zeros((14, width), BF16),
        ]
    )
    came = [shift(sent, n_t, s) for s in range(1, n_t)]

    w_t = w_qkv.transpose(0, 2, 1).reshape(3 * local, width)
    w_t = rows_of(w_t, core * (3 * local // 2), 3 * local // 2)
    q3, k3, v3, qt, kt, vt, lmt = attn_prep(hidden, w_qkv, b_qv, table, noise)
    n_sup = tokens // lmt.shape[1]
    cuts = [max(n_sup - 2, 1), max(n_sup - 1, 2)]
    part = attn_fwd(qt, k3, vt, lmt, 0, cuts[0])
    part, came, w_t = lax.optimization_barrier((part, came, w_t))
    w_side = lax.all_gather(w_t, "tensor", axis=0)

    cut = slab + piece
    wide_a = jnp.stack([x[:cut] for x in came])
    wide_b = jnp.stack([x[cut : cut + slab] for x in came])
    first_a = dp_swap(wide_a, low_bits[0])
    first_b = dp_swap(wide_b, high_bits[0])
    part = attn_fwd(qt, k3, vt, lmt, cuts[0], cuts[1], part)
    part, first_a, first_b = lax.optimization_barrier((part, first_a, first_b))
    ctx, ctxt, lse = attn_fwd(qt, k3, vt, lmt, cuts[1], n_sup, part)
    wide_a = spread(wide_a, low_bits, first_a)
    wide_b = spread(wide_b, high_bits, first_b)
    ctx_parts = [rows_of(ctx, ti * chunk, chunk)] + [
        shift(rows_of(ctx, lax.rem(ti + s, n_t) * chunk, chunk), n_t, s) for s in range(1, n_t)
    ]
    *ctx_parts, wide_a, wide_b, w_side = lax.optimization_barrier((*ctx_parts, wide_a, wide_b, w_side))
    up_m = wide_a[:, :, :slab].reshape(-1, width)
    down_m = wide_b.reshape(-1, width)
    wao = wide_a[:, :, slab:].transpose(1, 0, 2, 3).reshape(n_t - 1, local, width)
    wao = jnp.concatenate([w_attn_out[None], wao])
    up_t = dp_swap(up_m, 1)
    down_t = dp_swap(down_m, 1)
    b_all = jnp.stack(
        [b_up]
        + [x[cut + slab].astype(F32) + x[cut + slab + 1].astype(F32) for x in came]
    ).reshape(n_t, 2, spots, slab)
    b_mine = lax.dynamic_index_in_dim(b_all, core, 1, keepdims=False)
    b_theirs = lax.dynamic_index_in_dim(b_all, 1 - core, 1, keepdims=False)
    bup = jnp.stack([b_mine, b_theirs]).transpose(0, 2, 1, 3).reshape(2 * spots, 1, n_t * slab)

    w_other = dp_swap(w_side, 1)
    vec = jnp.stack([b_attn_out, gain_one, bias_one, b_down, gain_two, bias_two, b_down, b_down])
    (out_own, out_low, act_k, act_s, gb_k, gb_s, first_low, grad_ffn, grad_attn, grad_resid, vecs, gbup, *gctx_rel) = ffn(
        core.reshape(1),
        ctx_parts,
        wao,
        rows_of(hidden, ti * chunk, chunk),
        rows_of(teacher, ti * chunk, chunk),
        lax.dynamic_slice_in_dim(valid_f, ti * chunk, chunk)[:, None],
        vec,
        bup,
        (up_own, up_m, up_t),
        (w_down, down_m, down_t),
        slab,
    )

    vecs, w_other, w_side = lax.optimization_barrier((vecs, w_other, w_side))
    up = core == 1
    gbu = gbup.reshape(2, spots, n_t, slab)
    gbu = jnp.where(up, gbu[::-1], gbu).transpose(2, 0, 1, 3).reshape(n_t, units)
    gbu = gbu[jnp.stack([lax.rem(ti - z + n_t, n_t) for z in range(n_t)])]
    pack = jnp.concatenate([vecs.reshape(-1), gbu.reshape(-1)]).reshape(-1, 128)
    pack_came = dp_swap(pack, 1)

    parts = [gctx_rel[0]] + [shift(gctx_rel[s], n_t, -s) for s in range(1, n_t)]

    send = wgrad(slab, spots, gb_s, first_low, act_s, grad_ffn, grad_attn, ctx_parts)
    got = dp_swap(send, 1)
    first_low, send, pack, pack_came = lax.optimization_barrier((first_low, send, pack, pack_came))
    keep = wgrad(slab, spots, gb_k, first_low, act_k, grad_ffn, grad_attn, ctx_parts)
    got, keep, pack, pack_came = lax.optimization_barrier((got, keep, pack, pack_came))
    lead = (2,) * len(low_bits)
    shape = lambda x, n: x.reshape(lead + (n_t, n, width))
    a_keep, a_send, _ = narrow_pair(shape(keep[:, :, :cut], cut), shape(got[:, :, :cut], cut), low_bits)
    b_keep, b_send, _ = narrow_pair(shape(keep[:, :, cut:], slab), shape(got[:, :, cut:], slab), high_bits)
    *parts, a_send, b_send, a_keep, b_keep, out_low, pack, pack_came = lax.optimization_barrier(
        (*parts, a_send, b_send, a_keep, b_keep, out_low, pack, pack_came)
    )
    a_came = dp_swap(a_send, low_bits[0])
    b_came = dp_swap(b_send, high_bits[0])
    pack = pack + pack_came
    packs = [pack] + [dp_swap(pack, 2 * r) for r in range(1, spots)]
    out_all = lax.all_gather(out_low, "tensor", axis=0, tiled=True)

    gqkv, glm = attn_bwd(ti.reshape(1), parts, ctxt, q3, k3, v3, qt, kt, lse, lmt)
    gqkv, glm, a_keep, a_came, b_keep, b_came, *packs = lax.optimization_barrier(
        (gqkv, glm, a_keep, a_came, b_keep, b_came, *packs)
    )
    parts = [rows_of(gqkv, ti * chunk, chunk)] + [
        shift(rows_of(gqkv, lax.rem(ti + s, n_t) * chunk, chunk), n_t, s) for s in range(1, n_t)
    ]
    a_keep, a_send, bit = narrow_pair(a_keep, a_came, low_bits[1:])
    a_came = dp_swap(a_send, bit)
    b_keep, b_send, bit = narrow_pair(b_keep, b_came, high_bits[1:])
    b_came = dp_swap(b_send, bit)
    tail = tail_of(hidden, gqkv, glm, table, noise, 3 * local)
    w_all = jnp.concatenate([jnp.where(up, w_other, w_side), jnp.where(up, w_side, w_other)], axis=1)
    held = lax.optimization_barrier((*parts, w_all, tail, a_keep, a_came, b_keep, b_came, *packs))
    parts, w_all, (tail, a_keep, a_came, b_keep, b_came, *packs) = held[:n_t], held[n_t], held[n_t + 1 :]
    g_a = (a_keep.astype(F32) + a_came.astype(F32)).astype(BF16)
    g_b = (b_keep.astype(F32) + b_came.astype(F32)).astype(BF16)
    g_a = finish(narrow(g_a, low_bits[2:]))
    g_b = finish(narrow(g_b, high_bits[2:]))
    pack = packs[0]
    for p in packs[1:]:
        pack = pack + p
    pack_came = swap(pack, "tensor", n_t, 1)
    total = jnp.concatenate([g_a, g_b], axis=1)
    pieces = [total[0]] + [shift(total[s], n_t, -s) for s in range(1, n_t)]
    tail = tail.reshape(2, spots, -1, tail.shape[1])
    send = lax.dynamic_index_in_dim(tail, 1 - core, 0, keepdims=False)
    keep = lax.dynamic_index_in_dim(tail, core, 0, keepdims=False)
    came = dp_swap(send, 1)
    back = back_of(ti.reshape(1), w_all, grad_resid, parts)
    back, keep, came, pack, pack_came, *pieces = lax.optimization_barrier(
        (back, keep, came, pack, pack_came, *pieces)
    )
    grad_hidden = lax.all_gather(back, "tensor", axis=0, tiled=True)
    summed = pieces[0].astype(F32)
    for p in pieces[1:]:
        summed = summed + p.astype(F32)
    held = quad_gather(summed.astype(BF16))
    tail = (keep.astype(F32) + came.astype(F32)).astype(BF16)
    tail = jnp.concatenate(quad_gather(finish(quad_sum(tail))))
    other = dp_swap(tail, 1)
    tail = jnp.concatenate([jnp.where(up, other, tail), jnp.where(up, tail, other)])
    g_ao = jnp.concatenate([x[slab:cut] for x in held])
    pair = jnp.stack([jnp.concatenate([x[:slab] for x in held]), jnp.concatenate([x[cut:] for x in held])])
    other = dp_swap(pair, 1)
    pair = jnp.concatenate([jnp.where(up, other, pair), jnp.where(up, pair, other)], axis=1)
    pack = pack + pack_came
    for bit in extra:
        pack = pack + dp_swap(pack, bit)
    bit = 2
    while bit < n_t:
        pack = pack + swap(pack, "tensor", n_t, bit)
        bit *= 2
    cols = table.shape[2]
    at = 2 * cols + 3 * local
    extra_cols = tail.shape[1] - at
    g_mask = jnp.stack([tail[:, :cols], tail[:, cols : 2 * cols]])
    g_qkv_w = jnp.stack([tail[:, 2 * cols + n * local : 2 * cols + (n + 1) * local] for n in range(3)])
    g_b_qv = tail[: 3 * local // extra_cols, at:].reshape(3, local)[0::2]
    out_states = out_all.astype(F32)
    g_up = pair[0].T
    g_down = pair[1]

    pack = pack.reshape(-1)
    rows = [pack[n * width : (n + 1) * width] for n in range(8)]
    gbu = lax.dynamic_slice_in_dim(pack, 8 * width + ti * units, units)
    total_valid = rows[7][0]
    loss = jnp.sum(rows[6]) / (total_valid * width)
    coef = 2.0 * tokens / total_valid
    grads = [
        grad_hidden, g_qkv_w.reshape(w_qkv.shape), g_b_qv.reshape(2, local), g_ao, rows[0], rows[1], rows[2],
        g_up, gbu, g_down, rows[3], rows[4], rows[5], g_mask.reshape(table.shape),
    ]
    return (out_states, loss, *[g.astype(F32) * coef for g in grads])


def solution(mesh):
    row, col = P("tensor", None), P(None, "tensor")
    heads = P("tensor", None, None)
    dp = P("dp", None)
    qkv = P(None, None, "tensor")
    sizes = dict(mesh.shape)
    return jax.shard_map(
        functools.partial(body, n_d=sizes["dp"], n_t=sizes["tensor"]),
        mesh=mesh,
        in_specs=(dp, dp, dp, qkv, col, row, P(), P(), P(), col, P("tensor"), row, P(), P(), P(), heads, heads),
        out_specs=(dp, P(), dp, qkv, col, row, P(), P(), P(), col, P("tensor"), row, P(), P(), P(), heads),
        check_vma=False,
    )
```

```python
import functools
import math

import jax
import jax.numpy as jnp
from jax import lax
from jax.experimental import pallas as pl
from jax.experimental.pallas import tpu as pltpu
from jax.sharding import PartitionSpec as P

BLOCK = 256
LOG2E = math.log2(math.e)
SOFTENING = 0.5
EPS = 1e-6
F32 = jnp.float32
BF16 = jnp.bfloat16


def dot(a, b):
    return jnp.dot(a, b, preferred_element_type=F32)


def dot_nt(a, b):
    return lax.dot_general(a, b, (((1,), (1,)), ((), ())), preferred_element_type=F32)


def dot_tn(a, b):
    return lax.dot_general(a, b, (((0,), (0,)), ((), ())), preferred_element_type=F32)


def dot_tt(a, b):
    return lax.dot_general(a, b, (((0,), (1,)), ((), ())), preferred_element_type=F32)


def cost(micros, moved):
    return pl.CostEstimate(flops=int(micros * 1e9), transcendentals=0, bytes_accessed=moved)


def prep_kernel(hid, w, b, bt, table, noise, q3, k3, v3, qt, kt, vt, lmt):
    heads = table.shape[0]
    tokens = hid.shape[0]
    hd = q3.shape[2]
    for h in range(heads):
        x = (table[h] + noise[h]) * (1.0 / SOFTENING)
        ls = jnp.minimum(x, 0.0) - jnp.log1p(jnp.exp(-jnp.abs(x)))
        lmt[h] = jnp.transpose(ls * LOG2E)

    step = 2 * BLOCK

    def project(i, _):
        rows = pl.ds(pl.multiple_of(i * step, step), step)
        x = hid[rows, :]
        for n, (nat, tr) in enumerate(((q3, qt), (k3, kt), (v3, vt))):
            y = dot(x, w[n])
            yt = dot_tt(w[n], x)
            if n != 1:
                y = y + b[n // 2 : n // 2 + 1, :]
                yt = yt + bt[:, n // 2 : n // 2 + 1]
            y = y.astype(BF16)
            for h in range(heads):
                nat[h, rows, :] = y[:, h * hd : (h + 1) * hd]
            tr[:, rows] = yt.astype(BF16)
        return 0

    lax.fori_loop(0, tokens // step, project, 0)


def attn_prep(hidden, w_qkv, b_qv, table, noise):
    tokens = hidden.shape[0]
    heads = table.shape[0]
    width = w_qkv.shape[2]
    sd = jax.ShapeDtypeStruct
    nat = sd((heads, tokens, width // heads), BF16)
    tr = sd((width, tokens), BF16)
    return pl.pallas_call(
        prep_kernel,
        out_shape=(nat, nat, nat, tr, tr, tr, sd(table.shape, F32)),
        compiler_params=pltpu.CompilerParams(vmem_limit_bytes=56 << 20),
        cost_estimate=cost(15, 20 << 20),
        name="attn_prep",
    )(hidden, w_qkv, b_qv, b_qv.T, table, noise)


def attn_fwd_kernel(lo, n_prev, qt, k3, vt, lmt, *refs):
    ctx, ctxt, lse = refs[n_prev:]
    heads, tokens, hd = k3.shape
    period = lmt.shape[1]
    width = heads * hd
    coef = LOG2E / math.sqrt(hd)
    parts = period // BLOCK
    lse[...] = jnp.zeros(lse.shape, F32)
    first = (pl.program_id(0) + lo) * parts

    def per_q(j, _):
        qb = first + j
        qcol = pl.ds(pl.multiple_of(qb * BLOCK, BLOCK), BLOCK)
        ocol = pl.ds(pl.multiple_of(j * BLOCK, BLOCK), BLOCK)
        mcol = ocol

        def per_k(kb, carry):
            krow = pl.ds(pl.multiple_of(kb * BLOCK, BLOCK), BLOCK)
            mrow = pl.ds(pl.multiple_of(lax.rem(kb, parts) * BLOCK, BLOCK), BLOCK)
            out = []
            ss = [dot(k3[h, krow, :], qt[h * hd : (h + 1) * hd, qcol]) for h in range(heads)]
            for h in range(heads):
                m, l, acc = carry[h]
                s = ss[h] * coef + lmt[h, mrow, mcol]
                mn = jnp.maximum(m, jnp.max(s, axis=0, keepdims=True))
                al = jnp.exp2(m - mn)
                p = jnp.exp2(s - mn)
                l = l * al + jnp.sum(p, axis=0, keepdims=True)
                acc = acc * al + dot(vt[h * hd : (h + 1) * hd, krow], p.astype(BF16))
                out.append((mn, l, acc))
            return tuple(out)

        init = tuple(
            (
                jnp.full((1, BLOCK), -1e30, F32),
                jnp.zeros((1, BLOCK), F32),
                jnp.zeros((hd, BLOCK), F32),
            )
            for _ in range(heads)
        )
        res = lax.fori_loop(0, qb + 1, per_k, init)
        cols = []
        for h in range(heads):
            m, l, acc = res[h]
            c = acc / l
            ctxt[h * hd : (h + 1) * hd, ocol] = c
            lse[h : h + 1, ocol] = m + jnp.log2(l)
            cols.append(c)
        pad = -width % 128
        if pad:
            cols.append(jnp.zeros((pad, BLOCK), F32))
        full = jnp.transpose(jnp.concatenate(cols, axis=0))
        ctx[ocol, :] = full[:, :width].astype(BF16)
        return 0

    lax.fori_loop(0, parts, per_q, 0)


def attn_fwd(qt, k3, vt, lmt, lo, hi, prev=()):
    heads, tokens, hd = k3.shape
    width = heads * hd
    period = lmt.shape[1]
    sd = jax.ShapeDtypeStruct
    whole = lambda x: pl.BlockSpec(x.shape, lambda i, n=len(x.shape): (0,) * n)
    return pl.pallas_call(
        functools.partial(attn_fwd_kernel, lo, len(prev)),
        grid=(hi - lo,),
        in_specs=[whole(x) for x in (qt, k3, vt, lmt)] + [pl.BlockSpec(memory_space=pl.ANY)] * len(prev),
        out_specs=(
            pl.BlockSpec((period, width), lambda i: (i + lo, 0)),
            pl.BlockSpec((width, period), lambda i: (0, i + lo)),
            pl.BlockSpec((8, period), lambda i: (0, i + lo)),
        ),
        out_shape=(sd((tokens, width), BF16), sd((width, tokens), F32), sd((8, tokens), F32)),
        input_output_aliases={4 + n: n for n in range(len(prev))},
        compiler_params=pltpu.CompilerParams(vmem_limit_bytes=56 << 20),
        cost_estimate=cost(1.5 * (hi * hi - lo * lo) / 2, 8 << 20),
        name="attn_fwd",
    )(qt, k3, vt, lmt, *prev)


def attn_bwd_kernel(n_t, place, *refs):
    pieces = refs[:n_t]
    (ctxt, q3, k3, v3, qt, kt, lse, lmt, gqkv, glm, gk, gv, g3, glmt, gctx, sems) = refs[n_t:]
    heads, tokens, hd = q3.shape
    chunk = tokens // n_t
    copies = []
    for s in range(n_t):
        at = lax.rem(place[0] + s, n_t) * chunk
        to = gctx.at[pl.ds(pl.multiple_of(at, chunk), chunk), :]
        copies.append(pltpu.make_async_copy(pieces[s], to, sems.at[s]))
    for cp in copies:
        cp.start()
    period = lmt.shape[1]
    width = heads * hd
    coef = LOG2E / math.sqrt(hd)
    scale = 1.0 / math.sqrt(hd)
    parts = period // BLOCK
    pad = -width % 128
    gk[...] = jnp.zeros(gk.shape, F32)
    gv[...] = jnp.zeros(gv.shape, F32)
    glmt[...] = jnp.zeros(glmt.shape, F32)
    for cp in copies:
        cp.wait()

    def per_q(i, _):
        qb = tokens // BLOCK - 1 - i
        qcol = pl.ds(pl.multiple_of(qb * BLOCK, BLOCK), BLOCK)
        mcol = pl.ds(pl.multiple_of(lax.rem(qb, parts) * BLOCK, BLOCK), BLOCK)
        g = gctx[qcol, :].astype(F32)
        gpad = jnp.concatenate([g, jnp.zeros((BLOCK, pad), F32)], axis=1) if pad else g
        gt = jnp.transpose(gpad)
        delta, gtb = [], []
        for h in range(heads):
            gth = gt[h * hd : (h + 1) * hd, :]
            delta.append(jnp.sum(gth * ctxt[h * hd : (h + 1) * hd, qcol], axis=0, keepdims=True))
            gtb.append(gth.astype(BF16))
            g3[h] = gctx[qcol, h * hd : (h + 1) * hd]

        def per_k(kb, carry):
            krow = pl.ds(pl.multiple_of(kb * BLOCK, BLOCK), BLOCK)
            mrow = pl.ds(pl.multiple_of(lax.rem(kb, parts) * BLOCK, BLOCK), BLOCK)
            out = []
            for h in range(heads):
                hs = slice(h * hd, (h + 1) * hd)
                s = dot(k3[h, krow, :], qt[hs, qcol]) * coef + lmt[h, mrow, mcol]
                p = jnp.exp2(s - lse[h : h + 1, qcol])
                dp = dot(v3[h, krow, :], gtb[h])
                ds = p * (dp - delta[h])
                dsb = ds.astype(BF16)
                glmt[h, mrow, mcol] += ds
                gv[h, krow, :] += dot(p.astype(BF16), g3[h])
                gk[h, krow, :] += dot(dsb, q3[h, qcol, :])
                out.append(carry[h] + dot(kt[hs, krow], dsb))
            return tuple(out)

        init = tuple(jnp.zeros((hd, BLOCK), F32) for _ in range(heads))
        res = lax.fori_loop(0, qb + 1, per_k, init)
        rows = [r * scale for r in res]
        if pad:
            rows.append(jnp.zeros((pad, BLOCK), F32))
        gq = jnp.transpose(jnp.concatenate(rows, axis=0))[:, :width]
        gkb = jnp.concatenate([gk[h, qcol, :] for h in range(heads)], axis=1) * scale
        gvb = jnp.concatenate([gv[h, qcol, :] for h in range(heads)], axis=1)
        rows = [gq, gkb, gvb]
        if gqkv.shape[1] > 3 * width:
            rows.append(jnp.zeros((BLOCK, gqkv.shape[1] - 3 * width), F32))
        gqkv[qcol, :] = jnp.concatenate(rows, axis=1).astype(BF16)
        return 0

    lax.fori_loop(0, tokens // BLOCK, per_q, 0)
    for h in range(heads):
        glm[h] = jnp.transpose(glmt[h])


def attn_bwd(place, parts, ctxt, q3, k3, v3, qt, kt, lse, lmt):
    heads, tokens, hd = q3.shape
    width = heads * hd
    n_t = len(parts)
    sd = jax.ShapeDtypeStruct
    vm = pl.BlockSpec(memory_space=pltpu.VMEM)
    return pl.pallas_call(
        functools.partial(attn_bwd_kernel, n_t),
        in_specs=[pl.BlockSpec(memory_space=pltpu.SMEM)] + [pl.BlockSpec(memory_space=pl.ANY)] * n_t + [vm] * 8,
        out_shape=(sd((tokens, -(-3 * width // 128) * 128), BF16), sd(lmt.shape, F32)),
        scratch_shapes=[
            pltpu.VMEM((heads, tokens, hd), F32),
            pltpu.VMEM((heads, tokens, hd), F32),
            pltpu.VMEM((heads, BLOCK, hd), BF16),
            pltpu.VMEM(lmt.shape, F32),
            pltpu.VMEM((tokens, width), BF16),
            pltpu.SemaphoreType.DMA((n_t,)),
        ],
        compiler_params=pltpu.CompilerParams(vmem_limit_bytes=56 << 20),
        cost_estimate=cost(400, 20 << 20),
        name="attn_bwd",
    )(place, *parts, ctxt, q3, k3, v3, qt, kt, lse, lmt)


def wgrad_kernel(slab, spots, gb, first, act, grad_ffn, grad_attn, *refs):
    ctx, (send, keep, ao) = refs[:-3], refs[-3:]
    i = pl.program_id(0)
    n_t = len(ctx)
    piece = send.shape[2] - 2 * slab

    @pl.when(i == 0)
    def _():
        for z in range(n_t):
            ao[z] = dot_tn(ctx[z][...], grad_attn[...]).astype(BF16)

    def write(to):
        up = dot_tn(gb[...], first[...]).astype(BF16)
        down = dot_tn(act[...], grad_ffn[...]).astype(BF16)
        rows = pl.ds(pl.multiple_of(lax.rem(i, spots) * piece, piece), piece)
        for z in range(n_t):
            to[0, z, :slab, :] = up[z * slab : (z + 1) * slab]
            to[0, z, slab : slab + piece, :] = ao[z, rows, :]
            to[0, z, slab + piece :, :] = down[z * slab : (z + 1) * slab]

    @pl.when(i < spots)
    def _():
        write(send)

    @pl.when(i >= spots)
    def _():
        write(keep)


def wgrad(slab, spots, gb, first, act, grad_ffn, grad_attn, ctx):
    chunk, width = first.shape
    n_t = len(ctx)
    local = ctx[0].shape[1]
    wide = n_t * slab
    tall = 2 * slab + local // spots
    sd = jax.ShapeDtypeStruct
    vm = pl.BlockSpec(memory_space=pltpu.VMEM)
    cols = pl.BlockSpec((chunk, wide), lambda i: (0, jax.lax.rem(i + spots, 2 * spots)))
    send = lambda i: jnp.minimum(i, spots - 1)
    keep = lambda i: jnp.maximum(i - spots, 0)
    outs = [pl.BlockSpec((1, n_t, tall, width), lambda i, at=at: (at(i), 0, 0, 0)) for at in (send, keep)]
    shape = sd((spots, n_t, tall, width), BF16)
    return pl.pallas_call(
        functools.partial(wgrad_kernel, slab, spots),
        grid=(2 * spots,),
        in_specs=[cols, vm, cols, vm, vm] + [vm] * n_t,
        out_specs=tuple(outs),
        out_shape=(shape, shape),
        scratch_shapes=[pltpu.VMEM((n_t, local, width), BF16)],
        compiler_params=pltpu.CompilerParams(vmem_limit_bytes=40 << 20),
        cost_estimate=cost(400, 10 << 20),
        name="wgrad",
    )(gb, first, act, grad_ffn, grad_attn, *ctx)


def tail_kernel(hid, gqkv, glm, table, noise, tail, acc):
    heads, period, _ = glm.shape
    tokens, width = hid.shape
    wide = acc.shape[1]
    tall, lanes = tail.shape
    at = 2 * period + wide
    extra = lanes - at
    step = 2 * BLOCK
    for n in range(heads * period // BLOCK):
        h, at = n * BLOCK // period, n * BLOCK % period
        x = (table[h, at : at + BLOCK, :] + noise[h, at : at + BLOCK, :]) * (1.0 / SOFTENING)
        e = jnp.exp(-jnp.abs(x))
        slope = jnp.where(x > 0, e, 1.0) / (1.0 + e) * (1.0 / SOFTENING)
        g = (glm[h, at : at + BLOCK, :] * slope).astype(BF16)
        row, col = n * BLOCK % tall, n * BLOCK // tall * period
        tail[row : row + BLOCK, col : col + period] = g
    acc[...] = jnp.zeros(acc.shape, F32)

    def add(i, total):
        rows = pl.ds(pl.multiple_of(i * step, step), step)
        y = gqkv[rows, :wide]
        acc[...] += dot_tn(hid[rows, :], y)
        return total + jnp.sum(y.astype(F32), axis=0, keepdims=True)

    total = lax.fori_loop(0, tokens // step, add, jnp.zeros((1, wide), F32))
    rows = [total[:, n * extra : (n + 1) * extra] for n in range(wide // extra)]
    rows.append(jnp.zeros((tall - len(rows), extra), F32))
    tail[:, 2 * period :] = jnp.concatenate([acc[...], jnp.concatenate(rows, axis=0)], axis=1).astype(BF16)


def tail_of(hidden, gqkv, glm, table, noise, wide):
    heads, period, _ = glm.shape
    width = hidden.shape[1]
    lanes = 2 * period + wide
    sd = jax.ShapeDtypeStruct
    return pl.pallas_call(
        tail_kernel,
        out_shape=sd((heads * period // 2, -(-lanes // 128) * 128), BF16),
        scratch_shapes=[pltpu.VMEM((width, wide), F32)],
        compiler_params=pltpu.CompilerParams(vmem_limit_bytes=56 << 20),
        cost_estimate=cost(400, 20 << 20),
        name="tail",
    )(hidden, gqkv, glm, table, noise)


def back_kernel(place, w, resid, *refs):
    pieces, out = refs[:-1], refs[-1]
    n_t, wide, _ = w.shape
    total = resid[...]
    for s in range(n_t):
        total = total + dot(pieces[s][:, :wide], w[lax.rem(place[0] + n_t - s, n_t)])
    out[...] = total.astype(BF16)


def back_of(place, w, resid, pieces):
    vm = pl.BlockSpec(memory_space=pltpu.VMEM)
    return pl.pallas_call(
        back_kernel,
        in_specs=[pl.BlockSpec(memory_space=pltpu.SMEM)] + [vm] * (2 + len(pieces)),
        out_shape=jax.ShapeDtypeStruct(resid.shape, BF16),
        compiler_params=pltpu.CompilerParams(vmem_limit_bytes=40 << 20),
        cost_estimate=cost(5, 10 << 20),
        name="back",
    )(place, w, resid, *pieces)


def norm_parts(resid):
    centred = resid - jnp.mean(resid, axis=-1, keepdims=True)
    rstd = lax.rsqrt(jnp.mean(centred * centred, axis=-1, keepdims=True) + EPS)
    return centred * rstd, rstd


def norm_back(grad, xhat, rstd, gain):
    gy = grad * gain
    return rstd * (
        gy
        - jnp.mean(gy, axis=-1, keepdims=True)
        - xhat * jnp.mean(gy * xhat, axis=-1, keepdims=True)
    )


def ffn_kernel(
    n_t, slab, core, *refs
):
    ctx = refs[:n_t]
    (wao, hid, teach, valid, vec, bup, up_o, up_m, up_t, dn_o, dn_m, dn_t,
     out, out_low, act, gb, first_low, grad_ffn, grad_attn, grad_resid, vecs, gbup) = refs[n_t : n_t + 22]
    gctx = refs[n_t + 22 : 2 * n_t + 22]
    up_s, dn_s, slope, xhat_s, sems = refs[2 * n_t + 22 :]
    units, width = up_s.shape
    half = units // 2
    spots = half // (n_t * slab)
    c = core[0]
    copies = []
    for n, (o, m, t, dst) in enumerate(((up_o, up_m, up_t, up_s), (dn_o, dn_m, dn_t, dn_s))):
        for side, f in enumerate((m, t)):
            base = (c if side == 0 else 1 - c) * (spots * slab)
            for p in range(spots):
                to = side * half + p * n_t * slab
                copies.append((n, o.at[pl.ds(pl.multiple_of(base + p * slab, slab), slab)], dst.at[pl.ds(to, slab)]))
                rest = (n_t - 1) * slab
                copies.append((n, f.at[pl.ds(p * rest, rest)], dst.at[pl.ds(to + slab, rest)]))
    copies = [pltpu.make_async_copy(a, b, sems.at[i]) for i, (n, a, b) in enumerate(copies)]
    for cp in copies:
        cp.start()
    b_ao, g1, b1, b_dn, g2, b2 = (vec[n : n + 1, :] for n in range(6))
    attention = sum(dot(ctx[s][...], wao[s]) for s in range(n_t)) + b_ao
    xhat1, rstd1 = norm_parts(hid[...].astype(F32) + attention)
    first = xhat1 * g1 + b1
    first_low[...] = first.astype(BF16)
    xhat_s[...] = xhat1
    for cp in copies:
        cp.wait()
    blocks, _, size = bup.shape

    def forward(i, feed):
        rows = pl.ds(pl.multiple_of(i * size, size), size)
        before = dot_nt(first_low[...], up_s[rows, :]) + bup[i]
        phi = 0.5 * (1.0 + lax.erf(before * math.sqrt(0.5)))
        dens = jnp.exp(-0.5 * before * before) * (1.0 / math.sqrt(2.0 * math.pi))
        low = (before * phi).astype(BF16)
        act[:, rows] = low
        slope[:, rows] = (phi + before * dens).astype(BF16)
        return feed + dot(low, dn_s[rows, :])

    feed = lax.fori_loop(0, blocks, forward, jnp.zeros(out.shape, F32))
    xhat2, rstd2 = norm_parts(first + feed + b_dn)
    own = xhat2 * g2 + b2
    out[...] = own
    out_low[...] = own.astype(BF16)
    residue = own - teach[...]
    weighed = valid[...] * residue
    grad_out = weighed
    total = lambda x: jnp.sum(x, axis=0, keepdims=True)
    vecs[4:5, :] = total(grad_out * xhat2)
    vecs[5:6, :] = total(grad_out)
    vecs[6:7, :] = total(weighed * residue)
    vecs[7:8, :] = jnp.broadcast_to(jnp.sum(valid[...], axis=0, keepdims=True), (1, width))
    grad_second = norm_back(grad_out, xhat2, rstd2, g2)
    grad_resid[...] = grad_second
    low = grad_second.astype(BF16)
    grad_ffn[...] = low
    vecs[3:4, :] = total(low.astype(F32))

    def backward(i, acc):
        rows = pl.ds(pl.multiple_of(i * size, size), size)
        g = dot_nt(grad_ffn[...], dn_s[rows, :]) * slope[:, rows].astype(F32)
        low = g.astype(BF16)
        gb[:, rows] = low
        gbup[i] = total(low.astype(F32))
        return acc + dot(low, up_s[rows, :])

    grad_first = lax.fori_loop(0, blocks, backward, jnp.zeros(out.shape, F32)) + grad_resid[...]
    xhat1 = xhat_s[...]
    vecs[1:2, :] = total(grad_first * xhat1)
    vecs[2:3, :] = total(grad_first)
    back = norm_back(grad_first, xhat1, rstd1, g1)
    grad_resid[...] = back
    low = back.astype(BF16)
    grad_attn[...] = low
    vecs[0:1, :] = total(low.astype(F32))
    local = ctx[0].shape[1]
    for s in range(n_t):
        gctx[s][...] = dot_nt(low, wao[s]).astype(BF16)


def ffn(core, ctx, wao, hid, teach, valid, vec, bup, ups, downs, slab):
    n_t = len(ctx)
    chunk, width = hid.shape
    local = ctx[0].shape[1]
    blocks, _, size = bup.shape
    units = blocks * size
    spots = units // (2 * n_t * slab)
    sd = jax.ShapeDtypeStruct
    vm = pl.BlockSpec(memory_space=pltpu.VMEM)
    sm = pl.BlockSpec(memory_space=pltpu.SMEM)
    hbm = pl.BlockSpec(memory_space=pl.ANY)
    return pl.pallas_call(
        functools.partial(ffn_kernel, n_t, slab),
        in_specs=[sm] + [vm] * (n_t + 6) + [hbm] * 6,
        out_shape=(
            sd((chunk, width), F32),
            sd((chunk, width), BF16),
            sd((chunk, units), BF16),
            sd((chunk, units), BF16),
            sd((chunk, width), BF16),
            sd((chunk, width), BF16),
            sd((chunk, width), BF16),
            sd((chunk, width), F32),
            sd((8, width), F32),
            sd((blocks, 1, size), F32),
            *[sd((chunk, local), BF16)] * n_t,
        ),
        scratch_shapes=[
            pltpu.VMEM((units, width), BF16),
            pltpu.VMEM((units, width), BF16),
            pltpu.VMEM((chunk, units), BF16),
            pltpu.VMEM((chunk, width), F32),
            pltpu.SemaphoreType.DMA((8 * spots,)),
        ],
        compiler_params=pltpu.CompilerParams(vmem_limit_bytes=56 << 20),
        cost_estimate=cost(34, 25 << 20),
        name="ffn",
    )(core, *ctx, wao, hid, teach, valid, vec, bup, *ups, *downs)


def shift(x, size, amount):
    return lax.ppermute(x, "tensor", [(j, (j + amount) % size) for j in range(size)])


def swap(x, axis, size, bit):
    return lax.ppermute(x, axis, [(j, j ^ bit) for j in range(size)])


def rows_of(x, start, count):
    return lax.dynamic_slice_in_dim(x, start, count, axis=0)


def body(
    hidden, teacher, valid, w_qkv, b_qv, w_attn_out, b_attn_out, gain_one, bias_one,
    w_up, b_up, w_down, b_down, gain_two, bias_two, table, noise, *, n_d, n_t,
):
    tokens, width = hidden.shape
    units = w_up.shape[1]
    local = w_qkv.shape[2]
    chunk = tokens // n_t
    ti = lax.axis_index("tensor")
    di = lax.axis_index("dp")
    group = min(n_d, 8)
    low_bits = [b for b in (2, 4) if b < group]
    high_bits = low_bits[::-1]
    extra = [b for b in (8, 16, 32, 64, 128, 256, 512) if b < n_d]
    spots = group // 2
    slab = units // group
    piece = local // spots
    core = di % 2
    spot = (di // 2) % spots

    def bit_of(bit):
        return (di // bit) % 2

    def dp_swap(x, bit):
        return swap(x, "dp", n_d, bit)

    def everyone(x):
        bit = 1
        while bit < n_d:
            x = x + dp_swap(x, bit)
            bit *= 2
        return x

    def spread(x, bits, other=None):
        done = []
        for bit in bits:
            if done or other is None:
                other = dp_swap(x, bit)
            up = bit_of(bit) == 1
            pos = sum(1 for b in done if b > bit)
            x = jnp.stack([jnp.where(up, other, x), jnp.where(up, x, other)], axis=pos)
            done.append(bit)
        return x.reshape((-1,) + x.shape[len(done) :])

    def narrow_start(x, bits):
        ax = sorted(bits, reverse=True).index(bits[0])
        up = bit_of(bits[0])
        send = lax.dynamic_index_in_dim(x, 1 - up, ax, keepdims=False)
        keep = lax.dynamic_index_in_dim(x, up, ax, keepdims=False)
        return keep, dp_swap(send, bits[0])

    def narrow_pair(x, y, bits, lo=0, count=None):
        ax = sorted(bits, reverse=True).index(bits[0])
        up = bit_of(bits[0])
        sizes = list(x.shape)
        sizes[ax] = 1
        sizes[-2] = count or sizes[-2]

        def half(i):
            at = [0] * x.ndim
            at[ax] = i
            at[-2] = lo
            part = lambda v: lax.dynamic_slice(v, at, sizes).astype(F32)
            return (part(x) + part(y)).astype(BF16).reshape(sizes[:ax] + sizes[ax + 1 :])

        return half(up), half(1 - up), bits[0]

    def narrow(x, bits):
        left = sorted(bits, reverse=True)
        for bit in bits:
            ax = left.index(bit)
            left.remove(bit)
            up = bit_of(bit)
            send = lax.dynamic_index_in_dim(x, 1 - up, ax, keepdims=False)
            keep = lax.dynamic_index_in_dim(x, up, ax, keepdims=False)
            x = (keep.astype(F32) + dp_swap(send, bit).astype(F32)).astype(BF16)
        return x

    def quad_parts(x):
        return [lax.dynamic_index_in_dim(x, spot ^ r, 0, keepdims=False) for r in range(spots)]

    def quad_sum(x):
        pieces = quad_parts(x)
        total = pieces[0].astype(F32)
        for r in range(1, spots):
            total = total + dp_swap(pieces[r], 2 * r).astype(F32)
        return total.astype(BF16)

    def quad_gather(x):
        held = [x] + [dp_swap(x, 2 * r) for r in range(1, spots)]
        step = 1
        while step < spots:
            flip = bit_of(2 * step) == 1
            held = [jnp.where(flip, held[r ^ step], held[r]) for r in range(spots)]
            step *= 2
        return held

    def finish(x):
        for bit in extra:
            x = (x.astype(F32) + dp_swap(x, bit).astype(F32)).astype(BF16)
        return x

    valid_f = valid[0].astype(F32)

    up_own = w_up.T
    b_hi = b_up.astype(BF16)
    b_lo = (b_up - b_hi.astype(F32)).astype(BF16)
    start = core * (spots * slab) + spot * slab
    sent = jnp.concatenate(
        [
            rows_of(up_own, start, slab),
            rows_of(w_attn_out, spot * piece, piece),
            rows_of(w_down, start, slab),
            b_hi[None],
            b_lo[None],
            jnp.zeros((14, width), BF16),
        ]
    )
    came = [shift(sent, n_t, s) for s in range(1, n_t)]

    w_t = w_qkv.transpose(0, 2, 1).reshape(3 * local, width)
    w_t = rows_of(w_t, core * (3 * local // 2), 3 * local // 2)
    q3, k3, v3, qt, kt, vt, lmt = attn_prep(hidden, w_qkv, b_qv, table, noise)
    n_sup = tokens // lmt.shape[1]
    cuts = [max(n_sup - 2, 1), max(n_sup - 1, 2)]
    part = attn_fwd(qt, k3, vt, lmt, 0, cuts[0])
    part, came, w_t = lax.optimization_barrier((part, came, w_t))
    w_side = lax.all_gather(w_t, "tensor", axis=0)

    cut = slab + piece
    wide_a = jnp.stack([x[:cut] for x in came])
    wide_b = jnp.stack([x[cut : cut + slab] for x in came])
    first_a = dp_swap(wide_a, low_bits[0])
    first_b = dp_swap(wide_b, high_bits[0])
    part = attn_fwd(qt, k3, vt, lmt, cuts[0], cuts[1], part)
    part, first_a, first_b = lax.optimization_barrier((part, first_a, first_b))
    ctx, ctxt, lse = attn_fwd(qt, k3, vt, lmt, cuts[1], n_sup, part)
    wide_a = spread(wide_a, low_bits, first_a)
    wide_b = spread(wide_b, high_bits, first_b)
    ctx_parts = [rows_of(ctx, ti * chunk, chunk)] + [
        shift(rows_of(ctx, lax.rem(ti + s, n_t) * chunk, chunk), n_t, s) for s in range(1, n_t)
    ]
    *ctx_parts, wide_a, wide_b, w_side = lax.optimization_barrier((*ctx_parts, wide_a, wide_b, w_side))
    up_m = wide_a[:, :, :slab].reshape(-1, width)
    down_m = wide_b.reshape(-1, width)
    wao = wide_a[:, :, slab:].transpose(1, 0, 2, 3).reshape(n_t - 1, local, width)
    wao = jnp.concatenate([w_attn_out[None], wao])
    up_t = dp_swap(up_m, 1)
    down_t = dp_swap(down_m, 1)
    b_all = jnp.stack(
        [b_up]
        + [x[cut + slab].astype(F32) + x[cut + slab + 1].astype(F32) for x in came]
    ).reshape(n_t, 2, spots, slab)
    b_mine = lax.dynamic_index_in_dim(b_all, core, 1, keepdims=False)
    b_theirs = lax.dynamic_index_in_dim(b_all, 1 - core, 1, keepdims=False)
    bup = jnp.stack([b_mine, b_theirs]).transpose(0, 2, 1, 3).reshape(2 * spots, 1, n_t * slab)

    w_other = dp_swap(w_side, 1)
    vec = jnp.stack([b_attn_out, gain_one, bias_one, b_down, gain_two, bias_two, b_down, b_down])
    (out_own, out_low, act, gb, first_low, grad_ffn, grad_attn, grad_resid, vecs, gbup, *gctx_rel) = ffn(
        core.reshape(1),
        ctx_parts,
        wao,
        rows_of(hidden, ti * chunk, chunk),
        rows_of(teacher, ti * chunk, chunk),
        lax.dynamic_slice_in_dim(valid_f, ti * chunk, chunk)[:, None],
        vec,
        bup,
        (up_own, up_m, up_t),
        (w_down, down_m, down_t),
        slab,
    )

    vecs, w_other, w_side = lax.optimization_barrier((vecs, w_other, w_side))
    up = core == 1
    gbu = gbup.reshape(2, spots, n_t, slab)
    gbu = jnp.where(up, gbu[::-1], gbu).transpose(2, 0, 1, 3).reshape(n_t, units)
    gbu = gbu[jnp.stack([lax.rem(ti - z + n_t, n_t) for z in range(n_t)])]
    pack = jnp.concatenate([vecs.reshape(-1), gbu.reshape(-1)]).reshape(-1, 128)

    parts = [gctx_rel[0]] + [shift(gctx_rel[s], n_t, -s) for s in range(1, n_t)]

    lead = (2,) * len(low_bits)
    send, keep = wgrad(slab, spots, gb, first_low, act, grad_ffn, grad_attn, ctx_parts)
    *parts, send, keep, out_low, pack = lax.optimization_barrier((*parts, send, keep, out_low, pack))
    pack_came = dp_swap(pack, 1)
    got = dp_swap(send, 1)
    out_all = lax.all_gather(out_low, "tensor", axis=0, tiled=True)

    gqkv, glm = attn_bwd(ti.reshape(1), parts, ctxt, q3, k3, v3, qt, kt, lse, lmt)
    gqkv, glm, keep, got, pack, pack_came = lax.optimization_barrier((gqkv, glm, keep, got, pack, pack_came))
    pack = pack + pack_came
    pack_came = dp_swap(pack, low_bits[0])
    parts = [rows_of(gqkv, ti * chunk, chunk)] + [
        shift(rows_of(gqkv, lax.rem(ti + s, n_t) * chunk, chunk), n_t, s) for s in range(1, n_t)
    ]
    keep = keep.reshape(lead + keep.shape[1:])
    got = got.reshape(lead + got.shape[1:])
    a_keep, a_send, bit = narrow_pair(keep, got, low_bits, 0, cut)
    a_came = dp_swap(a_send, bit)
    b_keep, b_send, bit = narrow_pair(keep, got, high_bits, cut, slab)
    b_came = dp_swap(b_send, bit)
    tail = tail_of(hidden, gqkv, glm, table, noise, 3 * local)
    w_all = jnp.concatenate([jnp.where(up, w_other, w_side), jnp.where(up, w_side, w_other)], axis=1)
    near = [s for s in range(n_t) if s in (0, 1, n_t - 1)]
    far = [s for s in range(n_t) if s not in near]
    held = lax.optimization_barrier(
        (w_all, tail, a_keep, a_came, b_keep, b_came, pack, pack_came, *[parts[s] for s in near])
    )
    w_all, tail, a_keep, a_came, b_keep, b_came, pack, pack_came = held[:8]
    for n, s in enumerate(near):
        parts[s] = held[8 + n]
    pack = pack + pack_came
    pack_came = dp_swap(pack, low_bits[1])
    a_keep, a_send, bit = narrow_pair(a_keep, a_came, low_bits[1:])
    a_came = dp_swap(a_send, bit)
    b_keep, b_send, bit = narrow_pair(b_keep, b_came, high_bits[1:])
    b_came = dp_swap(b_send, bit)
    tail = tail.reshape((2,) + lead + (-1, tail.shape[1]))
    send = lax.dynamic_index_in_dim(tail, 1 - core, 0, keepdims=False)
    t_keep = lax.dynamic_index_in_dim(tail, core, 0, keepdims=False)
    t_keep, t_send, bit = narrow_pair(t_keep, dp_swap(send, 1), low_bits)
    t_came = dp_swap(t_send, bit)
    held = lax.optimization_barrier(
        (a_keep, a_came, b_keep, b_came, pack, pack_came, *[parts[s] for s in far])
    )
    a_keep, a_came, b_keep, b_came, pack, pack_came = held[:6]
    for n, s in enumerate(far):
        parts[s] = held[6 + n]
    g_a = (a_keep.astype(F32) + a_came.astype(F32)).astype(BF16)
    g_b = (b_keep.astype(F32) + b_came.astype(F32)).astype(BF16)
    g_a = finish(narrow(g_a, low_bits[2:]))
    g_b = finish(narrow(g_b, high_bits[2:]))
    pack = pack + pack_came
    pack_came = swap(pack, "tensor", n_t, 1)
    total = jnp.concatenate([g_a, g_b], axis=1)
    pieces = [total[0]] + [shift(total[s], n_t, -s) for s in range(1, n_t)]
    back = back_of(ti.reshape(1), w_all, grad_resid, parts)
    tail = finish(narrow((t_keep.astype(F32) + t_came.astype(F32)).astype(BF16), low_bits[1:]))
    back, tail, pack, pack_came, *pieces = lax.optimization_barrier((back, tail, pack, pack_came, *pieces))
    grad_hidden = lax.all_gather(back, "tensor", axis=0, tiled=True)
    summed = pieces[0].astype(F32)
    for p in pieces[1:]:
        summed = summed + p.astype(F32)
    held = quad_gather(summed.astype(BF16))
    tail = jnp.concatenate(quad_gather(tail))
    other = dp_swap(tail, 1)
    tail = jnp.concatenate([jnp.where(up, other, tail), jnp.where(up, tail, other)])
    g_ao = jnp.concatenate([x[slab:cut] for x in held])
    pair = jnp.stack([jnp.concatenate([x[:slab] for x in held]), jnp.concatenate([x[cut:] for x in held])])
    other = dp_swap(pair, 1)
    pair = jnp.concatenate([jnp.where(up, other, pair), jnp.where(up, pair, other)], axis=1)
    pack = pack + pack_came
    for bit in low_bits[2:] + extra:
        pack = pack + dp_swap(pack, bit)
    bit = 2
    while bit < n_t:
        pack = pack + swap(pack, "tensor", n_t, bit)
        bit *= 2
    cols = table.shape[2]
    at = 2 * cols + 3 * local
    extra_cols = tail.shape[1] - at
    g_mask = jnp.stack([tail[:, :cols], tail[:, cols : 2 * cols]])
    g_qkv_w = jnp.stack([tail[:, 2 * cols + n * local : 2 * cols + (n + 1) * local] for n in range(3)])
    g_b_qv = tail[: 3 * local // extra_cols, at:].reshape(3, local)[0::2]
    out_states = out_all.astype(F32)
    g_up = pair[0].T
    g_down = pair[1]

    pack = pack.reshape(-1)
    rows = [pack[n * width : (n + 1) * width] for n in range(8)]
    gbu = lax.dynamic_slice_in_dim(pack, 8 * width + ti * units, units)
    total_valid = rows[7][0]
    loss = jnp.sum(rows[6]) / (total_valid * width)
    coef = 2.0 * tokens / total_valid
    grads = [
        grad_hidden, g_qkv_w.reshape(w_qkv.shape), g_b_qv.reshape(2, local), g_ao, rows[0], rows[1], rows[2],
        g_up, gbu, g_down, rows[3], rows[4], rows[5], g_mask.reshape(table.shape),
    ]
    return (out_states, loss, *[g.astype(F32) * coef for g in grads])


def solution(mesh):
    row, col = P("tensor", None), P(None, "tensor")
    heads = P("tensor", None, None)
    dp = P("dp", None)
    qkv = P(None, None, "tensor")
    sizes = dict(mesh.shape)
    return jax.shard_map(
        functools.partial(body, n_d=sizes["dp"], n_t=sizes["tensor"]),
        mesh=mesh,
        in_specs=(dp, dp, dp, qkv, col, row, P(), P(), P(), col, P("tensor"), row, P(), P(), P(), heads, heads),
        out_specs=(dp, P(), dp, qkv, col, row, P(), P(), P(), col, P("tensor"), row, P(), P(), P(), heads),
        check_vma=False,
    )
```

```python
import functools
import math

import jax
import jax.numpy as jnp
from jax import lax
from jax.experimental import pallas as pl
from jax.experimental.pallas import tpu as pltpu
from jax.sharding import PartitionSpec as P

BLOCK = 256
LOG2E = math.log2(math.e)
SOFTENING = 0.5
EPS = 1e-6
F32 = jnp.float32
BF16 = jnp.bfloat16


def dot(a, b):
    return jnp.dot(a, b, preferred_element_type=F32)


def dot_nt(a, b):
    return lax.dot_general(a, b, (((1,), (1,)), ((), ())), preferred_element_type=F32)


def dot_tn(a, b):
    return lax.dot_general(a, b, (((0,), (0,)), ((), ())), preferred_element_type=F32)


def dot_tt(a, b):
    return lax.dot_general(a, b, (((0,), (1,)), ((), ())), preferred_element_type=F32)


def cost(micros, moved):
    return pl.CostEstimate(flops=int(micros * 1e9), transcendentals=0, bytes_accessed=moved)


def prep_kernel(hid, w, b, bt, table, noise, q3, k3, v3, qt, kt, vt, lmt):
    heads = table.shape[0]
    tokens = hid.shape[0]
    hd = q3.shape[2]
    for h in range(heads):
        x = (table[h] + noise[h]) * (1.0 / SOFTENING)
        ls = jnp.minimum(x, 0.0) - jnp.log1p(jnp.exp(-jnp.abs(x)))
        lmt[h] = jnp.transpose(ls * LOG2E)

    step = 2 * BLOCK

    def project(i, _):
        rows = pl.ds(pl.multiple_of(i * step, step), step)
        x = hid[rows, :]
        for n, (nat, tr) in enumerate(((q3, qt), (k3, kt), (v3, vt))):
            y = dot(x, w[n])
            yt = dot_tt(w[n], x)
            if n != 1:
                y = y + b[n // 2 : n // 2 + 1, :]
                yt = yt + bt[:, n // 2 : n // 2 + 1]
            y = y.astype(BF16)
            for h in range(heads):
                nat[h, rows, :] = y[:, h * hd : (h + 1) * hd]
            tr[:, rows] = yt.astype(BF16)
        return 0

    lax.fori_loop(0, tokens // step, project, 0)


def attn_prep(hidden, w_qkv, b_qv, table, noise):
    tokens = hidden.shape[0]
    heads = table.shape[0]
    width = w_qkv.shape[2]
    sd = jax.ShapeDtypeStruct
    nat = sd((heads, tokens, width // heads), BF16)
    tr = sd((width, tokens), BF16)
    return pl.pallas_call(
        prep_kernel,
        out_shape=(nat, nat, nat, tr, tr, tr, sd(table.shape, F32)),
        compiler_params=pltpu.CompilerParams(vmem_limit_bytes=56 << 20),
        cost_estimate=cost(15, 20 << 20),
        name="attn_prep",
    )(hidden, w_qkv, b_qv, b_qv.T, table, noise)


def attn_fwd_kernel(lo, n_prev, qt, k3, vt, lmt, *refs):
    ctx, ctxt, lse = refs[n_prev:]
    heads, tokens, hd = k3.shape
    period = lmt.shape[1]
    width = heads * hd
    coef = LOG2E / math.sqrt(hd)
    parts = period // BLOCK
    lse[...] = jnp.zeros(lse.shape, F32)
    first = (pl.program_id(0) + lo) * parts

    def per_q(j, _):
        qb = first + j
        qcol = pl.ds(pl.multiple_of(qb * BLOCK, BLOCK), BLOCK)
        ocol = pl.ds(pl.multiple_of(j * BLOCK, BLOCK), BLOCK)
        mcol = ocol

        def per_k(kb, carry):
            krow = pl.ds(pl.multiple_of(kb * BLOCK, BLOCK), BLOCK)
            mrow = pl.ds(pl.multiple_of(lax.rem(kb, parts) * BLOCK, BLOCK), BLOCK)
            out = []
            ss = [dot(k3[h, krow, :], qt[h * hd : (h + 1) * hd, qcol]) for h in range(heads)]
            for h in range(heads):
                m, l, acc = carry[h]
                s = ss[h] * coef + lmt[h, mrow, mcol]
                mn = jnp.maximum(m, jnp.max(s, axis=0, keepdims=True))
                al = jnp.exp2(m - mn)
                p = jnp.exp2(s - mn)
                l = l * al + jnp.sum(p, axis=0, keepdims=True)
                acc = acc * al + dot(vt[h * hd : (h + 1) * hd, krow], p.astype(BF16))
                out.append((mn, l, acc))
            return tuple(out)

        init = tuple(
            (
                jnp.full((1, BLOCK), -1e30, F32),
                jnp.zeros((1, BLOCK), F32),
                jnp.zeros((hd, BLOCK), F32),
            )
            for _ in range(heads)
        )
        res = lax.fori_loop(0, qb + 1, per_k, init)
        cols = []
        for h in range(heads):
            m, l, acc = res[h]
            c = acc / l
            ctxt[h * hd : (h + 1) * hd, ocol] = c
            lse[h : h + 1, ocol] = m + jnp.log2(l)
            cols.append(c)
        pad = -width % 128
        if pad:
            cols.append(jnp.zeros((pad, BLOCK), F32))
        full = jnp.transpose(jnp.concatenate(cols, axis=0))
        ctx[ocol, :] = full[:, :width].astype(BF16)
        return 0

    lax.fori_loop(0, parts, per_q, 0)


def attn_fwd(qt, k3, vt, lmt, lo, hi, prev=()):
    heads, tokens, hd = k3.shape
    width = heads * hd
    period = lmt.shape[1]
    sd = jax.ShapeDtypeStruct
    whole = lambda x: pl.BlockSpec(x.shape, lambda i, n=len(x.shape): (0,) * n)
    return pl.pallas_call(
        functools.partial(attn_fwd_kernel, lo, len(prev)),
        grid=(hi - lo,),
        in_specs=[whole(x) for x in (qt, k3, vt, lmt)] + [pl.BlockSpec(memory_space=pl.ANY)] * len(prev),
        out_specs=(
            pl.BlockSpec((period, width), lambda i: (i + lo, 0)),
            pl.BlockSpec((width, period), lambda i: (0, i + lo)),
            pl.BlockSpec((8, period), lambda i: (0, i + lo)),
        ),
        out_shape=(sd((tokens, width), BF16), sd((width, tokens), F32), sd((8, tokens), F32)),
        input_output_aliases={4 + n: n for n in range(len(prev))},
        compiler_params=pltpu.CompilerParams(vmem_limit_bytes=56 << 20),
        cost_estimate=cost(1.5 * (hi * hi - lo * lo) / 2, 8 << 20),
        name="attn_fwd",
    )(qt, k3, vt, lmt, *prev)


def attn_bwd_kernel(n_t, place, *refs):
    pieces = refs[:n_t]
    (ctxt, q3, k3, v3, qt, kt, lse, lmt, gqkv, glm, gk, gv, g3, glmt, gctx, sems) = refs[n_t:]
    heads, tokens, hd = q3.shape
    chunk = tokens // n_t
    copies = []
    for s in range(n_t):
        at = lax.rem(place[0] + s, n_t) * chunk
        to = gctx.at[pl.ds(pl.multiple_of(at, chunk), chunk), :]
        copies.append(pltpu.make_async_copy(pieces[s], to, sems.at[s]))
    for cp in copies:
        cp.start()
    period = lmt.shape[1]
    width = heads * hd
    coef = LOG2E / math.sqrt(hd)
    scale = 1.0 / math.sqrt(hd)
    parts = period // BLOCK
    pad = -width % 128
    gk[...] = jnp.zeros(gk.shape, F32)
    gv[...] = jnp.zeros(gv.shape, F32)
    glmt[...] = jnp.zeros(glmt.shape, F32)
    for cp in copies:
        cp.wait()

    def per_q(i, _):
        qb = tokens // BLOCK - 1 - i
        qcol = pl.ds(pl.multiple_of(qb * BLOCK, BLOCK), BLOCK)
        mcol = pl.ds(pl.multiple_of(lax.rem(qb, parts) * BLOCK, BLOCK), BLOCK)
        g = gctx[qcol, :].astype(F32)
        gpad = jnp.concatenate([g, jnp.zeros((BLOCK, pad), F32)], axis=1) if pad else g
        gt = jnp.transpose(gpad)
        delta, gtb = [], []
        for h in range(heads):
            gth = gt[h * hd : (h + 1) * hd, :]
            delta.append(jnp.sum(gth * ctxt[h * hd : (h + 1) * hd, qcol], axis=0, keepdims=True))
            gtb.append(gth.astype(BF16))
            g3[h] = gctx[qcol, h * hd : (h + 1) * hd]

        def per_k(kb, carry):
            krow = pl.ds(pl.multiple_of(kb * BLOCK, BLOCK), BLOCK)
            mrow = pl.ds(pl.multiple_of(lax.rem(kb, parts) * BLOCK, BLOCK), BLOCK)
            out = []
            for h in range(heads):
                hs = slice(h * hd, (h + 1) * hd)
                s = dot(k3[h, krow, :], qt[hs, qcol]) * coef + lmt[h, mrow, mcol]
                p = jnp.exp2(s - lse[h : h + 1, qcol])
                dp = dot(v3[h, krow, :], gtb[h])
                ds = p * (dp - delta[h])
                dsb = ds.astype(BF16)
                glmt[h, mrow, mcol] += ds
                gv[h, krow, :] += dot(p.astype(BF16), g3[h])
                gk[h, krow, :] += dot(dsb, q3[h, qcol, :])
                out.append(carry[h] + dot(kt[hs, krow], dsb))
            return tuple(out)

        init = tuple(jnp.zeros((hd, BLOCK), F32) for _ in range(heads))
        res = lax.fori_loop(0, qb + 1, per_k, init)
        rows = [r * scale for r in res]
        if pad:
            rows.append(jnp.zeros((pad, BLOCK), F32))
        gq = jnp.transpose(jnp.concatenate(rows, axis=0))[:, :width]
        gkb = jnp.concatenate([gk[h, qcol, :] for h in range(heads)], axis=1) * scale
        gvb = jnp.concatenate([gv[h, qcol, :] for h in range(heads)], axis=1)
        y = jnp.concatenate([gq, gkb, gvb], axis=1).astype(BF16)
        pair = pl.ds(pl.multiple_of(qb // 2 * BLOCK, BLOCK), BLOCK)

        @pl.when(lax.rem(qb, 2) == 0)
        def _():
            gqkv[pair, : 3 * width] = y

        @pl.when(lax.rem(qb, 2) == 1)
        def _():
            gqkv[pair, 3 * width :] = y

        return 0

    lax.fori_loop(0, tokens // BLOCK, per_q, 0)
    for h in range(heads):
        glm[h] = jnp.transpose(glmt[h])


def attn_bwd(place, parts, ctxt, q3, k3, v3, qt, kt, lse, lmt):
    heads, tokens, hd = q3.shape
    width = heads * hd
    n_t = len(parts)
    sd = jax.ShapeDtypeStruct
    vm = pl.BlockSpec(memory_space=pltpu.VMEM)
    return pl.pallas_call(
        functools.partial(attn_bwd_kernel, n_t),
        in_specs=[pl.BlockSpec(memory_space=pltpu.SMEM)] + [pl.BlockSpec(memory_space=pl.ANY)] * n_t + [vm] * 8,
        out_shape=(sd((tokens // 2, 6 * width), BF16), sd(lmt.shape, F32)),
        scratch_shapes=[
            pltpu.VMEM((heads, tokens, hd), F32),
            pltpu.VMEM((heads, tokens, hd), F32),
            pltpu.VMEM((heads, BLOCK, hd), BF16),
            pltpu.VMEM(lmt.shape, F32),
            pltpu.VMEM((tokens, width), BF16),
            pltpu.SemaphoreType.DMA((n_t,)),
        ],
        compiler_params=pltpu.CompilerParams(vmem_limit_bytes=56 << 20),
        cost_estimate=cost(400, 20 << 20),
        name="attn_bwd",
    )(place, *parts, ctxt, q3, k3, v3, qt, kt, lse, lmt)


def wgrad_kernel(slab, spots, gb, first, act, grad_ffn, grad_attn, *refs):
    ctx, (send, keep, ao) = refs[:-3], refs[-3:]
    i = pl.program_id(0)
    n_t = len(ctx)
    piece = send.shape[2] - 2 * slab

    @pl.when(i == 0)
    def _():
        for z in range(n_t):
            ao[z] = dot_tn(ctx[z][...], grad_attn[...]).astype(BF16)

    def write(to):
        up = dot_tn(gb[...], first[...]).astype(BF16)
        down = dot_tn(act[...], grad_ffn[...]).astype(BF16)
        rows = pl.ds(pl.multiple_of(lax.rem(i, spots) * piece, piece), piece)
        for z in range(n_t):
            to[0, z, :slab, :] = up[z * slab : (z + 1) * slab]
            to[0, z, slab : slab + piece, :] = ao[z, rows, :]
            to[0, z, slab + piece :, :] = down[z * slab : (z + 1) * slab]

    @pl.when(i < spots)
    def _():
        write(send)

    @pl.when(i >= spots)
    def _():
        write(keep)


def wgrad(slab, spots, gb, first, act, grad_ffn, grad_attn, ctx):
    chunk, width = first.shape
    n_t = len(ctx)
    local = ctx[0].shape[1]
    wide = n_t * slab
    tall = 2 * slab + local // spots
    sd = jax.ShapeDtypeStruct
    vm = pl.BlockSpec(memory_space=pltpu.VMEM)
    cols = pl.BlockSpec((chunk, wide), lambda i: (0, jax.lax.rem(i + spots, 2 * spots)))
    send = lambda i: jnp.minimum(i, spots - 1)
    keep = lambda i: jnp.maximum(i - spots, 0)
    outs = [pl.BlockSpec((1, n_t, tall, width), lambda i, at=at: (at(i), 0, 0, 0)) for at in (send, keep)]
    shape = sd((spots, n_t, tall, width), BF16)
    return pl.pallas_call(
        functools.partial(wgrad_kernel, slab, spots),
        grid=(2 * spots,),
        in_specs=[cols, vm, cols, vm, vm] + [vm] * n_t,
        out_specs=tuple(outs),
        out_shape=(shape, shape),
        scratch_shapes=[pltpu.VMEM((n_t, local, width), BF16)],
        compiler_params=pltpu.CompilerParams(vmem_limit_bytes=40 << 20),
        cost_estimate=cost(400, 10 << 20),
        name="wgrad",
    )(gb, first, act, grad_ffn, grad_attn, *ctx)


def tail_kernel(hid, gqkv, glm, table, noise, tail, acc):
    heads, period, _ = glm.shape
    tokens, width = hid.shape
    wide = acc.shape[1]
    tall, lanes = tail.shape
    at = 2 * period + wide
    extra = lanes - at
    step = 2 * BLOCK
    for n in range(heads * period // BLOCK):
        h, at = n * BLOCK // period, n * BLOCK % period
        x = (table[h, at : at + BLOCK, :] + noise[h, at : at + BLOCK, :]) * (1.0 / SOFTENING)
        e = jnp.exp(-jnp.abs(x))
        slope = jnp.where(x > 0, e, 1.0) / (1.0 + e) * (1.0 / SOFTENING)
        g = (glm[h, at : at + BLOCK, :] * slope).astype(BF16)
        row, col = n * BLOCK % tall, n * BLOCK // tall * period
        tail[row : row + BLOCK, col : col + period] = g
    acc[...] = jnp.zeros(acc.shape, F32)

    def add(i, total):
        pair = pl.ds(pl.multiple_of(i * BLOCK, BLOCK), BLOCK)
        for n in range(2):
            rows = pl.ds(pl.multiple_of(i * step + n * BLOCK, BLOCK), BLOCK)
            y = gqkv[pair, n * wide : (n + 1) * wide]
            acc[...] += dot_tn(hid[rows, :], y)
            total = total + jnp.sum(y.astype(F32), axis=0, keepdims=True)
        return total

    total = lax.fori_loop(0, tokens // step, add, jnp.zeros((1, wide), F32))
    rows = [total[:, n * extra : (n + 1) * extra] for n in range(wide // extra)]
    rows.append(jnp.zeros((tall - len(rows), extra), F32))
    tail[:, 2 * period :] = jnp.concatenate([acc[...], jnp.concatenate(rows, axis=0)], axis=1).astype(BF16)


def tail_of(hidden, gqkv, glm, table, noise, wide):
    heads, period, _ = glm.shape
    width = hidden.shape[1]
    lanes = 2 * period + wide
    sd = jax.ShapeDtypeStruct
    return pl.pallas_call(
        tail_kernel,
        out_shape=sd((heads * period // 2, -(-lanes // 128) * 128), BF16),
        scratch_shapes=[pltpu.VMEM((width, wide), F32)],
        compiler_params=pltpu.CompilerParams(vmem_limit_bytes=56 << 20),
        cost_estimate=cost(400, 20 << 20),
        name="tail",
    )(hidden, gqkv, glm, table, noise)


def back_kernel(place, w, resid, *refs):
    pieces, out = refs[:-1], refs[-1]
    n_t, wide, _ = w.shape
    chunk = resid.shape[0]
    for at in range(0, chunk, 2 * BLOCK):
        for n in range(2):
            rows = slice(at + n * BLOCK, at + (n + 1) * BLOCK)
            total = resid[rows, :]
            for s in range(n_t):
                y = pieces[s][at // 2 : at // 2 + BLOCK, n * wide : (n + 1) * wide]
                total = total + dot(y, w[lax.rem(place[0] + n_t - s, n_t)])
            out[rows, :] = total.astype(BF16)


def back_of(place, w, resid, pieces):
    vm = pl.BlockSpec(memory_space=pltpu.VMEM)
    return pl.pallas_call(
        back_kernel,
        in_specs=[pl.BlockSpec(memory_space=pltpu.SMEM)] + [vm] * (2 + len(pieces)),
        out_shape=jax.ShapeDtypeStruct(resid.shape, BF16),
        compiler_params=pltpu.CompilerParams(vmem_limit_bytes=40 << 20),
        cost_estimate=cost(5, 10 << 20),
        name="back",
    )(place, w, resid, *pieces)


def norm_parts(resid):
    centred = resid - jnp.mean(resid, axis=-1, keepdims=True)
    rstd = lax.rsqrt(jnp.mean(centred * centred, axis=-1, keepdims=True) + EPS)
    return centred * rstd, rstd


def norm_back(grad, xhat, rstd, gain):
    gy = grad * gain
    return rstd * (
        gy
        - jnp.mean(gy, axis=-1, keepdims=True)
        - xhat * jnp.mean(gy * xhat, axis=-1, keepdims=True)
    )


def ffn_kernel(
    n_t, slab, core, *refs
):
    ctx = refs[:n_t]
    (wao, hid, teach, valid, vec, bup, up_o, up_m, up_t, dn_o, dn_m, dn_t,
     out, out_low, act, gb, first_low, grad_ffn, grad_attn, grad_resid, vecs, gbup) = refs[n_t : n_t + 22]
    gctx = refs[n_t + 22 : 2 * n_t + 22]
    up_s, dn_s, slope, xhat_s, sems = refs[2 * n_t + 22 :]
    units, width = up_s.shape
    half = units // 2
    spots = half // (n_t * slab)
    c = core[0]
    copies = []
    for n, (o, m, t, dst) in enumerate(((up_o, up_m, up_t, up_s), (dn_o, dn_m, dn_t, dn_s))):
        for side, f in enumerate((m, t)):
            base = (c if side == 0 else 1 - c) * (spots * slab)
            for p in range(spots):
                to = side * half + p * n_t * slab
                copies.append((n, o.at[pl.ds(pl.multiple_of(base + p * slab, slab), slab)], dst.at[pl.ds(to, slab)]))
                rest = (n_t - 1) * slab
                copies.append((n, f.at[pl.ds(p * rest, rest)], dst.at[pl.ds(to + slab, rest)]))
    copies = [pltpu.make_async_copy(a, b, sems.at[i]) for i, (n, a, b) in enumerate(copies)]
    for cp in copies:
        cp.start()
    b_ao, g1, b1, b_dn, g2, b2 = (vec[n : n + 1, :] for n in range(6))
    attention = sum(dot(ctx[s][...], wao[s]) for s in range(n_t)) + b_ao
    xhat1, rstd1 = norm_parts(hid[...].astype(F32) + attention)
    first = xhat1 * g1 + b1
    first_low[...] = first.astype(BF16)
    xhat_s[...] = xhat1
    for cp in copies:
        cp.wait()
    blocks, _, size = bup.shape

    def forward(i, feed):
        rows = pl.ds(pl.multiple_of(i * size, size), size)
        before = dot_nt(first_low[...], up_s[rows, :]) + bup[i]
        phi = 0.5 * (1.0 + lax.erf(before * math.sqrt(0.5)))
        dens = jnp.exp(-0.5 * before * before) * (1.0 / math.sqrt(2.0 * math.pi))
        low = (before * phi).astype(BF16)
        act[:, rows] = low
        slope[:, rows] = (phi + before * dens).astype(BF16)
        return feed + dot(low, dn_s[rows, :])

    feed = lax.fori_loop(0, blocks, forward, jnp.zeros(out.shape, F32))
    xhat2, rstd2 = norm_parts(first + feed + b_dn)
    own = xhat2 * g2 + b2
    out[...] = own
    out_low[...] = own.astype(BF16)
    residue = own - teach[...]
    weighed = valid[...] * residue
    grad_out = weighed
    total = lambda x: jnp.sum(x, axis=0, keepdims=True)
    vecs[4:5, :] = total(grad_out * xhat2)
    vecs[5:6, :] = total(grad_out)
    vecs[6:7, :] = total(weighed * residue)
    vecs[7:8, :] = jnp.broadcast_to(jnp.sum(valid[...], axis=0, keepdims=True), (1, width))
    grad_second = norm_back(grad_out, xhat2, rstd2, g2)
    grad_resid[...] = grad_second
    low = grad_second.astype(BF16)
    grad_ffn[...] = low
    vecs[3:4, :] = total(low.astype(F32))

    def backward(i, acc):
        rows = pl.ds(pl.multiple_of(i * size, size), size)
        g = dot_nt(grad_ffn[...], dn_s[rows, :]) * slope[:, rows].astype(F32)
        low = g.astype(BF16)
        gb[:, rows] = low
        gbup[i] = total(low.astype(F32))
        return acc + dot(low, up_s[rows, :])

    grad_first = lax.fori_loop(0, blocks, backward, jnp.zeros(out.shape, F32)) + grad_resid[...]
    xhat1 = xhat_s[...]
    vecs[1:2, :] = total(grad_first * xhat1)
    vecs[2:3, :] = total(grad_first)
    back = norm_back(grad_first, xhat1, rstd1, g1)
    grad_resid[...] = back
    low = back.astype(BF16)
    grad_attn[...] = low
    vecs[0:1, :] = total(low.astype(F32))
    local = ctx[0].shape[1]
    for s in range(n_t):
        gctx[s][...] = dot_nt(low, wao[s]).astype(BF16)


def ffn(core, ctx, wao, hid, teach, valid, vec, bup, ups, downs, slab):
    n_t = len(ctx)
    chunk, width = hid.shape
    local = ctx[0].shape[1]
    blocks, _, size = bup.shape
    units = blocks * size
    spots = units // (2 * n_t * slab)
    sd = jax.ShapeDtypeStruct
    vm = pl.BlockSpec(memory_space=pltpu.VMEM)
    sm = pl.BlockSpec(memory_space=pltpu.SMEM)
    hbm = pl.BlockSpec(memory_space=pl.ANY)
    return pl.pallas_call(
        functools.partial(ffn_kernel, n_t, slab),
        in_specs=[sm] + [vm] * (n_t + 6) + [hbm] * 6,
        out_shape=(
            sd((chunk, width), F32),
            sd((chunk, width), BF16),
            sd((chunk, units), BF16),
            sd((chunk, units), BF16),
            sd((chunk, width), BF16),
            sd((chunk, width), BF16),
            sd((chunk, width), BF16),
            sd((chunk, width), F32),
            sd((8, width), F32),
            sd((blocks, 1, size), F32),
            *[sd((chunk, local), BF16)] * n_t,
        ),
        scratch_shapes=[
            pltpu.VMEM((units, width), BF16),
            pltpu.VMEM((units, width), BF16),
            pltpu.VMEM((chunk, units), BF16),
            pltpu.VMEM((chunk, width), F32),
            pltpu.SemaphoreType.DMA((8 * spots,)),
        ],
        compiler_params=pltpu.CompilerParams(vmem_limit_bytes=56 << 20),
        cost_estimate=cost(34, 25 << 20),
        name="ffn",
    )(core, *ctx, wao, hid, teach, valid, vec, bup, *ups, *downs)


def shift(x, size, amount):
    return lax.ppermute(x, "tensor", [(j, (j + amount) % size) for j in range(size)])


def swap(x, axis, size, bit):
    return lax.ppermute(x, axis, [(j, j ^ bit) for j in range(size)])


def rows_of(x, start, count):
    return lax.dynamic_slice_in_dim(x, start, count, axis=0)


def body(
    hidden, teacher, valid, w_qkv, b_qv, w_attn_out, b_attn_out, gain_one, bias_one,
    w_up, b_up, w_down, b_down, gain_two, bias_two, table, noise, *, n_d, n_t,
):
    tokens, width = hidden.shape
    units = w_up.shape[1]
    local = w_qkv.shape[2]
    chunk = tokens // n_t
    ti = lax.axis_index("tensor")
    di = lax.axis_index("dp")
    group = min(n_d, 8)
    low_bits = [b for b in (2, 4) if b < group]
    high_bits = low_bits[::-1]
    extra = [b for b in (8, 16, 32, 64, 128, 256, 512) if b < n_d]
    spots = group // 2
    slab = units // group
    piece = local // spots
    core = di % 2
    spot = (di // 2) % spots

    def bit_of(bit):
        return (di // bit) % 2

    def dp_swap(x, bit):
        return swap(x, "dp", n_d, bit)

    def everyone(x):
        bit = 1
        while bit < n_d:
            x = x + dp_swap(x, bit)
            bit *= 2
        return x

    def spread(x, bits, other=None):
        done = []
        for bit in bits:
            if done or other is None:
                other = dp_swap(x, bit)
            up = bit_of(bit) == 1
            pos = sum(1 for b in done if b > bit)
            x = jnp.stack([jnp.where(up, other, x), jnp.where(up, x, other)], axis=pos)
            done.append(bit)
        return x.reshape((-1,) + x.shape[len(done) :])

    def narrow_start(x, bits):
        ax = sorted(bits, reverse=True).index(bits[0])
        up = bit_of(bits[0])
        send = lax.dynamic_index_in_dim(x, 1 - up, ax, keepdims=False)
        keep = lax.dynamic_index_in_dim(x, up, ax, keepdims=False)
        return keep, dp_swap(send, bits[0])

    def narrow_pair(x, y, bits, lo=0, count=None):
        ax = sorted(bits, reverse=True).index(bits[0])
        up = bit_of(bits[0])
        sizes = list(x.shape)
        sizes[ax] = 1
        sizes[-2] = count or sizes[-2]

        def half(i):
            at = [0] * x.ndim
            at[ax] = i
            at[-2] = lo
            part = lambda v: lax.dynamic_slice(v, at, sizes).astype(F32)
            return (part(x) + part(y)).astype(BF16).reshape(sizes[:ax] + sizes[ax + 1 :])

        return half(up), half(1 - up), bits[0]

    def narrow(x, bits):
        left = sorted(bits, reverse=True)
        for bit in bits:
            ax = left.index(bit)
            left.remove(bit)
            up = bit_of(bit)
            send = lax.dynamic_index_in_dim(x, 1 - up, ax, keepdims=False)
            keep = lax.dynamic_index_in_dim(x, up, ax, keepdims=False)
            x = (keep.astype(F32) + dp_swap(send, bit).astype(F32)).astype(BF16)
        return x

    def quad_parts(x):
        return [lax.dynamic_index_in_dim(x, spot ^ r, 0, keepdims=False) for r in range(spots)]

    def quad_sum(x):
        pieces = quad_parts(x)
        total = pieces[0].astype(F32)
        for r in range(1, spots):
            total = total + dp_swap(pieces[r], 2 * r).astype(F32)
        return total.astype(BF16)

    def quad_gather(x):
        held = [x] + [dp_swap(x, 2 * r) for r in range(1, spots)]
        step = 1
        while step < spots:
            flip = bit_of(2 * step) == 1
            held = [jnp.where(flip, held[r ^ step], held[r]) for r in range(spots)]
            step *= 2
        return held

    def finish(x):
        for bit in extra:
            x = (x.astype(F32) + dp_swap(x, bit).astype(F32)).astype(BF16)
        return x

    valid_f = valid[0].astype(F32)

    up_own = w_up.T
    b_hi = b_up.astype(BF16)
    b_lo = (b_up - b_hi.astype(F32)).astype(BF16)
    start = core * (spots * slab) + spot * slab
    sent = jnp.concatenate(
        [
            rows_of(up_own, start, slab),
            rows_of(w_attn_out, spot * piece, piece),
            rows_of(w_down, start, slab),
            b_hi[None],
            b_lo[None],
            jnp.zeros((14, width), BF16),
        ]
    )
    came = [shift(sent, n_t, s) for s in range(1, n_t)]

    w_t = w_qkv.transpose(0, 2, 1).reshape(3 * local, width)
    w_t = rows_of(w_t, core * (3 * local // 2), 3 * local // 2)
    q3, k3, v3, qt, kt, vt, lmt = attn_prep(hidden, w_qkv, b_qv, table, noise)
    n_sup = tokens // lmt.shape[1]
    cuts = [max(n_sup - 2, 1), max(n_sup - 1, 2)]
    part = attn_fwd(qt, k3, vt, lmt, 0, cuts[0])
    part, came, w_t = lax.optimization_barrier((part, came, w_t))
    w_side = lax.all_gather(w_t, "tensor", axis=0)

    cut = slab + piece
    wide_a = jnp.stack([x[:cut] for x in came])
    wide_b = jnp.stack([x[cut : cut + slab] for x in came])
    first_a = dp_swap(wide_a, low_bits[0])
    first_b = dp_swap(wide_b, high_bits[0])
    part = attn_fwd(qt, k3, vt, lmt, cuts[0], cuts[1], part)
    part, first_a, first_b = lax.optimization_barrier((part, first_a, first_b))
    ctx, ctxt, lse = attn_fwd(qt, k3, vt, lmt, cuts[1], n_sup, part)
    wide_a = spread(wide_a, low_bits, first_a)
    wide_b = spread(wide_b, high_bits, first_b)
    ctx_parts = [rows_of(ctx, ti * chunk, chunk)] + [
        shift(rows_of(ctx, lax.rem(ti + s, n_t) * chunk, chunk), n_t, s) for s in range(1, n_t)
    ]
    *ctx_parts, wide_a, wide_b, w_side = lax.optimization_barrier((*ctx_parts, wide_a, wide_b, w_side))
    up_m = wide_a[:, :, :slab].reshape(-1, width)
    down_m = wide_b.reshape(-1, width)
    wao = wide_a[:, :, slab:].transpose(1, 0, 2, 3).reshape(n_t - 1, local, width)
    wao = jnp.concatenate([w_attn_out[None], wao])
    up_t = dp_swap(up_m, 1)
    down_t = dp_swap(down_m, 1)
    b_all = jnp.stack(
        [b_up]
        + [x[cut + slab].astype(F32) + x[cut + slab + 1].astype(F32) for x in came]
    ).reshape(n_t, 2, spots, slab)
    b_mine = lax.dynamic_index_in_dim(b_all, core, 1, keepdims=False)
    b_theirs = lax.dynamic_index_in_dim(b_all, 1 - core, 1, keepdims=False)
    bup = jnp.stack([b_mine, b_theirs]).transpose(0, 2, 1, 3).reshape(2 * spots, 1, n_t * slab)

    w_other = dp_swap(w_side, 1)
    vec = jnp.stack([b_attn_out, gain_one, bias_one, b_down, gain_two, bias_two, b_down, b_down])
    (out_own, out_low, act, gb, first_low, grad_ffn, grad_attn, grad_resid, vecs, gbup, *gctx_rel) = ffn(
        core.reshape(1),
        ctx_parts,
        wao,
        rows_of(hidden, ti * chunk, chunk),
        rows_of(teacher, ti * chunk, chunk),
        lax.dynamic_slice_in_dim(valid_f, ti * chunk, chunk)[:, None],
        vec,
        bup,
        (up_own, up_m, up_t),
        (w_down, down_m, down_t),
        slab,
    )

    vecs, w_other, w_side = lax.optimization_barrier((vecs, w_other, w_side))
    up = core == 1
    gbu = gbup.reshape(2, spots, n_t, slab)
    gbu = jnp.where(up, gbu[::-1], gbu).transpose(2, 0, 1, 3).reshape(n_t, units)
    gbu = gbu[jnp.stack([lax.rem(ti - z + n_t, n_t) for z in range(n_t)])]
    pack = jnp.concatenate([vecs.reshape(-1), gbu.reshape(-1)]).reshape(-1, 128)

    parts = [gctx_rel[0]] + [shift(gctx_rel[s], n_t, -s) for s in range(1, n_t)]

    lead = (2,) * len(low_bits)
    send, keep = wgrad(slab, spots, gb, first_low, act, grad_ffn, grad_attn, ctx_parts)
    *parts, send, keep, out_low, pack = lax.optimization_barrier((*parts, send, keep, out_low, pack))
    pack_came = dp_swap(pack, 1)
    got = dp_swap(send, 1)
    out_all = lax.all_gather(out_low, "tensor", axis=0, tiled=True)

    gqkv, glm = attn_bwd(ti.reshape(1), parts, ctxt, q3, k3, v3, qt, kt, lse, lmt)
    gqkv, glm, keep, got, pack, pack_came = lax.optimization_barrier((gqkv, glm, keep, got, pack, pack_came))
    pack = pack + pack_came
    pack_came = dp_swap(pack, low_bits[0])
    pairs = chunk // 2
    parts = [rows_of(gqkv, ti * pairs, pairs)] + [
        shift(rows_of(gqkv, lax.rem(ti + s, n_t) * pairs, pairs), n_t, s) for s in range(1, n_t)
    ]
    tall = keep.shape[2]
    mid = -(-tall // 32) * 16
    keep = keep.reshape(lead + keep.shape[1:])
    got = got.reshape(lead + got.shape[1:])
    a_keep, a_send, bit = narrow_pair(keep, got, low_bits, 0, mid)
    a_came = dp_swap(a_send, bit)
    b_keep, b_send, bit = narrow_pair(keep, got, high_bits, mid, tall - mid)
    b_came = dp_swap(b_send, bit)
    tail = tail_of(hidden, gqkv, glm, table, noise, 3 * local)
    w_all = jnp.concatenate([jnp.where(up, w_other, w_side), jnp.where(up, w_side, w_other)], axis=1)
    near = [s for s in range(n_t) if s in (0, 1, n_t - 1)]
    far = [s for s in range(n_t) if s not in near]
    held = lax.optimization_barrier(
        (w_all, tail, a_keep, a_came, b_keep, b_came, pack, pack_came, *[parts[s] for s in near])
    )
    w_all, tail, a_keep, a_came, b_keep, b_came, pack, pack_came = held[:8]
    for n, s in enumerate(near):
        parts[s] = held[8 + n]
    pack = pack + pack_came
    pack_came = dp_swap(pack, low_bits[1])
    a_keep, a_send, bit = narrow_pair(a_keep, a_came, low_bits[1:])
    a_came = dp_swap(a_send, bit)
    b_keep, b_send, bit = narrow_pair(b_keep, b_came, high_bits[1:])
    b_came = dp_swap(b_send, bit)
    tail = tail.reshape((2,) + lead + (-1, tail.shape[1]))
    send = lax.dynamic_index_in_dim(tail, 1 - core, 0, keepdims=False)
    t_keep = lax.dynamic_index_in_dim(tail, core, 0, keepdims=False)
    t_keep, t_send, bit = narrow_pair(t_keep, dp_swap(send, 1), low_bits)
    t_came = dp_swap(t_send, bit)
    held = lax.optimization_barrier(
        (a_keep, a_came, b_keep, b_came, pack, pack_came, *[parts[s] for s in far])
    )
    a_keep, a_came, b_keep, b_came, pack, pack_came = held[:6]
    for n, s in enumerate(far):
        parts[s] = held[6 + n]
    g_a = (a_keep.astype(F32) + a_came.astype(F32)).astype(BF16)
    g_b = (b_keep.astype(F32) + b_came.astype(F32)).astype(BF16)
    g_a = finish(narrow(g_a, low_bits[2:]))
    g_b = finish(narrow(g_b, high_bits[2:]))
    pack = pack + pack_came
    pack_came = swap(pack, "tensor", n_t, 1)
    total = jnp.concatenate([g_a, g_b], axis=1)
    pieces = [total[0]] + [shift(total[s], n_t, -s) for s in range(1, n_t)]
    back = back_of(ti.reshape(1), w_all, grad_resid, parts)
    tail = finish(narrow((t_keep.astype(F32) + t_came.astype(F32)).astype(BF16), low_bits[1:]))
    back, tail, pack, pack_came, *pieces = lax.optimization_barrier((back, tail, pack, pack_came, *pieces))
    grad_hidden = lax.all_gather(back, "tensor", axis=0, tiled=True)
    summed = pieces[0].astype(F32)
    for p in pieces[1:]:
        summed = summed + p.astype(F32)
    held = quad_gather(summed.astype(BF16))
    tail = jnp.concatenate(quad_gather(tail))
    other = dp_swap(tail, 1)
    tail = jnp.concatenate([jnp.where(up, other, tail), jnp.where(up, tail, other)])
    g_ao = jnp.concatenate([x[slab:cut] for x in held])
    pair = jnp.stack([jnp.concatenate([x[:slab] for x in held]), jnp.concatenate([x[cut:] for x in held])])
    other = dp_swap(pair, 1)
    pair = jnp.concatenate([jnp.where(up, other, pair), jnp.where(up, pair, other)], axis=1)
    pack = pack + pack_came
    for bit in low_bits[2:] + extra:
        pack = pack + dp_swap(pack, bit)
    bit = 2
    while bit < n_t:
        pack = pack + swap(pack, "tensor", n_t, bit)
        bit *= 2
    cols = table.shape[2]
    at = 2 * cols + 3 * local
    extra_cols = tail.shape[1] - at
    g_mask = jnp.stack([tail[:, :cols], tail[:, cols : 2 * cols]])
    g_qkv_w = jnp.stack([tail[:, 2 * cols + n * local : 2 * cols + (n + 1) * local] for n in range(3)])
    g_b_qv = tail[: 3 * local // extra_cols, at:].reshape(3, local)[0::2]
    out_states = out_all.astype(F32)
    g_up = pair[0].T
    g_down = pair[1]

    pack = pack.reshape(-1)
    rows = [pack[n * width : (n + 1) * width] for n in range(8)]
    gbu = lax.dynamic_slice_in_dim(pack, 8 * width + ti * units, units)
    total_valid = rows[7][0]
    loss = jnp.sum(rows[6]) / (total_valid * width)
    coef = 2.0 * tokens / total_valid
    grads = [
        grad_hidden, g_qkv_w.reshape(w_qkv.shape), g_b_qv.reshape(2, local), g_ao, rows[0], rows[1], rows[2],
        g_up, gbu, g_down, rows[3], rows[4], rows[5], g_mask.reshape(table.shape),
    ]
    return (out_states, loss, *[g.astype(F32) * coef for g in grads])


def solution(mesh):
    row, col = P("tensor", None), P(None, "tensor")
    heads = P("tensor", None, None)
    dp = P("dp", None)
    qkv = P(None, None, "tensor")
    sizes = dict(mesh.shape)
    return jax.shard_map(
        functools.partial(body, n_d=sizes["dp"], n_t=sizes["tensor"]),
        mesh=mesh,
        in_specs=(dp, dp, dp, qkv, col, row, P(), P(), P(), col, P("tensor"), row, P(), P(), P(), heads, heads),
        out_specs=(dp, P(), dp, qkv, col, row, P(), P(), P(), col, P("tensor"), row, P(), P(), P(), heads),
        check_vma=False,
    )
```

```python
import functools
import math

import jax
import jax.numpy as jnp
from jax import lax
from jax.experimental import pallas as pl
from jax.experimental.pallas import tpu as pltpu
from jax.sharding import PartitionSpec as P

BLOCK = 256
LOG2E = math.log2(math.e)
SOFTENING = 0.5
EPS = 1e-6
F32 = jnp.float32
BF16 = jnp.bfloat16


def dot(a, b):
    return jnp.dot(a, b, preferred_element_type=F32)


def dot_nt(a, b):
    return lax.dot_general(a, b, (((1,), (1,)), ((), ())), preferred_element_type=F32)


def dot_tn(a, b):
    return lax.dot_general(a, b, (((0,), (0,)), ((), ())), preferred_element_type=F32)


def dot_tt(a, b):
    return lax.dot_general(a, b, (((0,), (1,)), ((), ())), preferred_element_type=F32)


def cost(micros, moved):
    return pl.CostEstimate(flops=int(micros * 1e9), transcendentals=0, bytes_accessed=moved)


def prep_kernel(hid, w, b, bt, table, noise, q3, k3, v3, qt, kt, vt, lmt):
    heads = table.shape[0]
    tokens = hid.shape[0]
    hd = q3.shape[2]
    for h in range(heads):
        x = (table[h] + noise[h]) * (1.0 / SOFTENING)
        ls = jnp.minimum(x, 0.0) - jnp.log1p(jnp.exp(-jnp.abs(x)))
        lmt[h] = jnp.transpose(ls * LOG2E)

    step = 2 * BLOCK

    def project(i, _):
        rows = pl.ds(pl.multiple_of(i * step, step), step)
        x = hid[rows, :]
        for n, (nat, tr) in enumerate(((q3, qt), (k3, kt), (v3, vt))):
            y = dot(x, w[n])
            yt = dot_tt(w[n], x)
            if n != 1:
                y = y + b[n // 2 : n // 2 + 1, :]
                yt = yt + bt[:, n // 2 : n // 2 + 1]
            y = y.astype(BF16)
            for h in range(heads):
                nat[h, rows, :] = y[:, h * hd : (h + 1) * hd]
            tr[:, rows] = yt.astype(BF16)
        return 0

    lax.fori_loop(0, tokens // step, project, 0)


def attn_prep(hidden, w_qkv, b_qv, table, noise):
    tokens = hidden.shape[0]
    heads = table.shape[0]
    width = w_qkv.shape[2]
    sd = jax.ShapeDtypeStruct
    nat = sd((heads, tokens, width // heads), BF16)
    tr = sd((width, tokens), BF16)
    return pl.pallas_call(
        prep_kernel,
        out_shape=(nat, nat, nat, tr, tr, tr, sd(table.shape, F32)),
        compiler_params=pltpu.CompilerParams(vmem_limit_bytes=56 << 20),
        cost_estimate=cost(15, 20 << 20),
        name="attn_prep",
    )(hidden, w_qkv, b_qv, b_qv.T, table, noise)


def attn_fwd_kernel(lo, n_prev, qt, k3, vt, lmt, *refs):
    ctx, ctxt, lse = refs[n_prev:]
    heads, tokens, hd = k3.shape
    period = lmt.shape[1]
    width = heads * hd
    coef = LOG2E / math.sqrt(hd)
    parts = period // BLOCK
    lse[...] = jnp.zeros(lse.shape, F32)
    first = (pl.program_id(0) + lo) * parts

    def per_q(j, _):
        qb = first + j
        qcol = pl.ds(pl.multiple_of(qb * BLOCK, BLOCK), BLOCK)
        ocol = pl.ds(pl.multiple_of(j * BLOCK, BLOCK), BLOCK)
        mcol = ocol

        def per_k(kb, carry):
            krow = pl.ds(pl.multiple_of(kb * BLOCK, BLOCK), BLOCK)
            mrow = pl.ds(pl.multiple_of(lax.rem(kb, parts) * BLOCK, BLOCK), BLOCK)
            out = []
            ss = [dot(k3[h, krow, :], qt[h * hd : (h + 1) * hd, qcol]) for h in range(heads)]
            for h in range(heads):
                m, l, acc = carry[h]
                s = ss[h] * coef + lmt[h, mrow, mcol]
                mn = jnp.maximum(m, jnp.max(s, axis=0, keepdims=True))
                al = jnp.exp2(m - mn)
                p = jnp.exp2(s - mn)
                l = l * al + jnp.sum(p, axis=0, keepdims=True)
                acc = acc * al + dot(vt[h * hd : (h + 1) * hd, krow], p.astype(BF16))
                out.append((mn, l, acc))
            return tuple(out)

        init = tuple(
            (
                jnp.full((1, BLOCK), -1e30, F32),
                jnp.zeros((1, BLOCK), F32),
                jnp.zeros((hd, BLOCK), F32),
            )
            for _ in range(heads)
        )
        res = lax.fori_loop(0, qb + 1, per_k, init)
        cols = []
        for h in range(heads):
            m, l, acc = res[h]
            c = acc / l
            ctxt[h * hd : (h + 1) * hd, ocol] = c
            lse[h : h + 1, ocol] = m + jnp.log2(l)
            cols.append(c)
        pad = -width % 128
        if pad:
            cols.append(jnp.zeros((pad, BLOCK), F32))
        full = jnp.transpose(jnp.concatenate(cols, axis=0))
        ctx[ocol, :] = full[:, :width].astype(BF16)
        return 0

    lax.fori_loop(0, parts, per_q, 0)


def attn_fwd(qt, k3, vt, lmt, lo, hi, prev=()):
    heads, tokens, hd = k3.shape
    width = heads * hd
    period = lmt.shape[1]
    sd = jax.ShapeDtypeStruct
    whole = lambda x: pl.BlockSpec(x.shape, lambda i, n=len(x.shape): (0,) * n)
    return pl.pallas_call(
        functools.partial(attn_fwd_kernel, lo, len(prev)),
        grid=(hi - lo,),
        in_specs=[whole(x) for x in (qt, k3, vt, lmt)] + [pl.BlockSpec(memory_space=pl.ANY)] * len(prev),
        out_specs=(
            pl.BlockSpec((period, width), lambda i: (i + lo, 0)),
            pl.BlockSpec((width, period), lambda i: (0, i + lo)),
            pl.BlockSpec((8, period), lambda i: (0, i + lo)),
        ),
        out_shape=(sd((tokens, width), BF16), sd((width, tokens), F32), sd((8, tokens), F32)),
        input_output_aliases={4 + n: n for n in range(len(prev))},
        compiler_params=pltpu.CompilerParams(vmem_limit_bytes=56 << 20),
        cost_estimate=cost(1.5 * (hi * hi - lo * lo) / 2, 8 << 20),
        name="attn_fwd",
    )(qt, k3, vt, lmt, *prev)


def attn_bwd_kernel(n_t, place, *refs):
    pieces = refs[:n_t]
    (ctxt, q3, k3, v3, qt, kt, lse, lmt, gqkv, glm, gk, gv, g3, glmt, gctx, sems) = refs[n_t:]
    heads, tokens, hd = q3.shape
    chunk = tokens // n_t
    copies = []
    for s in range(n_t):
        at = lax.rem(place[0] + s, n_t) * chunk
        to = gctx.at[pl.ds(pl.multiple_of(at, chunk), chunk), :]
        copies.append(pltpu.make_async_copy(pieces[s], to, sems.at[s]))
    for cp in copies:
        cp.start()
    period = lmt.shape[1]
    width = heads * hd
    coef = LOG2E / math.sqrt(hd)
    scale = 1.0 / math.sqrt(hd)
    parts = period // BLOCK
    pad = -width % 128
    gk[...] = jnp.zeros(gk.shape, F32)
    gv[...] = jnp.zeros(gv.shape, F32)
    glmt[...] = jnp.zeros(glmt.shape, F32)
    for cp in copies:
        cp.wait()

    def per_q(i, _):
        qb = tokens // BLOCK - 1 - i
        qcol = pl.ds(pl.multiple_of(qb * BLOCK, BLOCK), BLOCK)
        mcol = pl.ds(pl.multiple_of(lax.rem(qb, parts) * BLOCK, BLOCK), BLOCK)
        g = gctx[qcol, :].astype(F32)
        gpad = jnp.concatenate([g, jnp.zeros((BLOCK, pad), F32)], axis=1) if pad else g
        gt = jnp.transpose(gpad)
        delta, gtb = [], []
        for h in range(heads):
            gth = gt[h * hd : (h + 1) * hd, :]
            delta.append(jnp.sum(gth * ctxt[h * hd : (h + 1) * hd, qcol], axis=0, keepdims=True))
            gtb.append(gth.astype(BF16))
            g3[h] = gctx[qcol, h * hd : (h + 1) * hd]

        def per_k(kb, carry):
            krow = pl.ds(pl.multiple_of(kb * BLOCK, BLOCK), BLOCK)
            mrow = pl.ds(pl.multiple_of(lax.rem(kb, parts) * BLOCK, BLOCK), BLOCK)
            out = []
            for h in range(heads):
                hs = slice(h * hd, (h + 1) * hd)
                s = dot(k3[h, krow, :], qt[hs, qcol]) * coef + lmt[h, mrow, mcol]
                p = jnp.exp2(s - lse[h : h + 1, qcol])
                dp = dot(v3[h, krow, :], gtb[h])
                ds = p * (dp - delta[h])
                dsb = ds.astype(BF16)
                glmt[h, mrow, mcol] += ds
                gv[h, krow, :] += dot(p.astype(BF16), g3[h])
                gk[h, krow, :] += dot(dsb, q3[h, qcol, :])
                out.append(carry[h] + dot(kt[hs, krow], dsb))
            return tuple(out)

        init = tuple(jnp.zeros((hd, BLOCK), F32) for _ in range(heads))
        res = lax.fori_loop(0, qb + 1, per_k, init)
        rows = [r * scale for r in res]
        if pad:
            rows.append(jnp.zeros((pad, BLOCK), F32))
        gq = jnp.transpose(jnp.concatenate(rows, axis=0))[:, :width]
        gkb = jnp.concatenate([gk[h, qcol, :] for h in range(heads)], axis=1) * scale
        gvb = jnp.concatenate([gv[h, qcol, :] for h in range(heads)], axis=1)
        y = jnp.concatenate([gq, gkb, gvb], axis=1).astype(BF16)
        pair = pl.ds(pl.multiple_of(qb // 2 * BLOCK, BLOCK), BLOCK)

        @pl.when(lax.rem(qb, 2) == 0)
        def _():
            gqkv[pair, : 3 * width] = y

        @pl.when(lax.rem(qb, 2) == 1)
        def _():
            gqkv[pair, 3 * width :] = y

        return 0

    lax.fori_loop(0, tokens // BLOCK, per_q, 0)
    for h in range(heads):
        glm[h] = jnp.transpose(glmt[h])


def attn_bwd(place, parts, ctxt, q3, k3, v3, qt, kt, lse, lmt):
    heads, tokens, hd = q3.shape
    width = heads * hd
    n_t = len(parts)
    sd = jax.ShapeDtypeStruct
    vm = pl.BlockSpec(memory_space=pltpu.VMEM)
    return pl.pallas_call(
        functools.partial(attn_bwd_kernel, n_t),
        in_specs=[pl.BlockSpec(memory_space=pltpu.SMEM)] + [pl.BlockSpec(memory_space=pl.ANY)] * n_t + [vm] * 8,
        out_shape=(sd((tokens // 2, 6 * width), BF16), sd(lmt.shape, F32)),
        scratch_shapes=[
            pltpu.VMEM((heads, tokens, hd), F32),
            pltpu.VMEM((heads, tokens, hd), F32),
            pltpu.VMEM((heads, BLOCK, hd), BF16),
            pltpu.VMEM(lmt.shape, F32),
            pltpu.VMEM((tokens, width), BF16),
            pltpu.SemaphoreType.DMA((n_t,)),
        ],
        compiler_params=pltpu.CompilerParams(vmem_limit_bytes=56 << 20),
        cost_estimate=cost(400, 20 << 20),
        name="attn_bwd",
    )(place, *parts, ctxt, q3, k3, v3, qt, kt, lse, lmt)


def wgrad_kernel(slab, spots, gb, first, act, grad_ffn, grad_attn, *refs):
    ctx, (send, keep, ao) = refs[:-3], refs[-3:]
    i = pl.program_id(0)
    n_t = len(ctx)
    piece = send.shape[2] - 2 * slab

    @pl.when(i == 0)
    def _():
        for z in range(n_t):
            ao[z] = dot_tn(ctx[z][...], grad_attn[...]).astype(BF16)

    def write(to):
        up = dot_tn(gb[...], first[...]).astype(BF16)
        down = dot_tn(act[...], grad_ffn[...]).astype(BF16)
        rows = pl.ds(pl.multiple_of(lax.rem(i, spots) * piece, piece), piece)
        for z in range(n_t):
            to[0, z, :slab, :] = up[z * slab : (z + 1) * slab]
            to[0, z, slab : slab + piece, :] = ao[z, rows, :]
            to[0, z, slab + piece :, :] = down[z * slab : (z + 1) * slab]

    @pl.when(i < spots)
    def _():
        write(send)

    @pl.when(i >= spots)
    def _():
        write(keep)


def wgrad(slab, spots, gb, first, act, grad_ffn, grad_attn, ctx):
    chunk, width = first.shape
    n_t = len(ctx)
    local = ctx[0].shape[1]
    wide = n_t * slab
    tall = 2 * slab + local // spots
    sd = jax.ShapeDtypeStruct
    vm = pl.BlockSpec(memory_space=pltpu.VMEM)
    cols = pl.BlockSpec((chunk, wide), lambda i: (0, jax.lax.rem(i + spots, 2 * spots)))
    send = lambda i: jnp.minimum(i, spots - 1)
    keep = lambda i: jnp.maximum(i - spots, 0)
    outs = [pl.BlockSpec((1, n_t, tall, width), lambda i, at=at: (at(i), 0, 0, 0)) for at in (send, keep)]
    shape = sd((spots, n_t, tall, width), BF16)
    return pl.pallas_call(
        functools.partial(wgrad_kernel, slab, spots),
        grid=(2 * spots,),
        in_specs=[cols, vm, cols, vm, vm] + [vm] * n_t,
        out_specs=tuple(outs),
        out_shape=(shape, shape),
        scratch_shapes=[pltpu.VMEM((n_t, local, width), BF16)],
        compiler_params=pltpu.CompilerParams(vmem_limit_bytes=40 << 20),
        cost_estimate=cost(400, 10 << 20),
        name="wgrad",
    )(gb, first, act, grad_ffn, grad_attn, *ctx)


def tail_kernel(hid, gqkv, glm, table, noise, tail, acc):
    heads, period, _ = glm.shape
    tokens, width = hid.shape
    wide = acc.shape[1]
    tall, lanes = tail.shape
    at = 2 * period + wide
    extra = lanes - at
    step = 2 * BLOCK
    for n in range(heads * period // BLOCK):
        h, at = n * BLOCK // period, n * BLOCK % period
        x = (table[h, at : at + BLOCK, :] + noise[h, at : at + BLOCK, :]) * (1.0 / SOFTENING)
        e = jnp.exp(-jnp.abs(x))
        slope = jnp.where(x > 0, e, 1.0) / (1.0 + e) * (1.0 / SOFTENING)
        g = (glm[h, at : at + BLOCK, :] * slope).astype(BF16)
        row, col = n * BLOCK % tall, n * BLOCK // tall * period
        tail[row : row + BLOCK, col : col + period] = g
    acc[...] = jnp.zeros(acc.shape, F32)

    def add(i, total):
        pair = pl.ds(pl.multiple_of(i * BLOCK, BLOCK), BLOCK)
        for n in range(2):
            rows = pl.ds(pl.multiple_of(i * step + n * BLOCK, BLOCK), BLOCK)
            y = gqkv[pair, n * wide : (n + 1) * wide]
            acc[...] += dot_tn(hid[rows, :], y)
            total = total + jnp.sum(y.astype(F32), axis=0, keepdims=True)
        return total

    total = lax.fori_loop(0, tokens // step, add, jnp.zeros((1, wide), F32))
    rows = [total[:, n * extra : (n + 1) * extra] for n in range(wide // extra)]
    rows.append(jnp.zeros((tall - len(rows), extra), F32))
    tail[:, 2 * period :] = jnp.concatenate([acc[...], jnp.concatenate(rows, axis=0)], axis=1).astype(BF16)


def tail_of(hidden, gqkv, glm, table, noise, wide):
    heads, period, _ = glm.shape
    width = hidden.shape[1]
    lanes = 2 * period + wide
    sd = jax.ShapeDtypeStruct
    return pl.pallas_call(
        tail_kernel,
        out_shape=sd((heads * period // 2, -(-lanes // 128) * 128), BF16),
        scratch_shapes=[pltpu.VMEM((width, wide), F32)],
        compiler_params=pltpu.CompilerParams(vmem_limit_bytes=56 << 20),
        cost_estimate=cost(400, 20 << 20),
        name="tail",
    )(hidden, gqkv, glm, table, noise)


def back_kernel(place, w, resid, *refs):
    pieces, out = refs[:-1], refs[-1]
    n_t, wide, _ = w.shape
    chunk = resid.shape[0]
    for at in range(0, chunk, 2 * BLOCK):
        for n in range(2):
            rows = slice(at + n * BLOCK, at + (n + 1) * BLOCK)
            total = resid[rows, :]
            for s in range(n_t):
                y = pieces[s][at // 2 : at // 2 + BLOCK, n * wide : (n + 1) * wide]
                total = total + dot(y, w[lax.rem(place[0] + n_t - s, n_t)])
            out[rows, :] = total.astype(BF16)


def back_of(place, w, resid, pieces):
    vm = pl.BlockSpec(memory_space=pltpu.VMEM)
    return pl.pallas_call(
        back_kernel,
        in_specs=[pl.BlockSpec(memory_space=pltpu.SMEM)] + [vm] * (2 + len(pieces)),
        out_shape=jax.ShapeDtypeStruct(resid.shape, BF16),
        compiler_params=pltpu.CompilerParams(vmem_limit_bytes=40 << 20),
        cost_estimate=cost(5, 10 << 20),
        name="back",
    )(place, w, resid, *pieces)


def norm_parts(resid):
    centred = resid - jnp.mean(resid, axis=-1, keepdims=True)
    rstd = lax.rsqrt(jnp.mean(centred * centred, axis=-1, keepdims=True) + EPS)
    return centred * rstd, rstd


def norm_back(grad, xhat, rstd, gain):
    gy = grad * gain
    return rstd * (
        gy
        - jnp.mean(gy, axis=-1, keepdims=True)
        - xhat * jnp.mean(gy * xhat, axis=-1, keepdims=True)
    )


def ffn_kernel(
    n_t, slab, core, *refs
):
    ctx = refs[:n_t]
    (wao, hid, teach, valid, vec, bup, up_o, up_m, up_t, dn_o, dn_m, dn_t,
     out, out_low, act, gb, first_low, grad_ffn, grad_attn, grad_resid, vecs, gbup) = refs[n_t : n_t + 22]
    gctx = refs[n_t + 22 : 2 * n_t + 22]
    up_s, dn_s, slope, xhat_s, sems = refs[2 * n_t + 22 :]
    units, width = up_s.shape
    half = units // 2
    spots = half // (n_t * slab)
    c = core[0]
    copies = []
    for n, (o, m, t, dst) in enumerate(((up_o, up_m, up_t, up_s), (dn_o, dn_m, dn_t, dn_s))):
        for side, f in enumerate((m, t)):
            base = (c if side == 0 else 1 - c) * (spots * slab)
            for p in range(spots):
                to = side * half + p * n_t * slab
                copies.append((n, o.at[pl.ds(pl.multiple_of(base + p * slab, slab), slab)], dst.at[pl.ds(to, slab)]))
                rest = (n_t - 1) * slab
                copies.append((n, f.at[pl.ds(p * rest, rest)], dst.at[pl.ds(to + slab, rest)]))
    copies = [pltpu.make_async_copy(a, b, sems.at[i]) for i, (n, a, b) in enumerate(copies)]
    for cp in copies:
        cp.start()
    b_ao, g1, b1, b_dn, g2, b2 = (vec[n : n + 1, :] for n in range(6))
    attention = sum(dot(ctx[s][...], wao[s]) for s in range(n_t)) + b_ao
    xhat1, rstd1 = norm_parts(hid[...].astype(F32) + attention)
    first = xhat1 * g1 + b1
    first_low[...] = first.astype(BF16)
    xhat_s[...] = xhat1
    for cp in copies:
        cp.wait()
    blocks, _, size = bup.shape

    def forward(i, feed):
        rows = pl.ds(pl.multiple_of(i * size, size), size)
        before = dot_nt(first_low[...], up_s[rows, :]) + bup[i]
        phi = 0.5 * (1.0 + lax.erf(before * math.sqrt(0.5)))
        dens = jnp.exp(-0.5 * before * before) * (1.0 / math.sqrt(2.0 * math.pi))
        low = (before * phi).astype(BF16)
        act[:, rows] = low
        slope[:, rows] = (phi + before * dens).astype(BF16)
        return feed + dot(low, dn_s[rows, :])

    feed = lax.fori_loop(0, blocks, forward, jnp.zeros(out.shape, F32))
    xhat2, rstd2 = norm_parts(first + feed + b_dn)
    own = xhat2 * g2 + b2
    out[...] = own
    out_low[...] = own.astype(BF16)
    residue = own - teach[...]
    weighed = valid[...] * residue
    grad_out = weighed
    total = lambda x: jnp.sum(x, axis=0, keepdims=True)
    vecs[4:5, :] = total(grad_out * xhat2)
    vecs[5:6, :] = total(grad_out)
    vecs[6:7, :] = total(weighed * residue)
    vecs[7:8, :] = jnp.broadcast_to(jnp.sum(valid[...], axis=0, keepdims=True), (1, width))
    grad_second = norm_back(grad_out, xhat2, rstd2, g2)
    grad_resid[...] = grad_second
    low = grad_second.astype(BF16)
    grad_ffn[...] = low
    vecs[3:4, :] = total(low.astype(F32))

    def backward(i, acc):
        rows = pl.ds(pl.multiple_of(i * size, size), size)
        g = dot_nt(grad_ffn[...], dn_s[rows, :]) * slope[:, rows].astype(F32)
        low = g.astype(BF16)
        gb[:, rows] = low
        gbup[i] = total(low.astype(F32))
        return acc + dot(low, up_s[rows, :])

    grad_first = lax.fori_loop(0, blocks, backward, jnp.zeros(out.shape, F32)) + grad_resid[...]
    xhat1 = xhat_s[...]
    vecs[1:2, :] = total(grad_first * xhat1)
    vecs[2:3, :] = total(grad_first)
    back = norm_back(grad_first, xhat1, rstd1, g1)
    grad_resid[...] = back
    low = back.astype(BF16)
    grad_attn[...] = low
    vecs[0:1, :] = total(low.astype(F32))
    local = ctx[0].shape[1]
    for s in range(n_t):
        gctx[s][...] = dot_nt(low, wao[s]).astype(BF16)


def ffn(core, ctx, wao, hid, teach, valid, vec, bup, ups, downs, slab):
    n_t = len(ctx)
    chunk, width = hid.shape
    local = ctx[0].shape[1]
    blocks, _, size = bup.shape
    units = blocks * size
    spots = units // (2 * n_t * slab)
    sd = jax.ShapeDtypeStruct
    vm = pl.BlockSpec(memory_space=pltpu.VMEM)
    sm = pl.BlockSpec(memory_space=pltpu.SMEM)
    hbm = pl.BlockSpec(memory_space=pl.ANY)
    return pl.pallas_call(
        functools.partial(ffn_kernel, n_t, slab),
        in_specs=[sm] + [vm] * (n_t + 6) + [hbm] * 6,
        out_shape=(
            sd((chunk, width), F32),
            sd((chunk, width), BF16),
            sd((chunk, units), BF16),
            sd((chunk, units), BF16),
            sd((chunk, width), BF16),
            sd((chunk, width), BF16),
            sd((chunk, width), BF16),
            sd((chunk, width), F32),
            sd((8, width), F32),
            sd((blocks, 1, size), F32),
            *[sd((chunk, local), BF16)] * n_t,
        ),
        scratch_shapes=[
            pltpu.VMEM((units, width), BF16),
            pltpu.VMEM((units, width), BF16),
            pltpu.VMEM((chunk, units), BF16),
            pltpu.VMEM((chunk, width), F32),
            pltpu.SemaphoreType.DMA((8 * spots,)),
        ],
        compiler_params=pltpu.CompilerParams(vmem_limit_bytes=56 << 20),
        cost_estimate=cost(34, 25 << 20),
        name="ffn",
    )(core, *ctx, wao, hid, teach, valid, vec, bup, *ups, *downs)


def shift(x, size, amount):
    return lax.ppermute(x, "tensor", [(j, (j + amount) % size) for j in range(size)])


def swap(x, axis, size, bit):
    return lax.ppermute(x, axis, [(j, j ^ bit) for j in range(size)])


def rows_of(x, start, count):
    return lax.dynamic_slice_in_dim(x, start, count, axis=0)


def body(
    hidden, teacher, valid, w_qkv, b_qv, w_attn_out, b_attn_out, gain_one, bias_one,
    w_up, b_up, w_down, b_down, gain_two, bias_two, table, noise, *, n_d, n_t,
):
    tokens, width = hidden.shape
    units = w_up.shape[1]
    local = w_qkv.shape[2]
    chunk = tokens // n_t
    ti = lax.axis_index("tensor")
    di = lax.axis_index("dp")
    group = min(n_d, 8)
    low_bits = [b for b in (2, 4) if b < group]
    high_bits = low_bits[::-1]
    extra = [b for b in (8, 16, 32, 64, 128, 256, 512) if b < n_d]
    spots = group // 2
    slab = units // group
    piece = local // spots
    core = di % 2
    spot = (di // 2) % spots

    def bit_of(bit):
        return (di // bit) % 2

    def dp_swap(x, bit):
        return swap(x, "dp", n_d, bit)

    def everyone(x):
        bit = 1
        while bit < n_d:
            x = x + dp_swap(x, bit)
            bit *= 2
        return x

    def spread(x, bits, other=None):
        done = []
        for bit in bits:
            if done or other is None:
                other = dp_swap(x, bit)
            up = bit_of(bit) == 1
            pos = sum(1 for b in done if b > bit)
            x = jnp.stack([jnp.where(up, other, x), jnp.where(up, x, other)], axis=pos)
            done.append(bit)
        return x.reshape((-1,) + x.shape[len(done) :])

    def narrow_start(x, bits):
        ax = sorted(bits, reverse=True).index(bits[0])
        up = bit_of(bits[0])
        send = lax.dynamic_index_in_dim(x, 1 - up, ax, keepdims=False)
        keep = lax.dynamic_index_in_dim(x, up, ax, keepdims=False)
        return keep, dp_swap(send, bits[0])

    def narrow_pair(x, y, bits, lo=0, count=None):
        ax = sorted(bits, reverse=True).index(bits[0])
        up = bit_of(bits[0])
        sizes = list(x.shape)
        sizes[ax] = 1
        sizes[-2] = count or sizes[-2]

        def half(i):
            at = [0] * x.ndim
            at[ax] = i
            at[-2] = lo
            part = lambda v: lax.dynamic_slice(v, at, sizes).astype(F32)
            return (part(x) + part(y)).astype(BF16).reshape(sizes[:ax] + sizes[ax + 1 :])

        return half(up), half(1 - up), bits[0]

    def narrow(x, bits):
        left = sorted(bits, reverse=True)
        for bit in bits:
            ax = left.index(bit)
            left.remove(bit)
            up = bit_of(bit)
            send = lax.dynamic_index_in_dim(x, 1 - up, ax, keepdims=False)
            keep = lax.dynamic_index_in_dim(x, up, ax, keepdims=False)
            x = (keep.astype(F32) + dp_swap(send, bit).astype(F32)).astype(BF16)
        return x

    def quad_parts(x):
        return [lax.dynamic_index_in_dim(x, spot ^ r, 0, keepdims=False) for r in range(spots)]

    def quad_sum(x):
        pieces = quad_parts(x)
        total = pieces[0].astype(F32)
        for r in range(1, spots):
            total = total + dp_swap(pieces[r], 2 * r).astype(F32)
        return total.astype(BF16)

    def quad_gather(x):
        held = [x] + [dp_swap(x, 2 * r) for r in range(1, spots)]
        step = 1
        while step < spots:
            flip = bit_of(2 * step) == 1
            held = [jnp.where(flip, held[r ^ step], held[r]) for r in range(spots)]
            step *= 2
        return held

    def finish(x):
        for bit in extra:
            x = (x.astype(F32) + dp_swap(x, bit).astype(F32)).astype(BF16)
        return x

    valid_f = valid[0].astype(F32)

    up_own = w_up.T
    b_hi = b_up.astype(BF16)
    b_lo = (b_up - b_hi.astype(F32)).astype(BF16)
    start = core * (spots * slab) + spot * slab
    sent = jnp.concatenate(
        [
            rows_of(up_own, start, slab),
            rows_of(w_attn_out, spot * piece, piece),
            rows_of(w_down, start, slab),
            b_hi[None],
            b_lo[None],
            jnp.zeros((14, width), BF16),
        ]
    )
    came = [shift(sent, n_t, s) for s in range(1, n_t)]

    w_t = w_qkv.transpose(0, 2, 1).reshape(3 * local, width)
    w_t = rows_of(w_t, core * (3 * local // 2), 3 * local // 2)
    q3, k3, v3, qt, kt, vt, lmt = attn_prep(hidden, w_qkv, b_qv, table, noise)
    n_sup = tokens // lmt.shape[1]
    cuts = [max(n_sup - 2, 1), max(n_sup - 1, 2)]
    part = attn_fwd(qt, k3, vt, lmt, 0, cuts[0])
    part, came, w_t = lax.optimization_barrier((part, came, w_t))
    w_side = lax.all_gather(w_t, "tensor", axis=0)

    cut = slab + piece
    wide_a = jnp.stack([x[:cut] for x in came])
    wide_b = jnp.stack([x[cut : cut + slab] for x in came])
    first_a = dp_swap(wide_a, low_bits[0])
    first_b = dp_swap(wide_b, high_bits[0])
    part = attn_fwd(qt, k3, vt, lmt, cuts[0], cuts[1], part)
    part, first_a, first_b = lax.optimization_barrier((part, first_a, first_b))
    ctx, ctxt, lse = attn_fwd(qt, k3, vt, lmt, cuts[1], n_sup, part)
    wide_a = spread(wide_a, low_bits, first_a)
    wide_b = spread(wide_b, high_bits, first_b)
    ctx_parts = [rows_of(ctx, ti * chunk, chunk)] + [
        shift(rows_of(ctx, lax.rem(ti + s, n_t) * chunk, chunk), n_t, s) for s in range(1, n_t)
    ]
    *ctx_parts, wide_a, wide_b, w_side = lax.optimization_barrier((*ctx_parts, wide_a, wide_b, w_side))
    up_m = wide_a[:, :, :slab].reshape(-1, width)
    down_m = wide_b.reshape(-1, width)
    wao = wide_a[:, :, slab:].transpose(1, 0, 2, 3).reshape(n_t - 1, local, width)
    wao = jnp.concatenate([w_attn_out[None], wao])
    up_t = dp_swap(up_m, 1)
    down_t = dp_swap(down_m, 1)
    b_all = jnp.stack(
        [b_up]
        + [x[cut + slab].astype(F32) + x[cut + slab + 1].astype(F32) for x in came]
    ).reshape(n_t, 2, spots, slab)
    b_mine = lax.dynamic_index_in_dim(b_all, core, 1, keepdims=False)
    b_theirs = lax.dynamic_index_in_dim(b_all, 1 - core, 1, keepdims=False)
    bup = jnp.stack([b_mine, b_theirs]).transpose(0, 2, 1, 3).reshape(2 * spots, 1, n_t * slab)

    w_other = dp_swap(w_side, 1)
    vec = jnp.stack([b_attn_out, gain_one, bias_one, b_down, gain_two, bias_two, b_down, b_down])
    (out_own, out_low, act, gb, first_low, grad_ffn, grad_attn, grad_resid, vecs, gbup, *gctx_rel) = ffn(
        core.reshape(1),
        ctx_parts,
        wao,
        rows_of(hidden, ti * chunk, chunk),
        rows_of(teacher, ti * chunk, chunk),
        lax.dynamic_slice_in_dim(valid_f, ti * chunk, chunk)[:, None],
        vec,
        bup,
        (up_own, up_m, up_t),
        (w_down, down_m, down_t),
        slab,
    )

    vecs, w_other, w_side = lax.optimization_barrier((vecs, w_other, w_side))
    up = core == 1
    gbu = gbup.reshape(2, spots, n_t, slab)
    gbu = jnp.where(up, gbu[::-1], gbu).transpose(2, 0, 1, 3).reshape(n_t, units)
    gbu = gbu[jnp.stack([lax.rem(ti - z + n_t, n_t) for z in range(n_t)])]
    pack = jnp.concatenate([vecs.reshape(-1), gbu.reshape(-1)]).reshape(-1, 128)

    parts = [gctx_rel[0]] + [shift(gctx_rel[s], n_t, -s) for s in range(1, n_t)]

    lead = (2,) * len(low_bits)
    send, keep = wgrad(slab, spots, gb, first_low, act, grad_ffn, grad_attn, ctx_parts)
    *parts, send, keep, out_low, pack = lax.optimization_barrier((*parts, send, keep, out_low, pack))
    pack_came = dp_swap(pack, 1)
    got = dp_swap(send, 1)
    out_all = lax.all_gather(out_low, "tensor", axis=0, tiled=True)

    gqkv, glm = attn_bwd(ti.reshape(1), parts, ctxt, q3, k3, v3, qt, kt, lse, lmt)
    gqkv, glm, keep, got, pack, pack_came = lax.optimization_barrier((gqkv, glm, keep, got, pack, pack_came))
    pack = pack + pack_came
    pack_came = dp_swap(pack, low_bits[0])
    pairs = chunk // 2
    parts = [rows_of(gqkv, ti * pairs, pairs)] + [
        shift(rows_of(gqkv, lax.rem(ti + s, n_t) * pairs, pairs), n_t, s) for s in range(1, n_t)
    ]
    tall = keep.shape[2]
    mid = tall // 32 * 16
    keep = keep.reshape(lead + keep.shape[1:])
    got = got.reshape(lead + got.shape[1:])
    a_keep, a_send, bit = narrow_pair(keep, got, low_bits, 0, mid)
    a_came = dp_swap(a_send, bit)
    b_keep, b_send, bit = narrow_pair(keep, got, high_bits, mid, tall - mid)
    b_came = dp_swap(b_send, bit)
    tail = tail_of(hidden, gqkv, glm, table, noise, 3 * local)
    w_all = jnp.concatenate([jnp.where(up, w_other, w_side), jnp.where(up, w_side, w_other)], axis=1)
    near = [s for s in range(n_t) if s in (0, 1, n_t - 1)]
    far = [s for s in range(n_t) if s not in near]
    held = lax.optimization_barrier(
        (w_all, tail, a_keep, a_came, b_keep, b_came, pack, pack_came, *[parts[s] for s in near])
    )
    w_all, tail, a_keep, a_came, b_keep, b_came, pack, pack_came = held[:8]
    for n, s in enumerate(near):
        parts[s] = held[8 + n]
    pack = pack + pack_came
    pack_came = dp_swap(pack, low_bits[1])
    a_keep, a_send, bit = narrow_pair(a_keep, a_came, low_bits[1:])
    a_came = dp_swap(a_send, bit)
    b_keep, b_send, bit = narrow_pair(b_keep, b_came, high_bits[1:])
    b_came = dp_swap(b_send, bit)
    tail = tail.reshape((2,) + lead + (-1, tail.shape[1]))
    send = lax.dynamic_index_in_dim(tail, 1 - core, 0, keepdims=False)
    t_keep = lax.dynamic_index_in_dim(tail, core, 0, keepdims=False)
    t_keep, t_send, bit = narrow_pair(t_keep, dp_swap(send, 1), low_bits)
    t_came = dp_swap(t_send, bit)
    held = lax.optimization_barrier(
        (a_keep, a_came, b_keep, b_came, pack, pack_came, *[parts[s] for s in far])
    )
    a_keep, a_came, b_keep, b_came, pack, pack_came = held[:6]
    for n, s in enumerate(far):
        parts[s] = held[6 + n]
    g_a = (a_keep.astype(F32) + a_came.astype(F32)).astype(BF16)
    g_b = (b_keep.astype(F32) + b_came.astype(F32)).astype(BF16)
    g_a = finish(narrow(g_a, low_bits[2:]))
    g_b = finish(narrow(g_b, high_bits[2:]))
    pack = pack + pack_came
    pack_came = swap(pack, "tensor", n_t, 1)
    total = jnp.concatenate([g_a, g_b], axis=1)
    pieces = [total[0]] + [shift(total[s], n_t, -s) for s in range(1, n_t)]
    back = back_of(ti.reshape(1), w_all, grad_resid, parts)
    tail = finish(narrow((t_keep.astype(F32) + t_came.astype(F32)).astype(BF16), low_bits[1:]))
    back, tail, pack, pack_came, *pieces = lax.optimization_barrier((back, tail, pack, pack_came, *pieces))
    grad_hidden = lax.all_gather(back, "tensor", axis=0, tiled=True)
    summed = pieces[0].astype(F32)
    for p in pieces[1:]:
        summed = summed + p.astype(F32)
    held = quad_gather(summed.astype(BF16))
    tail = jnp.concatenate(quad_gather(tail))
    other = dp_swap(tail, 1)
    tail = jnp.concatenate([jnp.where(up, other, tail), jnp.where(up, tail, other)])
    g_ao = jnp.concatenate([x[slab:cut] for x in held])
    pair = jnp.stack([jnp.concatenate([x[:slab] for x in held]), jnp.concatenate([x[cut:] for x in held])])
    other = dp_swap(pair, 1)
    pair = jnp.concatenate([jnp.where(up, other, pair), jnp.where(up, pair, other)], axis=1)
    pack = pack + pack_came
    for bit in low_bits[2:] + extra:
        pack = pack + dp_swap(pack, bit)
    bit = 2
    while bit < n_t:
        pack = pack + swap(pack, "tensor", n_t, bit)
        bit *= 2
    cols = table.shape[2]
    at = 2 * cols + 3 * local
    extra_cols = tail.shape[1] - at
    g_mask = jnp.stack([tail[:, :cols], tail[:, cols : 2 * cols]])
    g_qkv_w = jnp.stack([tail[:, 2 * cols + n * local : 2 * cols + (n + 1) * local] for n in range(3)])
    g_b_qv = tail[: 3 * local // extra_cols, at:].reshape(3, local)[0::2]
    out_states = out_all.astype(F32)
    g_up = pair[0].T
    g_down = pair[1]

    pack = pack.reshape(-1)
    rows = [pack[n * width : (n + 1) * width] for n in range(8)]
    gbu = lax.dynamic_slice_in_dim(pack, 8 * width + ti * units, units)
    total_valid = rows[7][0]
    loss = jnp.sum(rows[6]) / (total_valid * width)
    coef = 2.0 * tokens / total_valid
    grads = [
        grad_hidden, g_qkv_w.reshape(w_qkv.shape), g_b_qv.reshape(2, local), g_ao, rows[0], rows[1], rows[2],
        g_up, gbu, g_down, rows[3], rows[4], rows[5], g_mask.reshape(table.shape),
    ]
    return (out_states, loss, *[g.astype(F32) * coef for g in grads])


def solution(mesh):
    row, col = P("tensor", None), P(None, "tensor")
    heads = P("tensor", None, None)
    dp = P("dp", None)
    qkv = P(None, None, "tensor")
    sizes = dict(mesh.shape)
    return jax.shard_map(
        functools.partial(body, n_d=sizes["dp"], n_t=sizes["tensor"]),
        mesh=mesh,
        in_specs=(dp, dp, dp, qkv, col, row, P(), P(), P(), col, P("tensor"), row, P(), P(), P(), heads, heads),
        out_specs=(dp, P(), dp, qkv, col, row, P(), P(), P(), col, P("tensor"), row, P(), P(), P(), heads),
        check_vma=False,
    )
```
